32 devices in a mesh: grp: 4 (over y, x), fsdp: 8 (over z, core).
Axes of the slice: x: 2, y: 2, z: 4, core: 2. Of those that a mesh axis runs over, the one named last changes fastest.
Arguments:
- prompt_in: bfloat16 [3, 16384, 768], P(None, ('grp', 'fsdp')), may hold values from -6 to 6
- cont_in: bfloat16 [3, 8192, 768], P(None, ('grp', 'fsdp')), may hold values from -6 to 6
- prompt_cot: bfloat16 [3, 16384, 768], P(None, ('grp', 'fsdp')), may hold values from -6 to 6
- cont_cot: bfloat16 [3, 8192, 768], P(None, ('grp', 'fsdp')), may hold values from -6 to 6
- cont_prompt: int32 [3, 4, 8], P(None, 'grp', 'fsdp'), may hold values from 0 to 1
- cont_len: int32 [3, 4, 8], P(None, 'grp', 'fsdp'), may hold values from 1 to 256, 1280 in all within a row
- ln1_gain: float32 [768], P(('grp', 'fsdp')), may hold values from 0.5 to 1.5
- ln1_bias: float32 [768], P(('grp', 'fsdp')), may hold values from -1 to 1
- attn_weight: float32 [768, 2304], P(('grp', 'fsdp')), may hold values from -0.3125 to 0.3125
- attn_bias: float32 [2, 768], P(None, ('grp', 'fsdp')), may hold values from -1 to 1
- proj_weight: float32 [768, 768], P(('grp', 'fsdp')), may hold values from -0.875 to 0.875
- proj_bias: float32 [768], P(('grp', 'fsdp')), may hold values from -1 to 1
- ln2_gain: float32 [768], P(('grp', 'fsdp')), may hold values from 0.5 to 1.5
- ln2_bias: float32 [768], P(('grp', 'fsdp')), may hold values from -1 to 1
- fc_weight: float32 [768, 3072], P(('grp', 'fsdp')), may hold values from -0.21875 to 0.21875
- fc_bias: float32 [3072], P(('grp', 'fsdp')), may hold values from -1 to 1
- out_weight: float32 [3072, 768], P(('grp', 'fsdp')), may hold values from -0.109375 to 0.109375
- out_bias: float32 [768], P(('grp', 'fsdp')), may hold values from -2 to 2
Outputs:
- prompt_out: bfloat16 [3, 16384, 768], P(None, ('grp', 'fsdp'))
- cont_out: bfloat16 [3, 8192, 768], P(None, ('grp', 'fsdp'))
- prompt_grad: bfloat16 [3, 16384, 768], P(None, ('grp', 'fsdp'))
- cont_grad: bfloat16 [3, 8192, 768], P(None, ('grp', 'fsdp'))
- ln1_gain_grad: float32 [768], P(('grp', 'fsdp'))
- ln1_bias_grad: float32 [768], P(('grp', 'fsdp'))
- attn_weight_grad: float32 [768, 2304], P(('grp', 'fsdp'))
- attn_bias_grad: float32 [2, 768], P(None, ('grp', 'fsdp'))
- proj_weight_grad: float32 [768, 768], P(('grp', 'fsdp'))
- proj_bias_grad: float32 [768], P(('grp', 'fsdp'))
- ln2_gain_grad: float32 [768], P(('grp', 'fsdp'))
- ln2_bias_grad: float32 [768], P(('grp', 'fsdp'))
- fc_weight_grad: float32 [768, 3072], P(('grp', 'fsdp'))
- fc_bias_grad: float32 [3072], P(('grp', 'fsdp'))
- out_weight_grad: float32 [3072, 768], P(('grp', 'fsdp'))
- out_bias_grad: float32 [768], P(('grp', 'fsdp'))
The draws below stay inside these ranges and needn't reach their ends.
Inputs may be any that keep to these rules, and one draw needn't show every extreme that they name: `cont_len`: in each micro-batch and group the longest continuation has 256 live rows.
All inputs are finite; a program needn't handle non-finite values.
Results may differ from the reference program's by a relative error of at most 0.039.
Values may be sent and summed in bfloat16 or wider, within the bound.
A program may use at most 1 GiB of HBM per device.

```python
import math
import jax
import jax.numpy as jnp
import numpy as np
from jax import lax

D = 768
HEADS = 12
HEAD_DIM = 64
FF = 3072
MB = 3
NPR = 2
PLEN = 2048
CLEN = 256
CONTS_G = 8
PTOK = 16384
CTOK = 8192
N_GRP = 4


def plant(values, own_key, low, high):
    longest = values.shape.index(max(values.shape))
    spots = []
    for shift in (0, 1):
        where = [jax.random.randint(jax.random.fold_in(own_key, axis), (), 0, length) for axis, length in enumerate(values.shape)]
        where[longest] = (where[longest] + shift) % values.shape[longest]
        spots.append(tuple(where))
    return values.at[spots[0]].set(low).at[spots[1]].set(high)


def raised(drawn, rng, source, target, blocks, factor):
    def block_of(axis_at):
        return (jnp.arange(drawn.shape[axis_at]) // (drawn.shape[axis_at] // blocks)).reshape((-1,) + (1,) * (drawn.ndim - 1 - axis_at))

    near = jax.random.permutation(rng, blocks)[block_of(target)]
    other_side = (block_of(target) + blocks // 2) % blocks
    return jnp.where((block_of(source) == near) | (block_of(source) == other_side), factor * drawn, drawn)


def block_levels(rng, extent, split, least, largest):
    def one(dim, shards_of):
        steps = jax.random.uniform(jax.random.fold_in(jax.random.fold_in(rng, 6), dim), (shards_of,), jnp.float32, least / len(split), largest / len(split))
        return jnp.repeat(jnp.exp(steps), extent[dim] // shards_of).reshape((-1,) + (1,) * (len(extent) - dim - 1))

    level = one(*split[0])
    for cut in split[1:]:
        level = level * one(*cut)
    return level


def split_up(number_of, total, limit, lean):
    loads = [(1 << 20) // math.isqrt(standing ** lean) + 1 for standing in range(2, number_of + 1)]
    rest, given = total - limit - (number_of - 1), [1] * (number_of - 1)
    while rest > 0:
        movable = [i for i in range(number_of - 1) if given[i] < limit]
        whole, left = sum([loads[i] for i in movable]), rest
        for i in movable:
            addition = min(limit - given[i], max(1, left * loads[i] // whole), rest)
            given[i] = given[i] + addition
            rest = rest - addition
    return np.array([limit] + given)


def uneven(key, number_of, total, bound, lean):
    if number_of == 2:
        one = jax.random.randint(key, (), max(1, total - bound), min(bound, total - 1) + 1)
        return jnp.stack([one, total - one])
    tallies = jnp.asarray(split_up(number_of, total, bound, lean), jnp.int32)
    couples = (number_of - 1) // 2
    giver, receiver = tallies[1:1 + 2 * couples:2], tallies[2:2 + 2 * couples:2]
    slack = jnp.minimum(giver - 1, bound - receiver)
    passed = jax.random.randint(jax.random.fold_in(key, 1), (couples,), 0, 1 << 20) % (slack + 1)
    tallies = tallies.at[1:1 + 2 * couples:2].set(giver - passed).at[2:2 + 2 * couples:2].set(receiver + passed)
    return tallies[jax.random.permutation(jax.random.fold_in(key, 2), number_of)]


def noise(stream_key, dims, deviation, limit, split=(), kind=jnp.bfloat16):
    values = jax.random.normal(stream_key, dims, jnp.float32) * deviation
    if len(split) > 0:
        values = block_levels(stream_key, dims, split, -0.22, 0.18) * values
    return jnp.clip(values, min=-limit, max=limit).astype(kind)


def noise_with(own_key, shape, scale, most, cuts, heavy, dtype=jnp.bfloat16):
    drawn = scale * jax.random.normal(own_key, shape, jnp.float32)
    if cuts:
        drawn = drawn * block_levels(own_key, shape, cuts, -0.22, 0.18)
    return jnp.clip(raised(drawn, jax.random.fold_in(own_key, 3), *heavy), -most, most).astype(dtype)


def setup_inputs(seed: int = 0) -> dict:
    seeds = jax.random.split(jax.random.key(seed), 19)
    prompt_in = noise(seeds[0], (MB, PTOK, D), 1.0, 6.0, ((1, 32),))
    cont_in = noise(seeds[1], (MB, CTOK, D), 1.0, 6.0, ((1, 32),))
    prompt_cot = noise_with(seeds[2], (MB, PTOK, D), 1.0, 6.0, ((1, 32),), (1, 2, 32, 2.75))
    cont_cot = noise_with(seeds[3], (MB, CTOK, D), 1.0, 6.0, ((1, 32),), (1, 2, 32, 2.75))
    cont_prompt = plant(jax.random.randint(seeds[4], (MB, N_GRP, CONTS_G), 0, NPR), jax.random.fold_in(seeds[4], 1), 0, NPR - 1).astype(jnp.int32)
    cont_len = jax.vmap(lambda own: uneven(own, CONTS_G, CONTS_G * CLEN * 5 // 8, CLEN, 2))(jax.random.split(seeds[5], MB * N_GRP)).reshape((MB, N_GRP, CONTS_G)).astype(jnp.int32)
    ln1_gain = jnp.clip(1.0 + 0.1 * jax.random.normal(seeds[6], (D,), jnp.float32), 0.5, 1.5)
    ln1_bias = noise(seeds[7], (D,), 0.2, 1.0, ((0, 32),), jnp.float32)
    attn_weight = noise(seeds[8], (D, 3 * D), (D // 2) ** -0.5, 0.3125, ((0, 32),), jnp.float32)
    attn_bias = noise(seeds[9], (2, D), 0.2, 1.0, ((1, 32),), jnp.float32)
    proj_weight = noise(seeds[10], (D, D), (D // 16) ** -0.5, 0.875, ((0, 32),), jnp.float32)
    proj_bias = noise(seeds[11], (D,), 0.2, 1.0, ((0, 32),), jnp.float32)
    ln2_gain = jnp.clip(1.0 + 0.1 * jax.random.normal(seeds[12], (D,), jnp.float32), 0.5, 1.5)
    ln2_bias = noise(seeds[13], (D,), 0.2, 1.0, ((0, 32),), jnp.float32)
    fc_weight = noise(seeds[14], (D, FF), D ** -0.5, 0.21875, ((0, 32),), jnp.float32)
    fc_bias = noise(seeds[15], (FF,), 0.2, 1.0, ((0, 32),), jnp.float32)
    out_weight = noise(seeds[16], (FF, D), FF ** -0.5, 0.109375, ((0, 32),), jnp.float32)
    out_bias = noise(seeds[17], (D,), 0.4, 2.0, ((0, 32),), jnp.float32)
    return dict(prompt_in=prompt_in, cont_in=cont_in, prompt_cot=prompt_cot, cont_cot=cont_cot, cont_prompt=cont_prompt, cont_len=cont_len, ln1_gain=ln1_gain, ln1_bias=ln1_bias, attn_weight=attn_weight, attn_bias=attn_bias, proj_weight=proj_weight, proj_bias=proj_bias, ln2_gain=ln2_gain, ln2_bias=ln2_bias, fc_weight=fc_weight, fc_bias=fc_bias, out_weight=out_weight, out_bias=out_bias)


@jax.custom_vjp
def low(v):
    return lax.optimization_barrier(v.astype(jnp.bfloat16)).astype(jnp.float32)

@jax.custom_vjp
def low_back(v):
    return v

def low_keep(v):
    return (low(v), None)

def low_pass(kept, grad):
    return (grad,)

def back_keep(v):
    return (v, None)

def back_low(kept, grad):
    return (low(grad),)
low.defvjp(low_keep, low_pass)
low_back.defvjp(back_keep, back_low)
EPSILON = 1e-05
HIGH = lax.Precision.HIGHEST

def rounded_both(value):
    return low_back(low(value))

def layer_norm(value, gain, shift):
    center = value - lax.optimization_barrier(jnp.mean(value, axis=-1, keepdims=True))
    spread = lax.optimization_barrier(jnp.mean(center * center, axis=-1, keepdims=True))
    return center * lax.rsqrt(spread + EPSILON) * gain + shift

def split_heads(value):
    return value.reshape(value.shape[0], HEADS, HEAD_DIM)

def attend(query, keys, values, allowed):
    raw = jnp.einsum('qhd,khd->hqk', split_heads(query), split_heads(keys), precision=HIGH)
    scores = low_back(raw * HEAD_DIM ** (-0.5))
    scores = jnp.where(allowed[None], scores, -1e+30)
    ceiling = lax.optimization_barrier(jnp.max(scores, axis=-1, keepdims=True))
    powers = jnp.exp(scores - ceiling)
    probs = low(powers / lax.optimization_barrier(jnp.sum(powers, axis=-1, keepdims=True)))
    mixed = jnp.einsum('hqk,khd->qhd', probs, split_heads(values), precision=HIGH)
    return mixed.reshape(query.shape[0], HEADS * HEAD_DIM)

def group_forward(params, prompt_rows, cont_rows, follows, lengths):
    used = [low(item) for item in params]
    gain_first, shift_first, w_attn, b_attn, w_proj, b_proj = (used[0], used[1], used[2], used[3], used[4], used[5])
    gain_second, shift_second, w_fc, b_fc, w_out, b_out = (used[6], used[7], used[8], used[9], used[10], used[11])
    conts = cont_rows.shape[0]
    split_at = NPR * PLEN
    inputs = jnp.concatenate([prompt_rows, cont_rows.reshape(conts * CLEN, D)], axis=0)
    live = (jnp.arange(CLEN)[None, :] < lengths[:, None]).astype(jnp.float32).reshape(conts * CLEN)
    valid = jnp.concatenate([jnp.ones((split_at,), jnp.float32), live])[:, None]
    normed = low(layer_norm(inputs, gain_first, shift_first))
    projected = jnp.dot(normed, w_attn, precision=HIGH)
    query = rounded_both(projected[:, :D] + b_attn[0])
    keys = rounded_both(projected[:, D:2 * D])
    values = rounded_both(projected[:, 2 * D:] + b_attn[1])
    prompt_keys = keys[:split_at].reshape(NPR, PLEN, D)
    prompt_values = values[:split_at].reshape(NPR, PLEN, D)
    causal = jnp.arange(PLEN)[None, :] <= jnp.arange(PLEN)[:, None]

    def prompt_one(items):
        return attend(items[0], items[1], items[2], causal)
    prompt_mix = lax.map(jax.checkpoint(prompt_one), (query[:split_at].reshape(NPR, PLEN, D), prompt_keys, prompt_values))
    own = jnp.arange(CLEN)[None, :] <= jnp.arange(CLEN)[:, None]
    seen = jnp.concatenate([jnp.ones((CLEN, PLEN), jnp.bool_), own], axis=1)

    def cont_one(items):
        cont_query, cont_keys, cont_values, which = items
        all_keys = jnp.concatenate([prompt_keys[which], cont_keys], axis=0)
        all_values = jnp.concatenate([prompt_values[which], cont_values], axis=0)
        return attend(cont_query, all_keys, all_values, seen)
    cont_mix = lax.map(jax.checkpoint(cont_one), (query[split_at:].reshape(conts, CLEN, D), keys[split_at:].reshape(conts, CLEN, D), values[split_at:].reshape(conts, CLEN, D), follows))
    mixed = rounded_both(jnp.concatenate([prompt_mix.reshape(split_at, D), cont_mix.reshape(conts * CLEN, D)], axis=0))
    branch = low_back(jnp.dot(mixed, w_proj, precision=HIGH) + b_proj)
    hidden = inputs + valid * branch
    second = low(layer_norm(hidden, gain_second, shift_second))
    inner = low_back(jnp.dot(second, w_fc, precision=HIGH) + b_fc)
    active = low(jax.nn.gelu(inner, approximate=True))
    result = low_back(jnp.dot(active, w_out, precision=HIGH) + b_out)
    final = hidden + valid * result
    return (final[:split_at], final[split_at:].reshape(conts, CLEN, D))

def reference(prompt_in, cont_in, prompt_cot, cont_cot, cont_prompt, cont_len, ln1_gain, ln1_bias, attn_weight, attn_bias, proj_weight, proj_bias, ln2_gain, ln2_bias, fc_weight, fc_bias, out_weight, out_bias):
    params = (ln1_gain, ln1_bias, attn_weight, attn_bias, proj_weight, proj_bias, ln2_gain, ln2_bias, fc_weight, fc_bias, out_weight, out_bias)
    blocks = MB * N_GRP
    prompt_x = prompt_in.astype(jnp.float32).reshape(blocks, NPR * PLEN, D)
    cont_x = cont_in.astype(jnp.float32).reshape(blocks, CONTS_G, CLEN, D)
    prompt_g = prompt_cot.astype(jnp.float32).reshape(blocks, NPR * PLEN, D)
    cont_g = cont_cot.astype(jnp.float32).reshape(blocks, CONTS_G, CLEN, D)
    follows = cont_prompt.reshape(blocks, CONTS_G)
    lengths = cont_len.reshape(blocks, CONTS_G)

    def one_block(totals, items):
        prompt_rows, cont_rows, prompt_seed, cont_seed, which, sizes = items

        def forward(weights, first, second):
            return group_forward(weights, first, second, which, sizes)
        outputs, pull = jax.vjp(forward, params, prompt_rows, cont_rows)
        grads, grad_prompt, grad_cont = pull((prompt_seed, cont_seed))
        totals = jax.tree.map(lambda left, right: left + right, totals, grads)
        return (totals, (outputs[0].astype(jnp.bfloat16), outputs[1].astype(jnp.bfloat16), grad_prompt.astype(jnp.bfloat16), grad_cont.astype(jnp.bfloat16)))
    start = jax.tree.map(jnp.zeros_like, params)
    totals, pieces = lax.scan(one_block, start, (prompt_x, cont_x, prompt_g, cont_g, follows, lengths))
    return (pieces[0].reshape(MB, PTOK, D), pieces[1].reshape(MB, CTOK, D), pieces[2].reshape(MB, PTOK, D), pieces[3].reshape(MB, CTOK, D), totals[0], totals[1], totals[2], totals[3], totals[4], totals[5], totals[6], totals[7], totals[8], totals[9], totals[10], totals[11])
```

```python
import functools
import math

import jax
import jax.numpy as jnp
from jax import lax
from jax.experimental import pallas as pl
from jax.experimental.pallas import tpu as pltpu
from jax.sharding import PartitionSpec as P

D = 768
HEADS = 12
HEAD_DIM = 64
FF = 3072
MB = 3
NPR = 2
PLEN = 2048
ALL = ("grp", "fsdp")

EPSILON = 1e-05
MASKED = -1e30
BF = jnp.bfloat16
F32 = jnp.float32

HALF = D // 2
NH = HEADS // 2
PAIRS = NH // 2
TQ = 256
TK = 512
LOG2E = math.log2(math.e)
QSCALE = HEAD_DIM ** (-0.5) * LOG2E


def dot_nt(a, b):
    return lax.dot_general(a, b, (((1,), (1,)), ((), ())), preferred_element_type=F32)


def dot_nn(a, b):
    return lax.dot_general(a, b, (((1,), (0,)), ((), ())), preferred_element_type=F32)


def half_masks():
    lane = lax.broadcasted_iota(jnp.int32, (TQ, 128), 1)
    return (lane < HEAD_DIM, lane >= HEAD_DIM)


def attend_forward_kernel(
    info, q_ref, kvp_hbm, kvc_hbm, o_ref, lse_ref, kv, qm, s_ref, mx, acc, sems
):
    block = pl.program_id(0)
    prompt_rows = kvp_hbm.shape[0]
    cont_rows = kvc_hbm.shape[0]

    @pl.when(block == 0)
    def _():
        one = pltpu.make_async_copy(kvp_hbm, kv.at[pl.ds(0, prompt_rows)], sems.at[0])
        two = pltpu.make_async_copy(kvc_hbm, kv.at[pl.ds(prompt_rows, cont_rows)], sems.at[1])
        one.start()
        two.start()
        one.wait()
        two.wait()

    base = pl.multiple_of(info[block, 0], TQ)
    tiles = info[block, 1]
    extra = info[block, 2]
    diag = pl.multiple_of(info[block, 3], TQ)
    extra_row = pl.multiple_of(base + tiles * TK, TQ)
    low, high = half_masks()
    zero = jnp.zeros((TQ, 128), BF)
    for pair in range(PAIRS):
        part = q_ref[:, pair * 128 : (pair + 1) * 128]
        qm[2 * pair] = jnp.where(low, part, zero)
        qm[2 * pair + 1] = jnp.where(high, part, zero)

    def score(pair, row, size, column, first, masked):
        keys = kv[pl.ds(row, size), pair * 128 : (pair + 1) * 128]
        for side in (0, 1):
            raw = dot_nt(qm[2 * pair + side], keys)
            if masked:
                across = lax.broadcasted_iota(jnp.int32, (TQ, size), 1)
                down = lax.broadcasted_iota(jnp.int32, (TQ, size), 0)
                raw = jnp.where(across <= down, raw, MASKED)
            slot = 2 * (pair % 2) + side
            s_ref[slot, :, pl.ds(column, size)] = raw
            top = raw[:, :128]
            for piece in range(1, size // 128):
                top = jnp.maximum(top, raw[:, piece * 128 : (piece + 1) * 128])
            if not first:
                top = jnp.maximum(top, mx[slot])
            mx[slot] = top

    def settle(pair):
        for side in (0, 1):
            slot = 2 * (pair % 2) + side
            top = jnp.max(mx[slot], axis=1, keepdims=True)
            mx[slot] = jnp.broadcast_to(top, (TQ, 128))

    def blend(pair, row, size, column, first):
        vals = kv[pl.ds(row, size), HALF + pair * 128 : HALF + (pair + 1) * 128]
        wide = jnp.concatenate([vals, jnp.ones((size, 128), BF)], axis=1)
        for side in (0, 1):
            slot = 2 * (pair % 2) + side
            top = jnp.concatenate([mx[slot]] * (size // 128), axis=1)
            power = jnp.exp2(s_ref[slot, :, pl.ds(column, size)] - top).astype(BF)
            new = dot_nn(power, wide)
            if first:
                acc[side] = new
            else:
                acc[side] += new

    def sweep(step):
        step(diag, TQ, 0, True)

        @pl.when(extra > 0)
        def _():
            step(extra_row, TQ, TQ, False)

        def one(index, carry):
            row = pl.multiple_of(base + index * TK, TQ)
            step(row, TK, pl.multiple_of(2 * TQ + index * TK, TQ), False)
            return carry

        lax.fori_loop(0, tiles, one, 0)

    sweep(lambda row, size, column, first: score(0, row, size, column, first, first))
    for pair in range(PAIRS):
        settle(pair)

        def both(row, size, column, first):
            if pair + 1 < PAIRS:
                score(pair + 1, row, size, column, first, first)
            blend(pair, row, size, column, first)

        sweep(both)
        sides = []
        for side in (0, 1):
            total = acc[side][:, 128:]
            sides.append(acc[side][:, :128] / total)
            tall = jnp.transpose(mx[2 * (pair % 2) + side] + jnp.log2(total))
            lse_ref[0, 2 * pair + side] = tall[0]
        o_ref[:, pair * 128 : (pair + 1) * 128] = jnp.where(low, sides[0], sides[1]).astype(BF)


def attend_forward(info, q, kvp, kvc):
    rows = q.shape[0]
    keys = kvp.shape[0] + kvc.shape[0]
    blocks = rows // TQ
    return pl.pallas_call(
        attend_forward_kernel,
        grid_spec=pltpu.PrefetchScalarGridSpec(
            num_scalar_prefetch=1,
            grid=(blocks,),
            in_specs=[
                pl.BlockSpec((TQ, HALF), lambda i, s: (i, 0)),
                pl.BlockSpec(memory_space=pl.ANY),
                pl.BlockSpec(memory_space=pl.ANY),
            ],
            out_specs=[
                pl.BlockSpec((TQ, HALF), lambda i, s: (i, 0)),
                pl.BlockSpec((1, 8, TQ), lambda i, s: (i, 0, 0)),
            ],
            scratch_shapes=[
                pltpu.VMEM((keys, D), BF),
                pltpu.VMEM((NH, TQ, 128), BF),
                pltpu.VMEM((4, TQ, PLEN + 2 * TQ), F32),
                pltpu.VMEM((4, TQ, 128), F32),
                pltpu.VMEM((2, TQ, 256), F32),
                pltpu.SemaphoreType.DMA((2,)),
            ],
        ),
        out_shape=(
            jax.ShapeDtypeStruct((rows, HALF), BF),
            jax.ShapeDtypeStruct((blocks, 8, TQ), F32),
        ),
        compiler_params=pltpu.CompilerParams(
            dimension_semantics=("arbitrary",), vmem_limit_bytes=50 << 20
        ),
        cost_estimate=pl.CostEstimate(
            flops=int(4 * rows * PLEN * HALF * 4), bytes_accessed=20 << 20, transcendentals=0
        ),
        name="attend_forward",
    )(info, q, kvp, kvc)


def attend_backward_kernel(
    info,
    q_ref,
    do_ref,
    o_ref,
    lse_ref,
    kvp_hbm,
    kvc_hbm,
    dq_ref,
    dkvp_hbm,
    dkvc_hbm,
    kv,
    kt,
    dkv,
    qm,
    dom,
    dqt,
    drow,
    sems,
):
    block = pl.program_id(0)
    prompt_rows = kvp_hbm.shape[0]
    cont_rows = kvc_hbm.shape[0]
    keys_all = prompt_rows + cont_rows

    @pl.when(block == 0)
    def _():
        one = pltpu.make_async_copy(kvp_hbm, kv.at[pl.ds(0, prompt_rows)], sems.at[0])
        two = pltpu.make_async_copy(kvc_hbm, kv.at[pl.ds(prompt_rows, cont_rows)], sems.at[1])
        one.start()
        two.start()
        one.wait()
        two.wait()

        def prepare(index, carry):
            row = pl.multiple_of(index * TQ, TQ)
            dkv[pl.ds(row, TQ), :] = jnp.zeros((TQ, D), F32)
            for pair in range(PAIRS):
                piece = kv[pl.ds(row, TQ), pair * 128 : (pair + 1) * 128]
                kt[pair * 128 : (pair + 1) * 128, pl.ds(row, TQ)] = jnp.transpose(
                    piece.astype(F32)
                ).astype(BF)
            return carry

        lax.fori_loop(0, keys_all // TQ, prepare, 0)

    base = pl.multiple_of(info[block, 0], TQ)
    tiles = info[block, 1]
    extra = info[block, 2]
    diag = pl.multiple_of(info[block, 3], TQ)
    extra_row = pl.multiple_of(base + tiles * TK, TQ)
    low, high = half_masks()
    zero = jnp.zeros((TQ, 128), BF)
    for pair in range(PAIRS):
        lanes = slice(pair * 128, (pair + 1) * 128)
        part = q_ref[:, lanes]
        qm[2 * pair] = jnp.where(low, part, zero)
        qm[2 * pair + 1] = jnp.where(high, part, zero)
        part = do_ref[:, lanes]
        dom[2 * pair] = jnp.where(low, part, zero)
        dom[2 * pair + 1] = jnp.where(high, part, zero)
        product = jnp.transpose(part.astype(F32) * o_ref[:, lanes].astype(F32))
        drow[2 * pair] = jnp.sum(product[:HEAD_DIM], axis=0)
        drow[2 * pair + 1] = jnp.sum(product[HEAD_DIM:], axis=0)

    def step(row, size, first):
        for pair in range(PAIRS):
            lanes = slice(pair * 128, (pair + 1) * 128)
            more = slice(HALF + pair * 128, HALF + (pair + 1) * 128)
            keys = kv[pl.ds(row, size), lanes]
            vals = kv[pl.ds(row, size), more]
            dk = None
            dv = None
            for side in (0, 1):
                head = 2 * pair + side
                raw = dot_nt(keys, qm[head])
                if first:
                    across = lax.broadcasted_iota(jnp.int32, (size, TQ), 1)
                    down = lax.broadcasted_iota(jnp.int32, (size, TQ), 0)
                    raw = jnp.where(down <= across, raw, MASKED)
                probs = jnp.exp2(raw - lse_ref[0, head : head + 1, :])
                grad = dot_nt(vals, dom[head])
                slope = (probs * (grad - drow[head : head + 1, :])).astype(BF)
                probs = probs.astype(BF)
                part_v = dot_nn(probs, dom[head])
                part_k = dot_nn(slope, qm[head])
                dv = part_v if dv is None else dv + part_v
                dk = part_k if dk is None else dk + part_k
                spot = slice(head * HEAD_DIM, (head + 1) * HEAD_DIM)
                new = dot_nn(kt[spot, pl.ds(row, size)], slope)
                if first:
                    dqt[spot, :] = new
                else:
                    dqt[spot, :] += new
            dkv[pl.ds(row, size), lanes] += dk
            dkv[pl.ds(row, size), more] += dv

    step(diag, TQ, True)

    @pl.when(extra > 0)
    def _():
        step(extra_row, TQ, False)

    def one(index, carry):
        step(pl.multiple_of(base + index * TK, TQ), TK, False)
        return carry

    lax.fori_loop(0, tiles, one, 0)
    for pair in range(PAIRS):
        lanes = slice(pair * 128, (pair + 1) * 128)
        dq_ref[:, lanes] = (jnp.transpose(dqt[lanes, :]) * HEAD_DIM ** (-0.5)).astype(BF)

    @pl.when(block == pl.num_programs(0) - 1)
    def _():
        def finish(index, carry):
            row = pl.multiple_of(index * TQ, TQ)
            kv[pl.ds(row, TQ), :HALF] = (dkv[pl.ds(row, TQ), :HALF] * (1.0 / LOG2E)).astype(BF)
            kv[pl.ds(row, TQ), HALF:] = dkv[pl.ds(row, TQ), HALF:].astype(BF)
            return carry

        lax.fori_loop(0, keys_all // TQ, finish, 0)
        one = pltpu.make_async_copy(kv.at[pl.ds(0, prompt_rows)], dkvp_hbm, sems.at[0])
        two = pltpu.make_async_copy(kv.at[pl.ds(prompt_rows, cont_rows)], dkvc_hbm, sems.at[1])
        one.start()
        two.start()
        one.wait()
        two.wait()


def attend_backward(info, q, do, o, lse, kvp, kvc):
    rows = q.shape[0]
    keys = kvp.shape[0] + kvc.shape[0]
    blocks = rows // TQ
    tile = pl.BlockSpec((TQ, HALF), lambda i, s: (i, 0))
    whole = pl.BlockSpec(memory_space=pl.ANY)
    return pl.pallas_call(
        attend_backward_kernel,
        grid_spec=pltpu.PrefetchScalarGridSpec(
            num_scalar_prefetch=1,
            grid=(blocks,),
            in_specs=[
                tile,
                tile,
                tile,
                pl.BlockSpec((1, 8, TQ), lambda i, s: (i, 0, 0)),
                whole,
                whole,
            ],
            out_specs=[tile, whole, whole],
            scratch_shapes=[
                pltpu.VMEM((keys, D), BF),
                pltpu.VMEM((HALF, keys), BF),
                pltpu.VMEM((keys, D), F32),
                pltpu.VMEM((NH, TQ, 128), BF),
                pltpu.VMEM((NH, TQ, 128), BF),
                pltpu.VMEM((HALF, TQ), F32),
                pltpu.VMEM((8, TQ), F32),
                pltpu.SemaphoreType.DMA((2,)),
            ],
        ),
        out_shape=(
            jax.ShapeDtypeStruct((rows, HALF), BF),
            jax.ShapeDtypeStruct(kvp.shape, BF),
            jax.ShapeDtypeStruct(kvc.shape, BF),
        ),
        compiler_params=pltpu.CompilerParams(
            dimension_semantics=("arbitrary",), vmem_limit_bytes=56 << 20
        ),
        cost_estimate=pl.CostEstimate(
            flops=int(10 * rows * PLEN * HALF * 4), bytes_accessed=30 << 20, transcendentals=0
        ),
        name="attend_backward",
    )(info, q, do, o, lse, kvp, kvc)


def normal_form(value):
    center = value - jnp.mean(value, axis=-1, keepdims=True)
    spread = jnp.mean(center * center, axis=-1, keepdims=True)
    return center * lax.rsqrt(spread + EPSILON)


def layer_norm(value, gain, shift):
    return normal_form(value) * gain + shift


def gelu_tanh(value):
    return jax.nn.gelu(value, approximate=True)


def row_sum(value):
    return jnp.sum(value.astype(F32), axis=0)


def body(
    prompt_in,
    cont_in,
    prompt_cot,
    cont_cot,
    cont_prompt,
    cont_len,
    ln1_gain,
    ln1_bias,
    attn_weight,
    attn_bias,
    proj_weight,
    proj_bias,
    ln2_gain,
    ln2_bias,
    fc_weight,
    fc_bias,
    out_weight,
    out_bias,
):
    fsdp = lax.axis_size("fsdp")
    devices = fsdp * lax.axis_size("grp")
    prow = prompt_in.shape[1]
    crow = cont_in.shape[1]
    conts = cont_prompt.shape[2]
    clen = crow // conts
    mine = prow + crow
    prompt_rows = NPR * PLEN
    place = lax.axis_index("fsdp")
    core = place % 2
    mate = [(i, i ^ 1) for i in range(fsdp)]
    chip_row = place // 2 * (2 * prow)
    share = D // devices
    wide = FF // D

    def swap(value):
        return lax.ppermute(value, "fsdp", mate)

    prompt_all = [lax.all_gather(prompt_in[m], "fsdp", axis=0, tiled=True) for m in range(MB)]
    cont_mate = swap(cont_in)
    plan_mate = swap(cont_prompt[:, 0, :].astype(F32)).astype(jnp.int32)

    vectors = (ln1_gain, ln1_bias, attn_bias[0], attn_bias[1], proj_bias, ln2_gain, ln2_bias, out_bias)
    columns = jnp.concatenate(
        [v[:, None] for v in vectors] + [fc_bias.reshape(share, wide)], axis=1
    )
    columns = jnp.pad(columns, ((0, 0), (0, 128 - columns.shape[1])))
    first = jnp.concatenate([attn_weight, columns], axis=1).astype(BF)
    first = lax.all_gather(first, ALL, axis=0, tiled=True)
    rest = jnp.concatenate([proj_weight, fc_weight, out_weight.reshape(share, FF)], axis=1).astype(BF)
    rest = lax.all_gather(rest, ALL, axis=0, tiled=True)
    small = first[:, 3 * D :].astype(F32)
    gain_a, shift_a, bias_q, bias_v, b_proj, gain_b, shift_b, b_out = (small[:, i] for i in range(8))
    b_fc = small[:, 8 : 8 + wide].reshape(FF)
    w_heads = lax.dynamic_index_in_dim(
        first[:, : 3 * D].reshape(D, 3, 2, HALF), core, axis=2, keepdims=False
    )
    w_q = w_heads[:, 0]
    w_kv = w_heads[:, 1:].reshape(D, D)
    bias_q = lax.dynamic_slice_in_dim(bias_q, core * HALF, HALF)
    bias_v = lax.dynamic_slice_in_dim(bias_v, core * HALF, HALF)
    bias_kv = jnp.concatenate([jnp.zeros((HALF,), F32), bias_v])
    w_proj = rest[:, :D]
    w_fc = rest[:, D : D + FF]
    w_out = rest[:, D + FF :].reshape(FF, D)

    first_place = chip_row % PLEN
    block_place = first_place + TQ * jnp.arange(2 * prow // TQ)
    prompt_plan = jnp.stack(
        [
            jnp.broadcast_to(chip_row - first_place, block_place.shape),
            block_place // TK,
            block_place % TK // TQ,
            chip_row + TQ * jnp.arange(2 * prow // TQ),
        ],
        axis=1,
    )

    def plan_of(m):
        follows = jnp.concatenate([cont_prompt[m, 0], plan_mate[m]])
        count = follows.shape[0]
        cont_plan = jnp.stack(
            [
                follows * PLEN,
                jnp.full((count,), PLEN // TK),
                jnp.zeros((count,), jnp.int32),
                prompt_rows + clen * jnp.arange(count),
            ],
            axis=1,
        )
        return jnp.concatenate([prompt_plan, cont_plan], axis=0).astype(jnp.int32)

    def split_rows(value):
        own = lax.dynamic_slice_in_dim(value, core * prow, prow, 0)
        other = lax.dynamic_slice_in_dim(value, (1 - core) * prow, prow, 0)
        return (
            jnp.concatenate([own, value[2 * prow : 2 * prow + crow]], axis=0),
            jnp.concatenate([other, value[2 * prow + crow :]], axis=0),
        )

    saved = []
    mixed = []
    for m in range(MB):
        a_prompt = layer_norm(prompt_all[m].astype(F32), gain_a, shift_a).astype(BF)
        cont_pair = jnp.concatenate([cont_in[m], cont_mate[m]], axis=0)
        a_cont = layer_norm(cont_pair.astype(F32), gain_a, shift_a).astype(BF)
        a_chip = jnp.concatenate(
            [lax.dynamic_slice_in_dim(a_prompt, chip_row, 2 * prow, 0), a_cont], axis=0
        )
        kvp = (jnp.dot(a_prompt, w_kv, preferred_element_type=F32) + bias_kv).astype(BF)
        kvc = (jnp.dot(a_cont, w_kv, preferred_element_type=F32) + bias_kv).astype(BF)
        query = ((jnp.dot(a_chip, w_q, preferred_element_type=F32) + bias_q) * QSCALE).astype(BF)
        plan = plan_of(m)
        o, lse = attend_forward(plan, query, kvp, kvc)
        own, other = split_rows(o)
        back = swap(other)
        mixed.append(
            jnp.where(
                core == 0,
                jnp.concatenate([own, back], axis=1),
                jnp.concatenate([back, own], axis=1),
            )
        )
        saved.append((a_prompt, a_cont, a_chip, kvp, kvc, query, plan, o, lse))

    inputs = jnp.concatenate([prompt_in, cont_in], axis=1).astype(F32).reshape(MB * mine, D)
    live = (jnp.arange(clen)[None, None, :] < cont_len[:, 0, :, None]).astype(F32)
    valid = jnp.concatenate(
        [jnp.ones((MB, prow), F32), live.reshape(MB, crow)], axis=1
    ).reshape(MB * mine)[:, None]
    ob = jnp.concatenate(mixed, axis=0)
    hidden = inputs + valid * (jnp.dot(ob, w_proj, preferred_element_type=F32) + b_proj)
    normed_second, pull_second = jax.vjp(layer_norm, hidden, gain_b, shift_b)
    second = normed_second.astype(BF)
    inner = jnp.dot(second, w_fc, preferred_element_type=F32) + b_fc
    active_full, pull_gelu = jax.vjp(gelu_tanh, inner)
    active = active_full.astype(BF)
    result = jnp.dot(active, w_out, preferred_element_type=F32) + b_out
    final = (hidden + valid * result).astype(BF).reshape(MB, mine, D)

    grad_out = jnp.concatenate([prompt_cot, cont_cot], axis=1).astype(F32).reshape(MB * mine, D)
    dz = (valid * grad_out).astype(BF)
    g_out_bias = row_sum(dz)
    g_out = jnp.einsum("rf,rd->fd", active, dz, preferred_element_type=F32)
    d_active = jnp.einsum("rd,fd->rf", dz, w_out, preferred_element_type=F32)
    du = pull_gelu(d_active)[0].astype(BF)
    g_fc_bias = row_sum(du)
    g_fc = jnp.einsum("rd,rf->df", second, du, preferred_element_type=F32)
    d_second = jnp.einsum("rf,df->rd", du, w_fc, preferred_element_type=F32)
    d_norm, g_gain_b, g_shift_b = pull_second(d_second)
    dh = grad_out + d_norm
    dy = (valid * dh).astype(BF)
    g_proj_bias = row_sum(dy)
    g_proj = jnp.einsum("rd,re->de", ob, dy, preferred_element_type=F32)
    dob = jnp.einsum("re,de->rd", dy, w_proj, preferred_element_type=F32).astype(BF)
    dob = dob.reshape(MB, mine, D)

    early = jnp.concatenate(
        [
            g_proj.astype(BF),
            g_fc.astype(BF),
            g_out.astype(BF).reshape(D, FF),
        ],
        axis=1,
    )
    early = lax.psum_scatter(early, ALL, scatter_dimension=0, tiled=True).astype(F32)

    g_q = g_kv = g_bias_q = g_bias_v = None
    d_rows = []
    for m in range(MB):
        a_prompt, a_cont, a_chip, kvp, kvc, query, plan, o, lse = saved[m]
        own = lax.dynamic_slice_in_dim(dob[m], core * HALF, HALF, 1)
        other = lax.dynamic_slice_in_dim(dob[m], (1 - core) * HALF, HALF, 1)
        back = swap(other)
        do = jnp.concatenate(
            [
                jnp.where(
                    core == 0,
                    jnp.concatenate([own[:prow], back[:prow]], axis=0),
                    jnp.concatenate([back[:prow], own[:prow]], axis=0),
                ),
                own[prow:],
                back[prow:],
            ],
            axis=0,
        )
        dq, dkvp, dkvc = attend_backward(plan, query, do, o, lse, kvp, kvc)
        table = jnp.einsum("re,de->rd", dkvp, w_kv, preferred_element_type=F32).astype(BF)
        table = lax.psum_scatter(table, "fsdp", scatter_dimension=0, tiled=True).astype(F32)
        part_q = jnp.einsum("rd,re->de", a_chip, dq, preferred_element_type=F32)
        part_kv = jnp.einsum(
            "rd,re->de", a_prompt, dkvp, preferred_element_type=F32
        ) + jnp.einsum("rd,re->de", a_cont, dkvc, preferred_element_type=F32)
        sum_q = row_sum(dq)
        sum_v = row_sum(dkvp[:, HALF:]) + row_sum(dkvc[:, HALF:])
        if g_q is None:
            g_q, g_kv, g_bias_q, g_bias_v = part_q, part_kv, sum_q, sum_v
        else:
            g_q, g_kv = g_q + part_q, g_kv + part_kv
            g_bias_q, g_bias_v = g_bias_q + sum_q, g_bias_v + sum_v
        chip = jnp.einsum("re,de->rd", dq, w_q, preferred_element_type=F32)
        cont = jnp.einsum("re,de->rd", dkvc, w_kv, preferred_element_type=F32)
        chip = jnp.concatenate([chip[: 2 * prow], chip[2 * prow :] + cont], axis=0)
        own, other = split_rows(chip)
        back = swap(other.astype(BF)).astype(F32)
        d_rows.append(
            own + back + jnp.concatenate([table, jnp.zeros((crow, D), F32)], axis=0)
        )

    heads = jnp.concatenate([g_q[:, None, None], g_kv.reshape(D, 2, 1, HALF)], axis=1)
    late = jnp.where(
        (jnp.arange(2) == core)[None, None, :, None], heads, 0.0
    ).reshape(D, 3 * D)
    late = lax.psum_scatter(late.astype(BF), ALL, scatter_dimension=0, tiled=True).astype(F32)

    d_first = jnp.concatenate(d_rows, axis=0)
    _, pull_first = jax.vjp(layer_norm, inputs, gain_a, shift_a)
    d_inputs, g_gain_a, g_shift_a = pull_first(d_first)
    d_inputs = (dh + d_inputs).astype(BF).reshape(MB, mine, D)

    def spread(value):
        return jnp.where((jnp.arange(2) == core)[:, None], value[None, :], 0.0).reshape(D)

    sums = jnp.stack(
        [
            g_gain_a,
            g_shift_a,
            spread(g_bias_q),
            spread(g_bias_v),
            g_proj_bias,
            g_gain_b,
            g_shift_b,
            g_out_bias,
        ]
        + [g_fc_bias.reshape(D, wide)[:, i] for i in range(wide)],
        axis=0,
    )
    sums = lax.psum(sums, ALL)
    index = lax.axis_index("grp") * fsdp + place
    sums = lax.dynamic_slice_in_dim(sums, index * share, share, 1)
    return (
        final[:, :prow],
        final[:, prow:],
        d_inputs[:, :prow],
        d_inputs[:, prow:],
        sums[0],
        sums[1],
        late,
        sums[2:4],
        early[:, :D],
        sums[4],
        sums[5],
        sums[6],
        early[:, D : D + FF],
        sums[8:].T.reshape(share * wide),
        early[:, D + FF :].reshape(share * wide, D),
        sums[7],
    )


def solution(mesh):
    rows = P(None, ALL, None)
    conts = P(None, "grp", "fsdp")
    vector = P(ALL)
    matrix = P(ALL, None)
    pair = P(None, ALL)
    params = (
        vector,
        vector,
        matrix,
        pair,
        matrix,
        vector,
        vector,
        vector,
        matrix,
        vector,
        matrix,
        vector,
    )
    return jax.shard_map(
        body,
        mesh=mesh,
        in_specs=(rows, rows, rows, rows, conts, conts) + params,
        out_specs=(rows, rows, rows, rows) + params,
        check_vma=False,
    )
```

```python
import functools
import math

import jax
import jax.numpy as jnp
from jax import lax
from jax.experimental import pallas as pl
from jax.experimental.pallas import tpu as pltpu
from jax.sharding import PartitionSpec as P

D = 768
HEADS = 12
HEAD_DIM = 64
FF = 3072
MB = 3
NPR = 2
PLEN = 2048
ALL = ("grp", "fsdp")

EPSILON = 1e-05
MASKED = -1e30
BF = jnp.bfloat16
F32 = jnp.float32

HALF = D // 2
NH = HEADS // 2
PAIRS = NH // 2
TK = 512
LOG2E = math.log2(math.e)
QSCALE = HEAD_DIM ** (-0.5) * LOG2E


def dot_nt(a, b):
    return lax.dot_general(a, b, (((1,), (1,)), ((), ())), preferred_element_type=F32)


def dot_nn(a, b):
    return lax.dot_general(a, b, (((1,), (0,)), ((), ())), preferred_element_type=F32)


def half_masks(rows):
    lane = lax.broadcasted_iota(jnp.int32, (rows, 128), 1)
    return (lane < HEAD_DIM, lane >= HEAD_DIM)


def attend_forward_kernel(
    info, q_ref, kvp_hbm, kvc_hbm, o_ref, lse_ref, kv, qm, s_ref, mx, acc, sems
):
    block = pl.program_id(0)
    prompt_rows = kvp_hbm.shape[0]
    cont_rows = kvc_hbm.shape[0]

    @pl.when(block == 0)
    def _():
        one = pltpu.make_async_copy(kvp_hbm, kv.at[pl.ds(0, prompt_rows)], sems.at[0])
        two = pltpu.make_async_copy(kvc_hbm, kv.at[pl.ds(prompt_rows, cont_rows)], sems.at[1])
        one.start()
        two.start()
        one.wait()
        two.wait()

    TQ = q_ref.shape[0]
    base = pl.multiple_of(info[block, 0], TQ)
    tiles = info[block, 1]
    extra = info[block, 2]
    extra_row = pl.multiple_of(info[block, 3], TQ)
    diag = pl.multiple_of(info[block, 4], TQ)
    low, high = half_masks(TQ)
    zero = jnp.zeros((TQ, 128), BF)
    for pair in range(PAIRS):
        part = q_ref[:, pair * 128 : (pair + 1) * 128]
        qm[2 * pair] = jnp.where(low, part, zero)
        qm[2 * pair + 1] = jnp.where(high, part, zero)

    def score(pair, row, size, column, first, masked):
        keys = kv[pl.ds(row, size), pair * 128 : (pair + 1) * 128]
        for side in (0, 1):
            raw = dot_nt(qm[2 * pair + side], keys)
            if masked:
                across = lax.broadcasted_iota(jnp.int32, (TQ, size), 1)
                down = lax.broadcasted_iota(jnp.int32, (TQ, size), 0)
                raw = jnp.where(across <= down, raw, MASKED)
            slot = 2 * (pair % 2) + side
            s_ref[slot, :, pl.ds(column, size)] = raw
            top = raw[:, :128]
            for piece in range(1, size // 128):
                top = jnp.maximum(top, raw[:, piece * 128 : (piece + 1) * 128])
            if not first:
                top = jnp.maximum(top, mx[slot])
            mx[slot] = top

    def settle(pair):
        for side in (0, 1):
            slot = 2 * (pair % 2) + side
            top = jnp.max(mx[slot], axis=1, keepdims=True)
            mx[slot] = jnp.broadcast_to(top, (TQ, 128))

    def blend(pair, row, size, column, first):
        vals = kv[pl.ds(row, size), HALF + pair * 128 : HALF + (pair + 1) * 128]
        wide = jnp.concatenate([vals, jnp.ones((size, 128), BF)], axis=1)
        for side in (0, 1):
            slot = 2 * (pair % 2) + side
            top = jnp.concatenate([mx[slot]] * (size // 128), axis=1)
            power = jnp.exp2(s_ref[slot, :, pl.ds(column, size)] - top).astype(BF)
            new = dot_nn(power, wide)
            if first:
                acc[side] = new
            else:
                acc[side] += new

    def sweep(step):
        step(diag, TQ, 0, True)

        def some(index, carry):
            row = pl.multiple_of(extra_row + index * TQ, TQ)
            step(row, TQ, pl.multiple_of(TQ + index * TQ, TQ), False)
            return carry

        lax.fori_loop(0, extra, some, 0)

        def one(index, carry):
            row = pl.multiple_of(base + index * TK, TQ)
            step(row, TK, pl.multiple_of(TK + index * TK, TQ), False)
            return carry

        lax.fori_loop(0, tiles, one, 0)

    sweep(lambda row, size, column, first: score(0, row, size, column, first, first))
    for pair in range(PAIRS):
        settle(pair)

        def both(row, size, column, first):
            if pair + 1 < PAIRS:
                score(pair + 1, row, size, column, first, first)
            blend(pair, row, size, column, first)

        sweep(both)
        sides = []
        for side in (0, 1):
            total = acc[side][:, 128:]
            sides.append(acc[side][:, :128] / total)
            tall = jnp.transpose(mx[2 * (pair % 2) + side] + jnp.log2(total))
            lse_ref[0, 2 * pair + side] = tall[0]
        o_ref[:, pair * 128 : (pair + 1) * 128] = jnp.where(low, sides[0], sides[1]).astype(BF)


def attend_forward(info, q, kvp, kvc, TQ):
    rows = q.shape[0]
    keys = kvp.shape[0] + kvc.shape[0]
    blocks = rows // TQ
    return pl.pallas_call(
        attend_forward_kernel,
        grid_spec=pltpu.PrefetchScalarGridSpec(
            num_scalar_prefetch=1,
            grid=(blocks,),
            in_specs=[
                pl.BlockSpec((TQ, HALF), lambda i, s: (i, 0)),
                pl.BlockSpec(memory_space=pl.ANY),
                pl.BlockSpec(memory_space=pl.ANY),
            ],
            out_specs=[
                pl.BlockSpec((TQ, HALF), lambda i, s: (i, 0)),
                pl.BlockSpec((1, 8, TQ), lambda i, s: (i, 0, 0)),
            ],
            scratch_shapes=[
                pltpu.VMEM((keys, D), BF),
                pltpu.VMEM((NH, TQ, 128), BF),
                pltpu.VMEM((4, TQ, PLEN + TK), F32),
                pltpu.VMEM((4, TQ, 128), F32),
                pltpu.VMEM((2, TQ, 256), F32),
                pltpu.SemaphoreType.DMA((2,)),
            ],
        ),
        out_shape=(
            jax.ShapeDtypeStruct((rows, HALF), BF),
            jax.ShapeDtypeStruct((blocks, 8, TQ), F32),
        ),
        compiler_params=pltpu.CompilerParams(
            dimension_semantics=("arbitrary",), vmem_limit_bytes=50 << 20
        ),
        cost_estimate=pl.CostEstimate(
            flops=int(4 * rows * PLEN * HALF * 4), bytes_accessed=20 << 20, transcendentals=0
        ),
        name="attend_forward",
    )(info, q, kvp, kvc)


def attend_backward_kernel(
    info,
    q_ref,
    do_ref,
    o_ref,
    lse_ref,
    kvp_hbm,
    kvc_hbm,
    dq_ref,
    dkvp_hbm,
    dkvc_hbm,
    kv,
    kt,
    dkv,
    qm,
    dom,
    dqt,
    drow,
    sems,
):
    TQ = q_ref.shape[0]
    block = pl.program_id(0)
    prompt_rows = kvp_hbm.shape[0]
    cont_rows = kvc_hbm.shape[0]
    keys_all = prompt_rows + cont_rows

    @pl.when(block == 0)
    def _():
        one = pltpu.make_async_copy(kvp_hbm, kv.at[pl.ds(0, prompt_rows)], sems.at[0])
        two = pltpu.make_async_copy(kvc_hbm, kv.at[pl.ds(prompt_rows, cont_rows)], sems.at[1])
        one.start()
        two.start()
        one.wait()
        two.wait()

        def prepare(index, carry):
            row = pl.multiple_of(index * TQ, TQ)
            dkv[pl.ds(row, TQ), :] = jnp.zeros((TQ, D), F32)
            for pair in range(PAIRS):
                piece = kv[pl.ds(row, TQ), pair * 128 : (pair + 1) * 128]
                kt[pair * 128 : (pair + 1) * 128, pl.ds(row, TQ)] = jnp.transpose(
                    piece.astype(F32)
                ).astype(BF)
            return carry

        lax.fori_loop(0, keys_all // TQ, prepare, 0)

    base = pl.multiple_of(info[block, 0], TQ)
    tiles = info[block, 1]
    extra = info[block, 2]
    extra_row = pl.multiple_of(info[block, 3], TQ)
    diag = pl.multiple_of(info[block, 4], TQ)
    low, high = half_masks(TQ)
    zero = jnp.zeros((TQ, 128), BF)
    for pair in range(PAIRS):
        lanes = slice(pair * 128, (pair + 1) * 128)
        part = q_ref[:, lanes]
        qm[2 * pair] = jnp.where(low, part, zero)
        qm[2 * pair + 1] = jnp.where(high, part, zero)
        part = do_ref[:, lanes]
        dom[2 * pair] = jnp.where(low, part, zero)
        dom[2 * pair + 1] = jnp.where(high, part, zero)
        product = jnp.transpose(part.astype(F32) * o_ref[:, lanes].astype(F32))
        drow[2 * pair] = jnp.sum(product[:HEAD_DIM], axis=0)
        drow[2 * pair + 1] = jnp.sum(product[HEAD_DIM:], axis=0)

    def step(row, size, first):
        for pair in range(PAIRS):
            lanes = slice(pair * 128, (pair + 1) * 128)
            more = slice(HALF + pair * 128, HALF + (pair + 1) * 128)
            keys = kv[pl.ds(row, size), lanes]
            vals = kv[pl.ds(row, size), more]
            dk = None
            dv = None
            for side in (0, 1):
                head = 2 * pair + side
                raw = dot_nt(keys, qm[head])
                if first:
                    across = lax.broadcasted_iota(jnp.int32, (size, TQ), 1)
                    down = lax.broadcasted_iota(jnp.int32, (size, TQ), 0)
                    raw = jnp.where(down <= across, raw, MASKED)
                probs = jnp.exp2(raw - lse_ref[0, head : head + 1, :])
                grad = dot_nt(vals, dom[head])
                slope = (probs * (grad - drow[head : head + 1, :])).astype(BF)
                probs = probs.astype(BF)
                part_v = dot_nn(probs, dom[head])
                part_k = dot_nn(slope, qm[head])
                dv = part_v if dv is None else dv + part_v
                dk = part_k if dk is None else dk + part_k
                spot = slice(head * HEAD_DIM, (head + 1) * HEAD_DIM)
                new = dot_nn(kt[spot, pl.ds(row, size)], slope)
                if first:
                    dqt[spot, :] = new
                else:
                    dqt[spot, :] += new
            dkv[pl.ds(row, size), lanes] += dk
            dkv[pl.ds(row, size), more] += dv

    step(diag, TQ, True)

    def some(index, carry):
        step(pl.multiple_of(extra_row + index * TQ, TQ), TQ, False)
        return carry

    lax.fori_loop(0, extra, some, 0)

    def one(index, carry):
        step(pl.multiple_of(base + index * TK, TQ), TK, False)
        return carry

    lax.fori_loop(0, tiles, one, 0)
    for pair in range(PAIRS):
        lanes = slice(pair * 128, (pair + 1) * 128)
        dq_ref[:, lanes] = (jnp.transpose(dqt[lanes, :]) * HEAD_DIM ** (-0.5)).astype(BF)

    @pl.when(block == pl.num_programs(0) - 1)
    def _():
        def finish(index, carry):
            row = pl.multiple_of(index * TQ, TQ)
            kv[pl.ds(row, TQ), :HALF] = (dkv[pl.ds(row, TQ), :HALF] * (1.0 / LOG2E)).astype(BF)
            kv[pl.ds(row, TQ), HALF:] = dkv[pl.ds(row, TQ), HALF:].astype(BF)
            return carry

        lax.fori_loop(0, keys_all // TQ, finish, 0)
        one = pltpu.make_async_copy(kv.at[pl.ds(0, prompt_rows)], dkvp_hbm, sems.at[0])
        two = pltpu.make_async_copy(kv.at[pl.ds(prompt_rows, cont_rows)], dkvc_hbm, sems.at[1])
        one.start()
        two.start()
        one.wait()
        two.wait()


def attend_backward(info, q, do, o, lse, kvp, kvc, TQ):
    rows = q.shape[0]
    keys = kvp.shape[0] + kvc.shape[0]
    blocks = rows // TQ
    tile = pl.BlockSpec((TQ, HALF), lambda i, s: (i, 0))
    whole = pl.BlockSpec(memory_space=pl.ANY)
    return pl.pallas_call(
        attend_backward_kernel,
        grid_spec=pltpu.PrefetchScalarGridSpec(
            num_scalar_prefetch=1,
            grid=(blocks,),
            in_specs=[
                tile,
                tile,
                tile,
                pl.BlockSpec((1, 8, TQ), lambda i, s: (i, 0, 0)),
                whole,
                whole,
            ],
            out_specs=[tile, whole, whole],
            scratch_shapes=[
                pltpu.VMEM((keys, D), BF),
                pltpu.VMEM((HALF, keys), BF),
                pltpu.VMEM((keys, D), F32),
                pltpu.VMEM((NH, TQ, 128), BF),
                pltpu.VMEM((NH, TQ, 128), BF),
                pltpu.VMEM((HALF, TQ), F32),
                pltpu.VMEM((8, TQ), F32),
                pltpu.SemaphoreType.DMA((2,)),
            ],
        ),
        out_shape=(
            jax.ShapeDtypeStruct((rows, HALF), BF),
            jax.ShapeDtypeStruct(kvp.shape, BF),
            jax.ShapeDtypeStruct(kvc.shape, BF),
        ),
        compiler_params=pltpu.CompilerParams(
            dimension_semantics=("arbitrary",), vmem_limit_bytes=56 << 20
        ),
        cost_estimate=pl.CostEstimate(
            flops=int(10 * rows * PLEN * HALF * 4), bytes_accessed=30 << 20, transcendentals=0
        ),
        name="attend_backward",
    )(info, q, do, o, lse, kvp, kvc)


def normal_form(value):
    center = value - jnp.mean(value, axis=1, keepdims=True)
    return center * lax.rsqrt(jnp.mean(center * center, axis=1, keepdims=True) + EPSILON)


def flip(value):
    return jnp.transpose(value.astype(F32)).astype(BF)


def project_kernel(prompt_tiles, has, spot, xp_ref, xc_ref, w_ref, vec_ref, kvp_ref, kvc_ref, q_ref):
    step = pl.program_id(0)
    is_cont = step >= prompt_tiles
    x = jnp.where(is_cont, xc_ref[...].astype(F32), xp_ref[...].astype(F32))
    normed = (normal_form(x) * vec_ref[0:1, :] + vec_ref[1:2, :]).astype(BF)
    kv = (dot_nn(normed, w_ref[:, HALF : 3 * HALF]) + vec_ref[2:3, :]).astype(BF)

    @pl.when(jnp.logical_not(is_cont))
    def _():
        kvp_ref[...] = kv

    @pl.when(is_cont)
    def _():
        kvc_ref[...] = kv

    @pl.when(has[step] > 0)
    def _():
        query = dot_nn(normed, w_ref[:, :HALF]) + vec_ref[3:4, :HALF]
        q_ref[...] = (query * QSCALE).astype(BF)


def tile_specs(tile, prompt_tiles):
    prompts = pl.BlockSpec((tile, D), lambda i, h, s: (jnp.minimum(i, prompt_tiles - 1), 0))
    conts = pl.BlockSpec((tile, D), lambda i, h, s: (jnp.maximum(i - prompt_tiles, 0), 0))
    heads = pl.BlockSpec((tile, HALF), lambda i, h, s: (s[i], 0))
    return prompts, conts, heads


def project(has, spot, xp, xc, weight, vec, rows, tile):
    prompt_tiles = xp.shape[0] // tile
    steps = prompt_tiles + xc.shape[0] // tile
    prompts, conts, heads = tile_specs(tile, prompt_tiles)
    total = xp.shape[0] + xc.shape[0]
    return pl.pallas_call(
        functools.partial(project_kernel, prompt_tiles),
        grid_spec=pltpu.PrefetchScalarGridSpec(
            num_scalar_prefetch=2,
            grid=(steps,),
            in_specs=[
                prompts,
                conts,
                pl.BlockSpec(weight.shape, lambda i, h, s: (0, 0)),
                pl.BlockSpec(vec.shape, lambda i, h, s: (0, 0)),
            ],
            out_specs=[prompts, conts, heads],
        ),
        out_shape=(
            jax.ShapeDtypeStruct(xp.shape, BF),
            jax.ShapeDtypeStruct(xc.shape, BF),
            jax.ShapeDtypeStruct((rows, HALF), BF),
        ),
        compiler_params=pltpu.CompilerParams(
            dimension_semantics=("arbitrary",), vmem_limit_bytes=32 << 20
        ),
        cost_estimate=pl.CostEstimate(
            flops=2 * D * (total * D + rows * HALF), bytes_accessed=20 << 20, transcendentals=0
        ),
        name="project",
    )(has, spot, xp, xc, weight, vec)


def unproject_kernel(
    prompt_tiles,
    chained,
    has,
    spot,
    xp_ref,
    xc_ref,
    dkvp_ref,
    dkvc_ref,
    dq_ref,
    w_ref,
    vec_ref,
    *refs,
):
    if chained:
        old_w, old_vec, old_bias = refs[:3]
        refs = refs[3:]
    tp_ref, tc_ref, gw_ref, gvec_ref, gbias_ref = refs
    step = pl.program_id(0)
    is_cont = step >= prompt_tiles

    @pl.when(step == 0)
    def _():
        if chained:
            gw_ref[...] = old_w[...]
            gvec_ref[...] = old_vec[...]
            gbias_ref[...] = old_bias[...]
        else:
            gw_ref[...] = jnp.zeros_like(gw_ref)
            gvec_ref[...] = jnp.zeros_like(gvec_ref)
            gbias_ref[...] = jnp.zeros_like(gbias_ref)

    x = jnp.where(is_cont, xc_ref[...].astype(F32), xp_ref[...].astype(F32))
    hat = normal_form(x)
    normed_t = flip(hat * vec_ref[0:1, :] + vec_ref[1:2, :])
    dkv = jnp.where(is_cont, dkvc_ref[...].astype(F32), dkvp_ref[...].astype(F32)).astype(BF)
    gw_ref[:, HALF : 3 * HALF] += dot_nn(normed_t, dkv)
    gbias_ref[0:1, HALF : 3 * HALF] += jnp.sum(dkv.astype(F32), axis=0, keepdims=True)
    table = dot_nt(dkv, w_ref[:, HALF : 3 * HALF])

    def finish(value):
        gvec_ref[0:1, :] += jnp.sum(value * hat, axis=0, keepdims=True)
        gvec_ref[1:2, :] += jnp.sum(value, axis=0, keepdims=True)
        value = value.astype(BF)

        @pl.when(jnp.logical_not(is_cont))
        def _():
            tp_ref[...] = value

        @pl.when(is_cont)
        def _():
            tc_ref[...] = value

    @pl.when(has[step] == 0)
    def _():
        finish(table)

    @pl.when(has[step] > 0)
    def _():
        dq = dq_ref[...]
        gw_ref[:, :HALF] += dot_nn(normed_t, dq)
        gbias_ref[0:1, :HALF] += jnp.sum(dq.astype(F32), axis=0, keepdims=True)
        finish(table + dot_nt(dq, w_ref[:, :HALF]))


def unproject(has, spot, xp, xc, dkvp, dkvc, dq, weight, vec, totals, tile):
    prompt_tiles = xp.shape[0] // tile
    steps = prompt_tiles + xc.shape[0] // tile
    prompts, conts, heads = tile_specs(tile, prompt_tiles)
    total = xp.shape[0] + xc.shape[0]
    shapes = ((D, 3 * HALF), (8, D), (8, 3 * HALF))
    fixed = [pl.BlockSpec(shape, lambda i, h, s: (0, 0)) for shape in shapes]
    extra = () if totals is None else tuple(totals)
    return pl.pallas_call(
        functools.partial(unproject_kernel, prompt_tiles, totals is not None),
        grid_spec=pltpu.PrefetchScalarGridSpec(
            num_scalar_prefetch=2,
            grid=(steps,),
            in_specs=[
                prompts,
                conts,
                prompts,
                conts,
                heads,
                pl.BlockSpec(weight.shape, lambda i, h, s: (0, 0)),
                pl.BlockSpec(vec.shape, lambda i, h, s: (0, 0)),
            ]
            + (fixed if extra else []),
            out_specs=[prompts, conts] + fixed,
        ),
        out_shape=(
            jax.ShapeDtypeStruct(xp.shape, BF),
            jax.ShapeDtypeStruct(xc.shape, BF),
        )
        + tuple(jax.ShapeDtypeStruct(shape, F32) for shape in shapes),
        compiler_params=pltpu.CompilerParams(
            dimension_semantics=("arbitrary",), vmem_limit_bytes=40 << 20
        ),
        cost_estimate=pl.CostEstimate(
            flops=4 * D * (total * D + dq.shape[0] * HALF), bytes_accessed=30 << 20, transcendentals=0
        ),
        name="unproject",
    )(has, spot, xp, xc, dkvp, dkvc, dq, weight, vec, *extra)


def gelu_parts(value):
    rate = math.sqrt(2.0 / math.pi)
    square = value * value
    half = 0.5 + 0.5 * jnp.tanh(value * (rate + (rate * 0.044715) * square))
    slope = half + value * (half * (1.0 - half)) * (2.0 * rate + (6.0 * rate * 0.044715) * square)
    return value * half, slope


def feed_forward_kernel(
    prompt_parts,
    clen,
    count,
    groups,
    lens,
    places,
    xp_ref,
    xc_ref,
    gp_ref,
    gc_ref,
    mine_ref,
    mate_ref,
    vec_ref,
    bfc_ref,
    *refs,
):
    pieces = refs[:count]
    (
        fp_ref,
        fc_ref,
        hp_ref,
        hc_ref,
        dmine_ref,
        dmate_ref,
        gvec_ref,
        gbfc_ref,
        grads_hbm,
        wp,
        wfc,
        wout,
        ap,
        afc,
        aout,
        stage,
        sems,
    ) = refs[count:]
    core = places[0]
    batch = pl.program_id(0)
    part = pl.program_id(1)
    tile = mine_ref.shape[1]
    is_cont = part >= prompt_parts
    begin = (batch == 0) & (part == 0)

    @pl.when(begin)
    def _():
        loads = []
        for index, piece in enumerate(pieces):
            size = piece.shape[1]
            for inner in range(piece.shape[0]):
                row = pl.multiple_of(places[1 + index * piece.shape[0] + inner], 16)
                turned = pl.multiple_of(lax.rem(row + core * HALF, D), 16)
                source = piece.at[inner]
                moves = [
                    (source.at[:, pl.ds(0, D)], wp.at[pl.ds(turned, size), :]),
                    (source.at[:, pl.ds(D, FF)], wfc.at[pl.ds(row, size), :]),
                ]
                for block in range(FF // D):
                    moves.append(
                        (
                            source.at[:, pl.ds(D + FF + block * D, D)],
                            wout.at[pl.ds(block * D + row, size), :],
                        )
                    )
                for one, two in moves:
                    loads.append(pltpu.make_async_copy(one, two, sems.at[len(loads)]))
        for load in loads:
            load.start()
        ap[...] = jnp.zeros_like(ap)
        gvec_ref[...] = jnp.zeros_like(gvec_ref)
        gbfc_ref[...] = jnp.zeros_like(gbfc_ref)

        def clear(index, carry):
            row = pl.multiple_of(index * 64, 64)
            afc[pl.ds(row, 64), :] = jnp.zeros((64, FF), F32)
            aout[pl.ds(row, 64), :] = jnp.zeros((64, FF), F32)
            return carry

        lax.fori_loop(0, D // 64, clear, 0)
        for load in loads:
            load.wait()

    b_proj = vec_ref[0:1, :]
    gain = vec_ref[1:2, :]
    shift = vec_ref[2:3, :]
    b_out = vec_ref[3:4, :]
    x = jnp.where(is_cont, xc_ref[0].astype(F32), xp_ref[0].astype(F32))
    gy = jnp.where(is_cont, gc_ref[0].astype(F32), gp_ref[0].astype(F32))
    start = jnp.maximum(part - prompt_parts, 0) * tile
    length = lens[batch, start // clen]
    place = lax.broadcasted_iota(jnp.int32, (tile, 1), 0) + start % clen
    valid = jnp.where(jnp.logical_not(is_cont) | (place < length), 1.0, 0.0)

    mine = mine_ref[0]
    mate = mate_ref[0]
    h = x + valid * (dot_nn(mine, wp[:HALF, :]) + dot_nn(mate, wp[HALF:, :]) + b_proj)
    center = h - jnp.mean(h, axis=1, keepdims=True)
    rate = lax.rsqrt(jnp.mean(center * center, axis=1, keepdims=True) + EPSILON)
    hat = center * rate
    second = (hat * gain + shift).astype(BF)
    dz_full = valid * gy
    dz = dz_full.astype(BF)
    second_t = flip(second)
    dz_t = flip(dz)
    result = None
    back = None
    for index in range(FF // D):
        cols = slice(index * D, (index + 1) * D)
        inner = dot_nn(second, wfc[:, cols]) + bfc_ref[:, cols]
        act, slope = gelu_parts(inner)
        act = act.astype(BF)
        du_full = dot_nt(dz, wout[cols, :]) * slope
        du = du_full.astype(BF)
        gbfc_ref[0:1, cols] += jnp.sum(du_full, axis=0, keepdims=True)
        new = dot_nn(act, wout[cols, :])
        result = new if result is None else result + new
        new = dot_nt(du, wfc[:, cols])
        back = new if back is None else back + new
        aout[:, cols] += dot_nn(dz_t, act)
        afc[:, cols] += dot_nn(second_t, du)
    final = (h + valid * (result + b_out)).astype(BF)
    e2 = back * gain
    dh = gy + rate * (
        e2
        - jnp.mean(e2, axis=1, keepdims=True)
        - hat * jnp.mean(e2 * hat, axis=1, keepdims=True)
    )
    dy_full = valid * dh
    dy = dy_full.astype(BF)
    gvec_ref[0:1, :] += jnp.sum(dy_full, axis=0, keepdims=True)
    gvec_ref[1:2, :] += jnp.sum(back * hat, axis=0, keepdims=True)
    gvec_ref[2:3, :] += jnp.sum(back, axis=0, keepdims=True)
    gvec_ref[3:4, :] += jnp.sum(dz.astype(F32), axis=0, keepdims=True)
    ap[:HALF, :] += dot_nn(flip(mine), dy)
    ap[HALF:, :] += dot_nn(flip(mate), dy)
    dmine_ref[0] = dot_nt(dy, wp[:HALF, :]).astype(BF)
    dmate_ref[0] = dot_nt(dy, wp[HALF:, :]).astype(BF)
    dh = dh.astype(BF)

    @pl.when(jnp.logical_not(is_cont))
    def _():
        fp_ref[0] = final
        hp_ref[0] = dh

    @pl.when(is_cont)
    def _():
        fc_ref[0] = final
        hc_ref[0] = dh

    @pl.when((batch == pl.num_programs(0) - 1) & (part == pl.num_programs(1) - 1))
    def _():
        blocks, share = stage.shape[1], stage.shape[2]
        sends = []

        def send(column, fetch):
            slot = len(sends) % 2
            if len(sends) >= 2:
                sends[-2].wait()
            for block in range(blocks):
                stage[slot, block] = fetch(block).astype(BF)
            sends.append(
                pltpu.make_async_copy(
                    stage.at[slot], grads_hbm.at[:, :, pl.ds(column, D)], sems.at[slot]
                )
            )
            sends[-1].start()

        def first_row(block):
            return (block % groups * (blocks // groups) + block // groups) * share

        def proj_rows(block):
            row = lax.rem(first_row(block) + core * HALF, D)
            return ap[pl.ds(pl.multiple_of(row, math.gcd(share, HALF)), share), :]

        send(0, proj_rows)
        for part_of in range(FF // D):
            cols = slice(part_of * D, (part_of + 1) * D)
            send(D + part_of * D, lambda block: afc[first_row(block) : first_row(block) + share, cols])
        for part_of in range(FF // D):
            cols = slice(part_of * D, (part_of + 1) * D)
            ap[...] = jnp.transpose(aout[:, cols])
            send(
                D + FF + part_of * D,
                lambda block: ap[first_row(block) : first_row(block) + share, :],
            )
        for copy in sends[-2:]:
            copy.wait()


def feed_forward(lens, places, prompt_in, cont_in, prompt_cot, cont_cot, mine, mate, vec, bfc, pieces, groups, share):
    prow = prompt_in.shape[1]
    crow = cont_in.shape[1]
    clen = crow // lens.shape[1]
    tile = min(256, prow, clen)
    prompt_parts = prow // tile
    parts = prompt_parts + crow // tile
    prompts = pl.BlockSpec((1, tile, D), lambda m, i, s, t: (m, jnp.minimum(i, prompt_parts - 1), 0))
    conts = pl.BlockSpec((1, tile, D), lambda m, i, s, t: (m, jnp.maximum(i - prompt_parts, 0), 0))
    heads = pl.BlockSpec((1, tile, HALF), lambda m, i, s, t: (m, i, 0))
    whole = pl.BlockSpec(memory_space=pl.ANY)
    fixed = pl.BlockSpec((8, D), lambda m, i, s, t: (0, 0))
    long = pl.BlockSpec((8, FF), lambda m, i, s, t: (0, 0))
    shape = jax.ShapeDtypeStruct
    rows = MB * (prow + crow)
    return pl.pallas_call(
        functools.partial(feed_forward_kernel, prompt_parts, clen, len(pieces), groups),
        grid_spec=pltpu.PrefetchScalarGridSpec(
            num_scalar_prefetch=2,
            grid=(MB, parts),
            in_specs=[
                prompts,
                conts,
                prompts,
                conts,
                heads,
                heads,
                fixed,
                pl.BlockSpec((1, FF), lambda m, i, s, t: (0, 0)),
            ]
            + [whole] * len(pieces),
            out_specs=[prompts, conts, prompts, conts, heads, heads, fixed, long, whole],
            scratch_shapes=[
                pltpu.VMEM((D, D), BF),
                pltpu.VMEM((D, FF), BF),
                pltpu.VMEM((FF, D), BF),
                pltpu.VMEM((D, D), F32),
                pltpu.VMEM((D, FF), F32),
                pltpu.VMEM((D, FF), F32),
                pltpu.VMEM((2, D // share, share, D), BF),
                pltpu.SemaphoreType.DMA(
                    (max(16, (2 + FF // D) * sum(piece.shape[0] for piece in pieces)),)
                ),
            ],
        ),
        out_shape=(
            shape(prompt_in.shape, BF),
            shape(cont_in.shape, BF),
            shape(prompt_in.shape, BF),
            shape(cont_in.shape, BF),
            shape(mine.shape, BF),
            shape(mate.shape, BF),
            shape((8, D), F32),
            shape((8, FF), F32),
            shape((D // share, share, D + 2 * FF), BF),
        ),
        compiler_params=pltpu.CompilerParams(
            dimension_semantics=("arbitrary", "arbitrary"), vmem_limit_bytes=63 << 20
        ),
        cost_estimate=pl.CostEstimate(
            flops=6 * rows * (D * D + 2 * D * FF), bytes_accessed=50 << 20, transcendentals=0
        ),
        name="feed_forward",
    )(lens, places, prompt_in, cont_in, prompt_cot, cont_cot, mine, mate, vec, bfc, *pieces)


HEAD_COLS = 3 * HALF
SMALL_COLS = 128


def neighbour(value, axis, distance):
    pairs = [(i, i ^ distance) for i in range(lax.axis_size(axis))]
    return lax.ppermute(value, axis, pairs)


def swap(value):
    return neighbour(value, "fsdp", 1)


def is_square():
    return lax.axis_size("grp") == 4 and lax.axis_size("fsdp") == 8


def square_halves(block):
    half = block.shape[0] // 2
    pieces = []
    for index, (one, two) in enumerate(((1, 2), (2, 1))):
        piece = block[index * half : (index + 1) * half]
        both = jnp.stack([piece, neighbour(piece, "grp", one)])
        far = neighbour(both, "grp", two)
        pieces.append((both, (0, one), index))
        pieces.append((far, (two, 3), index))
    return pieces


def gather_parameters(packed, core):
    own = lax.axis_index("grp")
    cut = 3 * D + SMALL_COLS
    if not is_square():
        whole = lax.all_gather(packed, ALL, axis=0, tiled=True)
        heads = lax.dynamic_slice_in_dim(whole[:, : 3 * D], core * HEAD_COLS, HEAD_COLS, 1)
        front = jnp.concatenate([heads, whole[:, 3 * D : cut]], axis=1)
        return front, [whole[:, cut:].reshape(2, HALF, -1)], [0, HALF], whole
    zone = lax.all_gather(packed, "fsdp", axis=0, tiled=True)
    group_rows = zone.shape[0]
    heads = lax.dynamic_slice_in_dim(zone[:, : 3 * D], core * HEAD_COLS, HEAD_COLS, 1)
    parts = {}
    for both, offsets, index in square_halves(
        jnp.concatenate([heads, zone[:, 3 * D : cut]], axis=1)
    ):
        for which, offset in enumerate(offsets):
            parts[offset, index] = both[which]
    table = jnp.stack([jnp.concatenate([parts[k, 0], parts[k, 1]], axis=0) for k in range(4)])
    front = jnp.concatenate(
        [lax.dynamic_index_in_dim(table, own ^ k, 0, keepdims=False) for k in range(4)], axis=0
    )
    half = group_rows // 2
    rest = lax.dynamic_slice(zone, (core * half, cut), (half, zone.shape[1] - cut))
    pieces, rows = [], []
    for both, offsets, index in square_halves(rest):
        for source, side in ((both, core), (swap(both), 1 - core)):
            pieces.append(source)
            for offset in offsets:
                rows.append((own ^ offset) * group_rows + side * half + index * (half // 2))
    return front, pieces, rows, zone


def pick(array, index, axis):
    return lax.dynamic_index_in_dim(array, index, axis, keepdims=False)


def meet(array, index, axis, name, distance):
    other = neighbour(pick(array, 1 - index, axis), name, distance)
    return (pick(array, index, axis).astype(F32) + other.astype(F32)).astype(BF)


def reduce_steps():
    if not is_square():
        groups = [list(range(c, lax.axis_size("fsdp"), 2)) for c in (0, 1)]

        def along_grp(value):
            return lax.psum_scatter(value, "grp", scatter_dimension=0, tiled=True)

        def along_chips(value):
            return lax.psum_scatter(
                value, "fsdp", scatter_dimension=0, tiled=True, axis_index_groups=groups
            )

        return [along_grp, along_chips]

    own = lax.axis_index("grp")
    x, y = own % 2, own // 2
    z = lax.axis_index("fsdp") // 2

    def one(value):
        value = value.reshape(2, 2, 2, value.shape[0] // 8, value.shape[1])
        return meet(value[:, :, 0], x, 1, "grp", 1), meet(value[:, :, 1], y, 0, "grp", 2)

    def two(pair):
        value = jnp.concatenate(
            [meet(pair[0], y, 0, "grp", 2), meet(pair[1], x, 0, "grp", 1)], axis=0
        )
        return value.reshape(2, 2, value.shape[0] // 4, value.shape[1])

    def three(value):
        return meet(value, z % 2, 1, "fsdp", 2)

    def four(value):
        return meet(value, z // 2, 0, "fsdp", 4)

    return [one, two, three, four]


def reduce_parameters(value):
    for step in reduce_steps():
        value = step(value)
    return value


def own_rows(value, core):
    share = value.shape[0] // 2
    keep = lax.dynamic_slice_in_dim(value, core * share, share, 0)
    other = swap(lax.dynamic_slice_in_dim(value, (1 - core) * share, share, 0))
    return keep, other


def pin(first, second):
    return lax.optimization_barrier((first, second))


def square_steps(core):
    own = lax.axis_index("grp")
    x, y = own % 2, own // 2

    def one(value):
        cols = value.shape[-1] // 2
        value = value.reshape((2, 2) + value.shape[1:])
        return (
            meet(value[..., :cols], x, 1, "grp", 1),
            meet(value[..., cols:], y, 0, "grp", 2),
        )

    def two(pair):
        return jnp.concatenate(
            [meet(pair[0], y, 0, "grp", 2), meet(pair[1], x, 0, "grp", 1)], axis=1
        )

    return [one, two]


def body(
    prompt_in,
    cont_in,
    prompt_cot,
    cont_cot,
    cont_prompt,
    cont_len,
    ln1_gain,
    ln1_bias,
    attn_weight,
    attn_bias,
    proj_weight,
    proj_bias,
    ln2_gain,
    ln2_bias,
    fc_weight,
    fc_bias,
    out_weight,
    out_bias,
):
    fsdp = lax.axis_size("fsdp")
    devices = fsdp * lax.axis_size("grp")
    prow = prompt_in.shape[1]
    crow = cont_in.shape[1]
    conts = cont_prompt.shape[2]
    clen = crow // conts
    mine = prow + crow
    TQ = min(256, prow, clen)
    prompt_rows = NPR * PLEN
    place = lax.axis_index("fsdp")
    core = place % 2
    share = D // devices
    wide = FF // D

    vectors = (ln1_gain, ln1_bias, attn_bias[0], attn_bias[1], proj_bias, ln2_gain, ln2_bias, out_bias)
    columns = jnp.concatenate(
        [v[:, None] for v in vectors] + [fc_bias.reshape(wide, share).T], axis=1
    )
    columns = jnp.pad(columns, ((0, 0), (0, SMALL_COLS - columns.shape[1])))
    packed = jnp.concatenate(
        [
            attn_weight.reshape(share, 3, 2, HALF).transpose(0, 2, 1, 3).reshape(share, 3 * D),
            columns,
            proj_weight,
            fc_weight.reshape(share, devices, wide, share).transpose(0, 2, 1, 3).reshape(share, FF),
            out_weight.reshape(wide, share, D).transpose(1, 0, 2).reshape(share, FF),
        ],
        axis=1,
    ).astype(BF)
    front, pieces, piece_rows, zone = gather_parameters(packed, core)
    w_heads = front[:, :HEAD_COLS]
    small = front[:, HEAD_COLS:].astype(F32)
    gain_a, shift_a, bias_q, bias_v, b_proj, gain_b, shift_b, b_out = (small[:, i] for i in range(8))
    b_fc = small[:, 8 : 8 + wide].T.reshape(1, FF)
    bias_q = lax.dynamic_slice_in_dim(bias_q, core * HALF, HALF)
    bias_v = lax.dynamic_slice_in_dim(bias_v, core * HALF, HALF)
    none = jnp.zeros((HALF,), F32)
    vec_a = jnp.stack(
        [gain_a, shift_a, jnp.concatenate([none, bias_v]), jnp.concatenate([bias_q, none])]
        + [jnp.zeros((D,), F32)] * 4
    )
    vec_b = jnp.pad(jnp.stack([b_proj, gain_b, shift_b, b_out]), ((0, 4), (0, 0)))

    prompt_all = [lax.all_gather(prompt_in[m], "fsdp", axis=0, tiled=True) for m in range(MB)]
    cont_mate = swap(cont_in)
    plan_mate = swap(cont_prompt[:, 0, :].astype(F32)).astype(jnp.int32)

    own_row = place * prow
    mate_row = (place + 1 - 2 * core) * prow

    def prompt_plan(row):
        row = row + TQ * jnp.arange(prow // TQ)
        spot = row % PLEN
        return jnp.stack(
            [
                row - spot,
                spot // TK,
                spot % TK // TQ,
                row - spot + spot // TK * TK,
                row,
            ],
            axis=1,
        )

    def cont_plan(follows, first):
        blocks = clen // TQ
        follows = jnp.repeat(follows, blocks)
        index = jnp.arange(conts * blocks)
        begin = prompt_rows + first + index // blocks * clen
        return jnp.stack(
            [
                follows * PLEN,
                jnp.full(index.shape, PLEN // TK),
                index % blocks,
                begin,
                begin + index % blocks * TQ,
            ],
            axis=1,
        )

    def plan_of(m):
        return jnp.concatenate(
            [
                prompt_plan(own_row),
                cont_plan(cont_prompt[m, 0], 0),
                prompt_plan(mate_row),
                cont_plan(plan_mate[m], crow),
            ],
            axis=0,
        ).astype(jnp.int32)

    tiles = (prompt_rows + 2 * crow) // TQ
    index = jnp.arange(tiles)
    part, cpart = prow // TQ, crow // TQ
    own_tile, mate_tile, cont_tile = own_row // TQ, mate_row // TQ, prompt_rows // TQ
    is_own = (index >= own_tile) & (index < own_tile + part)
    is_mate = (index >= mate_tile) & (index < mate_tile + part)
    is_cont = index >= cont_tile
    has = (is_own | is_mate | is_cont).astype(jnp.int32)
    order_own = index - own_tile
    order_mate = index - mate_tile + part + cpart
    order_cont = index - cont_tile
    order_cont = jnp.where(order_cont < cpart, part + order_cont, 2 * part + order_cont)
    exact = jnp.where(is_cont, order_cont, jnp.where(is_own, order_own, order_mate))
    first_tile = jnp.minimum(own_tile, mate_tile)
    clipped = jnp.clip(index, first_tile, first_tile + 2 * part - 1)
    early_spot = jnp.where(
        (clipped >= own_tile) & (clipped < own_tile + part),
        clipped - own_tile,
        clipped - mate_tile + part + cpart,
    )
    spot = jnp.where(is_cont, exact, early_spot).astype(jnp.int32)

    saved = []
    outs_mine = []
    outs_mate = []
    for m in range(MB):
        x_prompt = prompt_all[m]
        if m > 0:
            x_prompt, saved[-1][-1] = pin(x_prompt, saved[-1][-1])
        x_cont = jnp.concatenate([cont_in[m], cont_mate[m]], axis=0)
        kvp, kvc, query = project(has, spot, x_prompt, x_cont, w_heads, vec_a, 2 * mine, TQ)
        plan = plan_of(m)
        o, lse = attend_forward(plan, query, kvp, kvc, TQ)
        outs_mine.append(o[:mine])
        outs_mate.append(swap(o[mine:]))
        saved.append([x_prompt, x_cont, kvp, kvc, query, plan, o, lse])

    groups, block_share = (4, share) if is_square() else (1, 8)
    places = jnp.stack([core] + [jnp.asarray(row, jnp.int32) for row in piece_rows]).astype(jnp.int32)
    (
        prompt_out,
        cont_out,
        prompt_dh,
        cont_dh,
        d_mine,
        d_mate,
        g_vec,
        g_fc_bias,
        g_rest,
    ) = feed_forward(
        cont_len[:, 0, :],
        places,
        prompt_in,
        cont_in,
        prompt_cot,
        cont_cot,
        jnp.stack(outs_mine),
        jnp.stack(outs_mate),
        vec_b,
        b_fc,
        pieces,
        groups,
        block_share,
    )
    d_back = swap(d_mate)
    moves = []
    if is_square():
        g_rest = lax.psum_scatter(g_rest, "fsdp", scatter_dimension=0, tiled=True)
        moves = square_steps(core)
    else:
        g_rest = lax.psum_scatter(g_rest.reshape(D, D + 2 * FF), ALL, scatter_dimension=0, tiled=True)
    early = [g_rest]

    def advance(held):
        if moves:
            early[0] = moves.pop(0)(early[0])
            held, early[0] = pin(held, early[0])
        return held

    totals = None
    tables = []
    conts_back = []
    for m in range(MB):
        x_prompt, x_cont, kvp, kvc, query, plan, o, lse = saved[m]
        do = jnp.concatenate([d_mine[m], d_back[m]], axis=0)
        if m > 0:
            do, tables[-1] = pin(do, tables[-1])
            tables[-1] = lax.psum_scatter(tables[-1], "fsdp", scatter_dimension=0, tiled=True)
        if m > 1:
            do, tables[m - 2] = pin(do, tables[m - 2])
        dq, dkvp, dkvc = attend_backward(plan, query, do, o, lse, kvp, kvc, TQ)
        if m > 0:
            dkvp = advance(dkvp)
        table, table_cont, *totals = unproject(
            has, spot, x_prompt, x_cont, dkvp, dkvc, dq, w_heads, vec_a, totals, TQ
        )
        tables.append(table)
        conts_back.append(
            table_cont[:crow].astype(F32) + swap(table_cont[crow:]).astype(F32)
        )
    if MB > 1:
        tables[-1], tables[-2] = pin(tables[-1], tables[-2])
    tables[-1] = lax.psum_scatter(tables[-1], "fsdp", scatter_dimension=0, tiled=True)
    while moves:
        early[0] = moves.pop(0)(early[0])
    g_heads, g_first, g_bias = totals

    def spread(value):
        return jnp.where((jnp.arange(2) == core)[:, None], value[None, :], 0.0).reshape(D)

    sums = jnp.stack(
        [
            g_first[0],
            g_first[1],
            spread(g_bias[0, :HALF]),
            spread(g_bias[0, 2 * HALF :]),
            g_vec[0],
            g_vec[1],
            g_vec[2],
            g_vec[3],
        ]
        + [g_fc_bias[0, i * D : (i + 1) * D] for i in range(wide)],
        axis=0,
    )
    sums_high = sums.astype(BF)
    sums_low = (sums - sums_high.astype(F32)).astype(BF)
    count = sums.shape[0]
    sums = jnp.concatenate(
        [sums_high, sums_low, jnp.zeros((SMALL_COLS - 2 * count, D), BF)], axis=0
    ).T
    late = reduce_parameters(jnp.concatenate([g_heads.astype(BF), sums], axis=1))
    late_own, late_other = own_rows(late, core)
    sums = late_own[:, HEAD_COLS:].astype(F32) + late_other[:, HEAD_COLS:].astype(F32)
    sums = (sums[:, :count] + sums[:, count : 2 * count]).T

    def by_core(own, other):
        return jnp.where(core == 0, own, other), jnp.where(core == 0, other, own)

    late = jnp.stack(by_core(late_own[:, :HEAD_COLS], late_other[:, :HEAD_COLS]), axis=1)
    late = late.reshape(share, 2, 3, HALF).transpose(0, 2, 1, 3).reshape(share, 3 * D)
    early = early[0].astype(F32)
    g_fc = early[:, D : D + FF].reshape(share, wide, devices, share)
    g_fc = g_fc.transpose(0, 2, 1, 3).reshape(share, FF)
    g_out = early[:, D + FF :].reshape(share, wide, D).transpose(1, 0, 2).reshape(share * wide, D)

    def input_grad(source, slope, change):
        source = source.astype(F32)
        center = source - jnp.mean(source, axis=-1, keepdims=True)
        rate = lax.rsqrt(jnp.mean(center * center, axis=-1, keepdims=True) + EPSILON)
        hat = center * rate
        e1 = change * gain_a
        change = e1 - jnp.mean(e1, axis=-1, keepdims=True)
        change = change - hat * jnp.mean(e1 * hat, axis=-1, keepdims=True)
        return (slope.astype(F32) + rate * change).astype(BF)

    prompt_grad = jnp.stack(
        [input_grad(prompt_in[m], prompt_dh[m], tables[m].astype(F32)) for m in range(MB)]
    )
    cont_grad = jnp.stack([input_grad(cont_in[m], cont_dh[m], conts_back[m]) for m in range(MB)])
    return (
        prompt_out,
        cont_out,
        prompt_grad,
        cont_grad,
        sums[0],
        sums[1],
        late.astype(F32),
        sums[2:4],
        early[:, :D],
        sums[4],
        sums[5],
        sums[6],
        g_fc,
        sums[8:].reshape(share * wide),
        g_out,
        sums[7],
    )


def solution(mesh):
    rows = P(None, ALL, None)
    conts = P(None, "grp", "fsdp")
    vector = P(ALL)
    matrix = P(ALL, None)
    pair = P(None, ALL)
    params = (
        vector,
        vector,
        matrix,
        pair,
        matrix,
        vector,
        vector,
        vector,
        matrix,
        vector,
        matrix,
        vector,
    )
    return jax.shard_map(
        body,
        mesh=mesh,
        in_specs=(rows, rows, rows, rows, conts, conts) + params,
        out_specs=(rows, rows, rows, rows) + params,
        check_vma=False,
    )
```

```python
import functools
import math

import jax
import jax.numpy as jnp
from jax import lax
from jax.experimental import pallas as pl
from jax.experimental.pallas import tpu as pltpu
from jax.sharding import PartitionSpec as P

D = 768
HEADS = 12
HEAD_DIM = 64
FF = 3072
MB = 3
NPR = 2
PLEN = 2048
ALL = ("grp", "fsdp")

EPSILON = 1e-05
MASKED = -1e30
BF = jnp.bfloat16
F32 = jnp.float32

HALF = D // 2
NH = HEADS // 2
PAIRS = NH // 2
TK = 512
LOG2E = math.log2(math.e)
QSCALE = HEAD_DIM ** (-0.5) * LOG2E


def dot_nt(a, b):
    return lax.dot_general(a, b, (((1,), (1,)), ((), ())), preferred_element_type=F32)


def dot_nn(a, b):
    return lax.dot_general(a, b, (((1,), (0,)), ((), ())), preferred_element_type=F32)


def half_masks(rows):
    lane = lax.broadcasted_iota(jnp.int32, (rows, 128), 1)
    return (lane < HEAD_DIM, lane >= HEAD_DIM)


def normal_form(value):
    center = value - jnp.mean(value, axis=1, keepdims=True)
    return center * lax.rsqrt(jnp.mean(center * center, axis=1, keepdims=True) + EPSILON)


def flip(value):
    return jnp.transpose(value.astype(F32)).astype(BF)


def stream_rows(xp_hbm, xc_hbm, rows, sems, visit):
    size = rows.shape[1]
    count = xp_hbm.shape[0] // size
    crow = xc_hbm.shape[0] // 2
    part = min(size, crow)

    def fetch(index, slot):
        row = pl.multiple_of(index * size, size)
        return pltpu.make_async_copy(xp_hbm.at[pl.ds(row, size)], rows.at[slot], sems.at[slot])

    fetch(0, 0).start()

    def one(index, carry):
        slot = lax.rem(index, 2)

        @pl.when(index + 1 < count)
        def _():
            fetch(index + 1, 1 - slot).start()

        fetch(index, slot).wait()
        visit(pl.multiple_of(index * size, size), size, rows[slot].astype(F32))
        return carry

    lax.fori_loop(0, count, one, 0)
    for index in range(2 * crow // part):
        copy = pltpu.make_async_copy(
            xc_hbm.at[pl.ds(index * part, part)], rows.at[0, pl.ds(0, part)], sems.at[0]
        )
        copy.start()
        copy.wait()
        visit(count * size + index * part, part, rows[0, :part].astype(F32))


def attend_forward_kernel(
    info,
    spot,
    xp_hbm,
    xc_hbm,
    xqp_ref,
    xqc_ref,
    w_ref,
    vec_ref,
    o_ref,
    lse_ref,
    q_ref,
    kv_hbm,
    kv,
    rows,
    qm,
    s_ref,
    mx,
    acc,
    sems,
    done,
):
    block = pl.program_id(0)
    gain, shift, bias_kv, bias_q = (vec_ref[i : i + 1, :] for i in range(4))

    def store(row, size):
        index = row // rows.shape[1]
        if isinstance(row, int):
            index = xp_hbm.shape[0] // rows.shape[1] + (row - xp_hbm.shape[0]) // size
        return pltpu.make_async_copy(
            kv.at[pl.ds(row, size)], kv_hbm.at[pl.ds(row, size)], done.at[index]
        )

    @pl.when(block == 0)
    def _():
        def visit(row, size, x):
            normed = (normal_form(x) * gain + shift).astype(BF)
            kv[pl.ds(row, size), :] = (dot_nn(normed, w_ref[:, HALF:]) + bias_kv).astype(BF)
            store(row, size).start()

        stream_rows(xp_hbm, xc_hbm, rows, sems, visit)

    TQ = q_ref.shape[0]
    x = jnp.where(spot[block, 0] > 0, xqc_ref[...].astype(F32), xqp_ref[...].astype(F32))
    normed = (normal_form(x) * gain + shift).astype(BF)
    query = ((dot_nn(normed, w_ref[:, :HALF]) + bias_q[:, :HALF]) * QSCALE).astype(BF)
    q_ref[...] = query
    base = pl.multiple_of(info[block, 0], TQ)
    tiles = info[block, 1]
    extra = info[block, 2]
    extra_row = pl.multiple_of(info[block, 3], TQ)
    diag = pl.multiple_of(info[block, 4], TQ)
    low, high = half_masks(TQ)
    zero = jnp.zeros((TQ, 128), BF)
    for pair in range(PAIRS):
        part = query[:, pair * 128 : (pair + 1) * 128]
        qm[2 * pair] = jnp.where(low, part, zero)
        qm[2 * pair + 1] = jnp.where(high, part, zero)

    def score(pair, row, size, column, first, masked):
        keys = kv[pl.ds(row, size), pair * 128 : (pair + 1) * 128]
        for side in (0, 1):
            raw = dot_nt(qm[2 * pair + side], keys)
            if masked:
                across = lax.broadcasted_iota(jnp.int32, (TQ, size), 1)
                down = lax.broadcasted_iota(jnp.int32, (TQ, size), 0)
                raw = jnp.where(across <= down, raw, MASKED)
            slot = 2 * (pair % 2) + side
            s_ref[slot, :, pl.ds(column, size)] = raw
            top = raw[:, :128]
            for piece in range(1, size // 128):
                top = jnp.maximum(top, raw[:, piece * 128 : (piece + 1) * 128])
            if not first:
                top = jnp.maximum(top, mx[slot])
            mx[slot] = top

    def settle(pair):
        for side in (0, 1):
            slot = 2 * (pair % 2) + side
            top = jnp.max(mx[slot], axis=1, keepdims=True)
            mx[slot] = jnp.broadcast_to(top, (TQ, 128))

    def blend(pair, row, size, column, first):
        vals = kv[pl.ds(row, size), HALF + pair * 128 : HALF + (pair + 1) * 128]
        wide = jnp.concatenate([vals, jnp.ones((size, 128), BF)], axis=1)
        for side in (0, 1):
            slot = 2 * (pair % 2) + side
            top = jnp.concatenate([mx[slot]] * (size // 128), axis=1)
            power = jnp.exp2(s_ref[slot, :, pl.ds(column, size)] - top).astype(BF)
            new = dot_nn(power, wide)
            if first:
                acc[side] = new
            else:
                acc[side] += new

    def sweep(step):
        step(diag, TQ, 0, True)

        def some(index, carry):
            row = pl.multiple_of(extra_row + index * TQ, TQ)
            step(row, TQ, pl.multiple_of(TQ + index * TQ, TQ), False)
            return carry

        lax.fori_loop(0, extra, some, 0)

        def one(index, carry):
            row = pl.multiple_of(base + index * TK, TQ)
            step(row, TK, pl.multiple_of(TK + index * TK, TQ), False)
            return carry

        lax.fori_loop(0, tiles, one, 0)

    sweep(lambda row, size, column, first: score(0, row, size, column, first, first))
    for pair in range(PAIRS):
        settle(pair)

        def both(row, size, column, first):
            if pair + 1 < PAIRS:
                score(pair + 1, row, size, column, first, first)
            blend(pair, row, size, column, first)

        sweep(both)
        sides = []
        for side in (0, 1):
            total = acc[side][:, 128:]
            sides.append(acc[side][:, :128] / total)
            tall = jnp.transpose(mx[2 * (pair % 2) + side] + jnp.log2(total))
            lse_ref[0, 2 * pair + side] = tall[0]
        o_ref[:, pair * 128 : (pair + 1) * 128] = jnp.where(low, sides[0], sides[1]).astype(BF)

    @pl.when(block == pl.num_programs(0) - 1)
    def _():
        size = rows.shape[1]
        part = min(size, xc_hbm.shape[0] // 2)
        for row in range(0, xp_hbm.shape[0], size):
            pltpu.make_async_copy(
                kv.at[pl.ds(row, size)], kv_hbm.at[pl.ds(row, size)], done.at[row // size]
            ).wait()
        for row in range(xp_hbm.shape[0], kv.shape[0], part):
            store(row, part).wait()


def query_specs(TQ):
    prompts = pl.BlockSpec((TQ, D), lambda i, s, t: (t[i, 1], 0))
    conts = pl.BlockSpec((TQ, D), lambda i, s, t: (t[i, 2], 0))
    return prompts, conts


def attend_forward(info, spot, xp, xc, weight, vec, TQ, size):
    blocks = info.shape[0]
    count = blocks * TQ
    keys = xp.shape[0] + xc.shape[0]
    tiles = xp.shape[0] // size + xc.shape[0] // min(size, xc.shape[0] // 2)
    whole = pl.BlockSpec(memory_space=pl.ANY)
    heads = pl.BlockSpec((TQ, HALF), lambda i, s, t: (i, 0))
    shape = jax.ShapeDtypeStruct
    return pl.pallas_call(
        attend_forward_kernel,
        grid_spec=pltpu.PrefetchScalarGridSpec(
            num_scalar_prefetch=2,
            grid=(blocks,),
            in_specs=[
                whole,
                whole,
                *query_specs(TQ),
                pl.BlockSpec(weight.shape, lambda i, s, t: (0, 0)),
                pl.BlockSpec(vec.shape, lambda i, s, t: (0, 0)),
            ],
            out_specs=[heads, pl.BlockSpec((1, 8, TQ), lambda i, s, t: (i, 0, 0)), heads, whole],
            scratch_shapes=[
                pltpu.VMEM((keys, D), BF),
                pltpu.VMEM((2, size, D), BF),
                pltpu.VMEM((NH, TQ, 128), BF),
                pltpu.VMEM((4, TQ, PLEN + TK), F32),
                pltpu.VMEM((4, TQ, 128), F32),
                pltpu.VMEM((2, TQ, 256), F32),
                pltpu.SemaphoreType.DMA((2,)),
                pltpu.SemaphoreType.DMA((tiles,)),
            ],
        ),
        out_shape=(
            shape((count, HALF), BF),
            shape((blocks, 8, TQ), F32),
            shape((count, HALF), BF),
            shape((keys, D), BF),
        ),
        compiler_params=pltpu.CompilerParams(
            dimension_semantics=("arbitrary",), vmem_limit_bytes=56 << 20
        ),
        cost_estimate=pl.CostEstimate(
            flops=int(4 * count * PLEN * HALF * 4) + 2 * D * D * keys,
            bytes_accessed=20 << 20,
            transcendentals=0,
        ),
        name="attend_forward",
    )(info, spot, xp, xc, xp, xc, weight, vec)


def attend_backward_kernel(
    chained,
    info,
    spot,
    xp_hbm,
    xc_hbm,
    kv_hbm,
    xqp_ref,
    xqc_ref,
    q_ref,
    do_ref,
    o_ref,
    lse_ref,
    w_ref,
    vec_ref,
    *refs,
):
    if chained:
        old_w, old_vec, old_bias = refs[:3]
        refs = refs[3:]
    (
        tp_hbm,
        tc_hbm,
        gw_hbm,
        gvec_ref,
        gbias_ref,
        kv,
        kt,
        dkv,
        gw,
        qd,
        rows,
        table,
        qm,
        dom,
        dqt,
        drow,
        sems,
        done,
    ) = refs
    block = pl.program_id(0)
    TQ = q_ref.shape[0]
    keys_all = kv.shape[0]
    gain, shift = (vec_ref[i : i + 1, :] for i in range(2))

    @pl.when(block == 0)
    def _():
        load = pltpu.make_async_copy(kv_hbm, kv, sems.at[0])
        load.start()
        if chained:
            more = pltpu.make_async_copy(old_w, gw, sems.at[1])
            more.start()
            gvec_ref[...] = old_vec[...]
            gbias_ref[...] = old_bias[...]
        else:
            gw[...] = jnp.zeros_like(gw)
            gvec_ref[...] = jnp.zeros_like(gvec_ref)
            gbias_ref[...] = jnp.zeros_like(gbias_ref)

        def clear(index, carry):
            dkv[pl.ds(pl.multiple_of(index * TQ, TQ), TQ), :] = jnp.zeros((TQ, D), F32)
            return carry

        lax.fori_loop(0, keys_all // TQ, clear, 0)
        load.wait()

        def prepare(index, carry):
            row = pl.multiple_of(index * TQ, TQ)
            kt[:, pl.ds(row, TQ)] = flip(kv[pl.ds(row, TQ), :HALF])
            return carry

        lax.fori_loop(0, keys_all // TQ, prepare, 0)
        if chained:
            more.wait()

    base = pl.multiple_of(info[block, 0], TQ)
    tiles = info[block, 1]
    extra = info[block, 2]
    extra_row = pl.multiple_of(info[block, 3], TQ)
    diag = pl.multiple_of(info[block, 4], TQ)
    low, high = half_masks(TQ)
    zero = jnp.zeros((TQ, 128), BF)
    for pair in range(PAIRS):
        lanes = slice(pair * 128, (pair + 1) * 128)
        part = q_ref[:, lanes]
        qm[2 * pair] = jnp.where(low, part, zero)
        qm[2 * pair + 1] = jnp.where(high, part, zero)
        part = do_ref[:, lanes]
        dom[2 * pair] = jnp.where(low, part, zero)
        dom[2 * pair + 1] = jnp.where(high, part, zero)
        product = jnp.transpose(part.astype(F32) * o_ref[:, lanes].astype(F32))
        drow[2 * pair] = jnp.sum(product[:HEAD_DIM], axis=0)
        drow[2 * pair + 1] = jnp.sum(product[HEAD_DIM:], axis=0)

    def step(row, size, first):
        for pair in range(PAIRS):
            lanes = slice(pair * 128, (pair + 1) * 128)
            more = slice(HALF + pair * 128, HALF + (pair + 1) * 128)
            keys = kv[pl.ds(row, size), lanes]
            vals = kv[pl.ds(row, size), more]
            dk = None
            dv = None
            for side in (0, 1):
                head = 2 * pair + side
                raw = dot_nt(keys, qm[head])
                if first:
                    across = lax.broadcasted_iota(jnp.int32, (size, TQ), 1)
                    down = lax.broadcasted_iota(jnp.int32, (size, TQ), 0)
                    raw = jnp.where(down <= across, raw, MASKED)
                probs = jnp.exp2(raw - lse_ref[0, head : head + 1, :])
                grad = dot_nt(vals, dom[head])
                slope = (probs * (grad - drow[head : head + 1, :])).astype(BF)
                probs = probs.astype(BF)
                part_v = dot_nn(probs, dom[head])
                part_k = dot_nn(slope, qm[head])
                dv = part_v if dv is None else dv + part_v
                dk = part_k if dk is None else dk + part_k
                spot = slice(head * HEAD_DIM, (head + 1) * HEAD_DIM)
                new = dot_nn(kt[spot, pl.ds(row, size)], slope)
                if first:
                    dqt[spot, :] = new
                else:
                    dqt[spot, :] += new
            dkv[pl.ds(row, size), lanes] += dk
            dkv[pl.ds(row, size), more] += dv

    step(diag, TQ, True)

    def some(index, carry):
        step(pl.multiple_of(extra_row + index * TQ, TQ), TQ, False)
        return carry

    lax.fori_loop(0, extra, some, 0)

    def one(index, carry):
        step(pl.multiple_of(base + index * TK, TQ), TK, False)
        return carry

    lax.fori_loop(0, tiles, one, 0)
    x = jnp.where(spot[block, 0] > 0, xqc_ref[...].astype(F32), xqp_ref[...].astype(F32))
    dq_full = jnp.transpose(dqt[...]) * HEAD_DIM ** (-0.5)
    dq = dq_full.astype(BF)
    gw[:, :HALF] += dot_nn(flip(normal_form(x) * gain + shift), dq)
    gbias_ref[0:1, :HALF] += jnp.sum(dq_full, axis=0, keepdims=True)
    qd[pl.ds(pl.multiple_of(block * TQ, TQ), TQ), :] = dot_nt(dq, w_ref[:, :HALF])

    @pl.when(block == pl.num_programs(0) - 1)
    def _():
        prompt_rows = xp_hbm.shape[0]
        size = rows.shape[1]
        crow = xc_hbm.shape[0] // 2
        part = min(size, crow)
        count = prompt_rows // size
        own, mate = spot[0, 3], spot[0, 4]

        def send(slot, row):
            return pltpu.make_async_copy(
                table.at[slot], tp_hbm.at[pl.ds(row, size)], done.at[slot]
            )

        def visit(row, size_now, x):
            hat = normal_form(x)
            grad_k = dkv[pl.ds(row, size_now), :HALF] * (1.0 / LOG2E)
            grad_v = dkv[pl.ds(row, size_now), HALF:]
            grad = jnp.concatenate([grad_k.astype(BF), grad_v.astype(BF)], axis=1)
            gw[:, HALF:] += dot_nn(flip(hat * gain + shift), grad)
            gbias_ref[0:1, HALF : 2 * HALF] += jnp.sum(grad_k, axis=0, keepdims=True)
            gbias_ref[0:1, 2 * HALF :] += jnp.sum(grad_v, axis=0, keepdims=True)
            change = dot_nt(grad, w_ref[:, HALF:])
            if isinstance(row, int):
                first = row - prompt_rows
                which = first // crow
                begin = which * (size + crow) + size + first - which * crow
                change = change + qd[begin : begin + size_now, :]
            else:
                index = row // size
                begin = jnp.where(index == mate, size + crow, 0)
                begin = pl.multiple_of(begin, math.gcd(size, crow))
                weight = jnp.where((index == own) | (index == mate), 1.0, 0.0)
                change = change + weight * qd[pl.ds(begin, size_now), :]
            gvec_ref[0:1, :] += jnp.sum(change * hat, axis=0, keepdims=True)
            gvec_ref[1:2, :] += jnp.sum(change, axis=0, keepdims=True)
            change = change.astype(BF)
            if isinstance(row, int):
                slot = (first // part) % 2
                if first // part >= 2:
                    pltpu.make_async_copy(
                        table.at[slot, pl.ds(0, part)],
                        tc_hbm.at[pl.ds(first - 2 * part, part)],
                        done.at[slot],
                    ).wait()
                else:
                    send(slot, prompt_rows - (2 - slot) * size).wait()
                table[slot, :part] = change
                pltpu.make_async_copy(
                    table.at[slot, pl.ds(0, part)],
                    tc_hbm.at[pl.ds(first, part)],
                    done.at[slot],
                ).start()
            else:
                slot = lax.rem(index, 2)

                @pl.when(index >= 2)
                def _():
                    send(slot, pl.multiple_of(row - 2 * size, size)).wait()

                table[slot] = change
                send(slot, row).start()

        stream_rows(xp_hbm, xc_hbm, rows, sems, visit)
        last = 2 * crow // part
        for index in range(last - 2, last):
            pltpu.make_async_copy(
                table.at[index % 2, pl.ds(0, part)],
                tc_hbm.at[pl.ds(index * part, part)],
                done.at[index % 2],
            ).wait()
        out = pltpu.make_async_copy(gw, gw_hbm, sems.at[0])
        out.start()
        out.wait()


def attend_backward(info, spot, xp, xc, kv, q, do, o, lse, weight, vec, totals, TQ, size):
    blocks = info.shape[0]
    count = blocks * TQ
    keys = kv.shape[0]
    whole = pl.BlockSpec(memory_space=pl.ANY)
    heads = pl.BlockSpec((TQ, HALF), lambda i, s, t: (i, 0))
    shape = jax.ShapeDtypeStruct
    fixed = [
        pl.BlockSpec((8, D), lambda i, s, t: (0, 0)),
        pl.BlockSpec((8, 3 * HALF), lambda i, s, t: (0, 0)),
    ]
    extra = () if totals is None else tuple(totals)
    return pl.pallas_call(
        functools.partial(attend_backward_kernel, totals is not None),
        grid_spec=pltpu.PrefetchScalarGridSpec(
            num_scalar_prefetch=2,
            grid=(blocks,),
            in_specs=[
                whole,
                whole,
                whole,
                *query_specs(TQ),
                heads,
                heads,
                heads,
                pl.BlockSpec((1, 8, TQ), lambda i, s, t: (i, 0, 0)),
                pl.BlockSpec(weight.shape, lambda i, s, t: (0, 0)),
                pl.BlockSpec(vec.shape, lambda i, s, t: (0, 0)),
            ]
            + ([whole] + fixed if extra else []),
            out_specs=[whole, whole, whole] + fixed,
            scratch_shapes=[
                pltpu.VMEM((keys, D), BF),
                pltpu.VMEM((HALF, keys), BF),
                pltpu.VMEM((keys, D), F32),
                pltpu.VMEM((D, 3 * HALF), F32),
                pltpu.VMEM((count, D), F32),
                pltpu.VMEM((2, size, D), BF),
                pltpu.VMEM((2, size, D), BF),
                pltpu.VMEM((NH, TQ, 128), BF),
                pltpu.VMEM((NH, TQ, 128), BF),
                pltpu.VMEM((HALF, TQ), F32),
                pltpu.VMEM((8, TQ), F32),
                pltpu.SemaphoreType.DMA((2,)),
                pltpu.SemaphoreType.DMA((2,)),
            ],
        ),
        out_shape=(
            shape(xp.shape, BF),
            shape(xc.shape, BF),
            shape((D, 3 * HALF), F32),
            shape((8, D), F32),
            shape((8, 3 * HALF), F32),
        ),
        compiler_params=pltpu.CompilerParams(
            dimension_semantics=("arbitrary",), vmem_limit_bytes=62 << 20
        ),
        cost_estimate=pl.CostEstimate(
            flops=int(10 * count * PLEN * HALF * 4) + 4 * D * D * keys,
            bytes_accessed=30 << 20,
            transcendentals=0,
        ),
        name="attend_backward",
    )(info, spot, xp, xc, kv, xp, xc, q, do, o, lse, weight, vec, *extra)


def gelu_parts(value):
    rate = math.sqrt(2.0 / math.pi)
    square = value * value
    half = 0.5 + 0.5 * jnp.tanh(value * (rate + (rate * 0.044715) * square))
    slope = half + value * (half * (1.0 - half)) * (2.0 * rate + (6.0 * rate * 0.044715) * square)
    return value * half, slope


def feed_forward_kernel(
    prompt_parts,
    clen,
    count,
    groups,
    lens,
    places,
    xp_ref,
    xc_ref,
    gp_ref,
    gc_ref,
    mine_ref,
    mate_ref,
    vec_ref,
    bfc_ref,
    *refs,
):
    pieces = refs[:count]
    (
        fp_ref,
        fc_ref,
        hp_ref,
        hc_ref,
        dmine_ref,
        dmate_ref,
        gvec_ref,
        gbfc_ref,
        grads_hbm,
        more_hbm,
        wp,
        wfc,
        wout,
        ap,
        afc,
        aout,
        stage,
        sems,
    ) = refs[count:]
    core = places[0]
    batch = pl.program_id(0)
    part = pl.program_id(1)
    tile = mine_ref.shape[1]
    is_cont = part >= prompt_parts
    begin = (batch == 0) & (part == 0)

    @pl.when(begin)
    def _():
        def loads_of(first_half):
            moves = []
            for index, piece in enumerate(pieces):
                size = piece.shape[1]
                half = None
                if first_half is not None:
                    half = first_half if index < count // 2 else 1 - first_half
                split = (D + 2 * FF) // 2 - D
                spans = [(wp, 0, 0, D), (wfc, 0, D, FF)]
                spans += [(wout, block * D, D + FF + block * D, D) for block in range(FF // D)]
                if half == 0:
                    spans = [(wp, 0, 0, D), (wfc, (0, 0), D, split)]
                elif half == 1:
                    spans = [(wfc, (0, split), 0, FF - split)]
                    spans += [
                        (wout, block * D, FF - split + block * D, D) for block in range(FF // D)
                    ]
                for inner in range(piece.shape[0]):
                    row = pl.multiple_of(places[1 + index * piece.shape[0] + inner], 16)
                    turned = pl.multiple_of(lax.rem(row + core * HALF, D), 16)
                    for target, offset, column, width in spans:
                        source = piece.at[inner, :, pl.ds(column, width)]
                        if target is wp:
                            view = wp.at[pl.ds(turned, size), :]
                        elif target is wfc:
                            begin = offset[1] if isinstance(offset, tuple) else 0
                            view = wfc.at[pl.ds(row, size), pl.ds(begin, width)]
                        else:
                            view = wout.at[pl.ds(offset + row, size), :]
                        moves.append((source, view))
            return [
                pltpu.make_async_copy(source, view, sems.at[index])
                for index, (source, view) in enumerate(moves)
            ]

        def load_all(first_half):
            loads = loads_of(first_half)
            for load in loads:
                load.start()
            for load in loads:
                load.wait()

        ap[...] = jnp.zeros_like(ap)
        gvec_ref[...] = jnp.zeros_like(gvec_ref)
        gbfc_ref[...] = jnp.zeros_like(gbfc_ref)

        def clear(index, carry):
            row = pl.multiple_of(index * 64, 64)
            afc[pl.ds(row, 64), :] = jnp.zeros((64, FF), F32)
            aout[pl.ds(row, 64), :] = jnp.zeros((64, FF), F32)
            return carry

        lax.fori_loop(0, D // 64, clear, 0)
        if groups == 1:
            load_all(None)
        else:

            @pl.when(core == 0)
            def _():
                load_all(0)

            @pl.when(core != 0)
            def _():
                load_all(1)

    b_proj = vec_ref[0:1, :]
    gain = vec_ref[1:2, :]
    shift = vec_ref[2:3, :]
    b_out = vec_ref[3:4, :]
    x = jnp.where(is_cont, xc_ref[0].astype(F32), xp_ref[0].astype(F32))
    gy = jnp.where(is_cont, gc_ref[0].astype(F32), gp_ref[0].astype(F32))
    start = jnp.maximum(part - prompt_parts, 0) * tile
    length = lens[batch, start // clen]
    place = lax.broadcasted_iota(jnp.int32, (tile, 1), 0) + start % clen
    valid = jnp.where(jnp.logical_not(is_cont) | (place < length), 1.0, 0.0)

    mine = mine_ref[0]
    mate = mate_ref[0]
    h = x + valid * (dot_nn(mine, wp[:HALF, :]) + dot_nn(mate, wp[HALF:, :]) + b_proj)
    center = h - jnp.mean(h, axis=1, keepdims=True)
    rate = lax.rsqrt(jnp.mean(center * center, axis=1, keepdims=True) + EPSILON)
    hat = center * rate
    second = (hat * gain + shift).astype(BF)
    dz_full = valid * gy
    dz = dz_full.astype(BF)
    second_t = flip(second)
    dz_t = flip(dz)
    result = None
    back = None
    for index in range(FF // D):
        cols = slice(index * D, (index + 1) * D)
        inner = dot_nn(second, wfc[:, cols]) + bfc_ref[:, cols]
        act, slope = gelu_parts(inner)
        act = act.astype(BF)
        du_full = dot_nt(dz, wout[cols, :]) * slope
        du = du_full.astype(BF)
        gbfc_ref[0:1, cols] += jnp.sum(du_full, axis=0, keepdims=True)
        new = dot_nn(act, wout[cols, :])
        result = new if result is None else result + new
        new = dot_nt(du, wfc[:, cols])
        back = new if back is None else back + new
        aout[:, cols] += dot_nn(dz_t, act)
        afc[:, cols] += dot_nn(second_t, du)
    final = (h + valid * (result + b_out)).astype(BF)
    e2 = back * gain
    dh = gy + rate * (
        e2
        - jnp.mean(e2, axis=1, keepdims=True)
        - hat * jnp.mean(e2 * hat, axis=1, keepdims=True)
    )
    dy_full = valid * dh
    dy = dy_full.astype(BF)
    gvec_ref[0:1, :] += jnp.sum(dy_full, axis=0, keepdims=True)
    gvec_ref[1:2, :] += jnp.sum(back * hat, axis=0, keepdims=True)
    gvec_ref[2:3, :] += jnp.sum(back, axis=0, keepdims=True)
    gvec_ref[3:4, :] += jnp.sum(dz.astype(F32), axis=0, keepdims=True)
    ap[:HALF, :] += dot_nn(flip(mine), dy)
    ap[HALF:, :] += dot_nn(flip(mate), dy)
    dmine_ref[0] = dot_nt(dy, wp[:HALF, :]).astype(BF)
    dmate_ref[0] = dot_nt(dy, wp[HALF:, :]).astype(BF)
    dh = dh.astype(BF)

    @pl.when(jnp.logical_not(is_cont))
    def _():
        fp_ref[0] = final
        hp_ref[0] = dh

    @pl.when(is_cont)
    def _():
        fc_ref[0] = final
        hc_ref[0] = dh

    @pl.when((batch == pl.num_programs(0) - 1) & (part == pl.num_programs(1) - 1))
    def _():
        blocks, share = stage.shape[1], stage.shape[2]
        sends = []

        def send(column, fetch):
            slot = len(sends) % 2
            if len(sends) >= 2:
                sends[-2].wait()
            for block in range(blocks):
                stage[slot, block] = fetch(block).astype(BF)
            width = grads_hbm.shape[2]
            if column < width:
                target = grads_hbm.at[:, :, pl.ds(column, D)]
            else:
                target = more_hbm.at[:, :, pl.ds(column - width, D)]
            sends.append(pltpu.make_async_copy(stage.at[slot], target, sems.at[slot]))
            sends[-1].start()

        def first_row(block):
            return (block % groups * (blocks // groups) + block // groups) * share

        def proj_rows(block):
            row = lax.rem(first_row(block) + core * HALF, D)
            return ap[pl.ds(pl.multiple_of(row, math.gcd(share, HALF)), share), :]

        send(0, proj_rows)
        for part_of in range(FF // D):
            cols = slice(part_of * D, (part_of + 1) * D)
            send(D + part_of * D, lambda block: afc[first_row(block) : first_row(block) + share, cols])
        for part_of in range(FF // D):
            cols = slice(part_of * D, (part_of + 1) * D)
            ap[...] = jnp.transpose(aout[:, cols])
            send(
                D + FF + part_of * D,
                lambda block: ap[first_row(block) : first_row(block) + share, :],
            )
        for copy in sends[-2:]:
            copy.wait()


def feed_forward(lens, places, prompt_in, cont_in, prompt_cot, cont_cot, mine, mate, vec, bfc, pieces, groups, share):
    prow = prompt_in.shape[1]
    crow = cont_in.shape[1]
    clen = crow // lens.shape[1]
    tile = min(256, prow, clen)
    prompt_parts = prow // tile
    parts = prompt_parts + crow // tile
    prompts = pl.BlockSpec((1, tile, D), lambda m, i, s, t: (m, jnp.minimum(i, prompt_parts - 1), 0))
    conts = pl.BlockSpec((1, tile, D), lambda m, i, s, t: (m, jnp.maximum(i - prompt_parts, 0), 0))
    heads = pl.BlockSpec((1, tile, HALF), lambda m, i, s, t: (m, i, 0))
    whole = pl.BlockSpec(memory_space=pl.ANY)
    fixed = pl.BlockSpec((8, D), lambda m, i, s, t: (0, 0))
    long = pl.BlockSpec((8, FF), lambda m, i, s, t: (0, 0))
    shape = jax.ShapeDtypeStruct
    rows = MB * (prow + crow)
    return pl.pallas_call(
        functools.partial(feed_forward_kernel, prompt_parts, clen, len(pieces), groups),
        grid_spec=pltpu.PrefetchScalarGridSpec(
            num_scalar_prefetch=2,
            grid=(MB, parts),
            in_specs=[
                prompts,
                conts,
                prompts,
                conts,
                heads,
                heads,
                fixed,
                pl.BlockSpec((1, FF), lambda m, i, s, t: (0, 0)),
            ]
            + [whole] * len(pieces),
            out_specs=[prompts, conts, prompts, conts, heads, heads, fixed, long, whole, whole],
            scratch_shapes=[
                pltpu.VMEM((D, D), BF),
                pltpu.VMEM((D, FF), BF),
                pltpu.VMEM((FF, D), BF),
                pltpu.VMEM((D, D), F32),
                pltpu.VMEM((D, FF), F32),
                pltpu.VMEM((D, FF), F32),
                pltpu.VMEM((2, D // share, share, D), BF),
                pltpu.SemaphoreType.DMA(
                    (max(16, (2 + FF // D) * sum(piece.shape[0] for piece in pieces)),)
                ),
            ],
        ),
        out_shape=(
            shape(prompt_in.shape, BF),
            shape(cont_in.shape, BF),
            shape(prompt_in.shape, BF),
            shape(cont_in.shape, BF),
            shape(mine.shape, BF),
            shape(mate.shape, BF),
            shape((8, D), F32),
            shape((8, FF), F32),
            shape((D // share, share, D + FF + FF // 2), BF),
            shape((D // share, share, FF // 2), BF),
        ),
        compiler_params=pltpu.CompilerParams(
            dimension_semantics=("arbitrary", "arbitrary"), vmem_limit_bytes=63 << 20
        ),
        cost_estimate=pl.CostEstimate(
            flops=6 * rows * (D * D + 2 * D * FF), bytes_accessed=50 << 20, transcendentals=0
        ),
        name="feed_forward",
    )(lens, places, prompt_in, cont_in, prompt_cot, cont_cot, mine, mate, vec, bfc, *pieces)


HEAD_COLS = 3 * HALF
SMALL_COLS = 128


def neighbour(value, axis, distance):
    pairs = [(i, i ^ distance) for i in range(lax.axis_size(axis))]
    return lax.ppermute(value, axis, pairs)


def swap(value):
    return neighbour(value, "fsdp", 1)


def is_square():
    return lax.axis_size("grp") == 4 and lax.axis_size("fsdp") == 8


def spread_one(block):
    half = block.shape[0] // 2
    pieces = [block[:half], block[half:]]
    return [
        jnp.stack([piece, neighbour(piece, "grp", distance)])
        for piece, distance in zip(pieces, (1, 2))
    ]


def spread_two(boths):
    return [neighbour(both, "grp", distance) for both, distance in zip(boths, (2, 1))]


def spread_pieces(boths, fars):
    return [
        (boths[0], (0, 1), 0),
        (fars[0], (2, 3), 0),
        (boths[1], (0, 2), 1),
        (fars[1], (1, 3), 1),
    ]


def gather_zone(packed):
    if not is_square():
        return lax.all_gather(packed, ALL, axis=0, tiled=True)
    groups = [list(range(c, lax.axis_size("fsdp"), 2)) for c in (0, 1)]
    return lax.all_gather(packed, "fsdp", axis=0, tiled=True, axis_index_groups=groups)


def chip_rows(keep, send, core):
    other = swap(send)
    return jnp.where(
        core == 0,
        jnp.concatenate([keep, other], axis=0),
        jnp.concatenate([other, keep], axis=0),
    )


def join_front(boths, fars):
    own = lax.axis_index("grp")
    parts = {}
    for pair, offsets, index in spread_pieces(boths, fars):
        for which, offset in enumerate(offsets):
            parts[offset, index] = pair[which]
    table = jnp.stack([jnp.concatenate([parts[k, 0], parts[k, 1]], axis=0) for k in range(4)])
    return jnp.concatenate(
        [lax.dynamic_index_in_dim(table, own ^ k, 0, keepdims=False) for k in range(4)], axis=0
    )


def join_rest(boths, fars):
    own = lax.axis_index("grp")
    size = boths[0].shape[1]
    pieces, rows = [], []
    for pair, offsets, index in spread_pieces(boths, fars):
        pieces.append(pair)
        for offset in offsets:
            rows.append((own ^ offset) * 2 * size + index * size)
    return pieces + [swap(piece) for piece in pieces], rows + rows


def pin(*values):
    return list(lax.optimization_barrier(tuple(values)))


def pick(array, index, axis):
    return lax.dynamic_index_in_dim(array, index, axis, keepdims=False)


def meet(array, index, axis, name, distance):
    other = neighbour(pick(array, 1 - index, axis), name, distance)
    return (pick(array, index, axis).astype(F32) + other.astype(F32)).astype(BF)


def reduce_steps():
    if not is_square():
        groups = [list(range(c, lax.axis_size("fsdp"), 2)) for c in (0, 1)]

        def along_grp(value):
            return lax.psum_scatter(value, "grp", scatter_dimension=0, tiled=True)

        def along_chips(value):
            return lax.psum_scatter(
                value, "fsdp", scatter_dimension=0, tiled=True, axis_index_groups=groups
            )

        return [along_grp, along_chips]

    own = lax.axis_index("grp")
    x, y = own % 2, own // 2
    z = lax.axis_index("fsdp") // 2

    def one(value):
        value = value.reshape(2, 2, 2, value.shape[0] // 8, value.shape[1])
        return meet(value[:, :, 0], x, 1, "grp", 1), meet(value[:, :, 1], y, 0, "grp", 2)

    def two(pair):
        value = jnp.concatenate(
            [meet(pair[0], y, 0, "grp", 2), meet(pair[1], x, 0, "grp", 1)], axis=0
        )
        return value.reshape(2, 2, value.shape[0] // 4, value.shape[1])

    def three(value):
        return meet(value, z % 2, 1, "fsdp", 2)

    def four(value):
        return meet(value, z // 2, 0, "fsdp", 4)

    return [one, two, three, four]


def reduce_parameters(value):
    for step in reduce_steps():
        value = step(value)
    return value


def own_rows(value, core):
    share = value.shape[0] // 2
    keep = lax.dynamic_slice_in_dim(value, core * share, share, 0)
    other = swap(lax.dynamic_slice_in_dim(value, (1 - core) * share, share, 0))
    return keep, other


def square_steps(core):
    own = lax.axis_index("grp")
    x, y = own % 2, own // 2

    def one(value):
        cols = value.shape[-1] // 2
        value = value.reshape((2, 2) + value.shape[1:])
        return (
            meet(value[..., :cols], x, 1, "grp", 1),
            meet(value[..., cols:], y, 0, "grp", 2),
        )

    def two(pair):
        return jnp.concatenate(
            [meet(pair[0], y, 0, "grp", 2), meet(pair[1], x, 0, "grp", 1)], axis=1
        )

    return [one, two]


def body(
    prompt_in,
    cont_in,
    prompt_cot,
    cont_cot,
    cont_prompt,
    cont_len,
    ln1_gain,
    ln1_bias,
    attn_weight,
    attn_bias,
    proj_weight,
    proj_bias,
    ln2_gain,
    ln2_bias,
    fc_weight,
    fc_bias,
    out_weight,
    out_bias,
):
    fsdp = lax.axis_size("fsdp")
    devices = fsdp * lax.axis_size("grp")
    prow = prompt_in.shape[1]
    crow = cont_in.shape[1]
    conts = cont_prompt.shape[2]
    clen = crow // conts
    mine = prow + crow
    TQ = min(256, prow, clen)
    prompt_rows = NPR * PLEN
    place = lax.axis_index("fsdp")
    core = place % 2
    share = D // devices
    wide = FF // D

    vectors = (ln1_gain, ln1_bias, attn_bias[0], attn_bias[1], proj_bias, ln2_gain, ln2_bias, out_bias)
    columns = jnp.concatenate(
        [v[:, None] for v in vectors] + [fc_bias.reshape(wide, share).T], axis=1
    )
    columns = jnp.pad(columns, ((0, 0), (0, SMALL_COLS - columns.shape[1])))
    prompt_all = [lax.all_gather(prompt_in[m], "fsdp", axis=0, tiled=True) for m in range(MB)]
    square = is_square()
    columns = columns.astype(BF)
    heads = attn_weight.astype(BF).reshape(share, 3, 2, HALF)
    keep = lax.dynamic_index_in_dim(heads, core, 2, keepdims=False).reshape(share, HEAD_COLS)
    send = lax.dynamic_index_in_dim(heads, 1 - core, 2, keepdims=False).reshape(share, HEAD_COLS)
    rest = jnp.concatenate(
        [
            proj_weight,
            fc_weight.reshape(share, devices, wide, share).transpose(0, 2, 1, 3).reshape(share, FF),
            out_weight.reshape(wide, share, D).transpose(1, 0, 2).reshape(share, FF),
        ],
        axis=1,
    ).astype(BF)
    if square:
        zone = gather_zone(
            chip_rows(
                jnp.concatenate([keep, columns], axis=1),
                jnp.concatenate([send, columns], axis=1),
                core,
            )
        )
        half = rest.shape[1] // 2
        rest = chip_rows(
            lax.dynamic_slice_in_dim(rest, core * half, half, 1),
            lax.dynamic_slice_in_dim(rest, (1 - core) * half, half, 1),
            core,
        )
        cut = half // 256 * 128
        first, zone = pin(rest[:, :cut], zone)
        zones = [gather_zone(first)]
        front_boths = spread_one(zone)
        zones[0], second, *front_boths = pin(zones[0], rest[:, cut:], *front_boths)
        zones.append(gather_zone(second))
        front_fars = spread_two(front_boths)
        zones[1], *front_fars = pin(zones[1], *front_fars)
        front = join_front(front_boths, front_fars)
        rest_boths = spread_one(jnp.concatenate(zones, axis=1))
    else:
        zone = gather_zone(jnp.concatenate([heads.reshape(share, 3 * D), columns], axis=1))
        front = jnp.concatenate(
            [
                lax.dynamic_index_in_dim(
                    zone[:, : 3 * D].reshape(D, 3, 2, HALF), core, 2, keepdims=False
                ).reshape(D, HEAD_COLS),
                zone[:, 3 * D :],
            ],
            axis=1,
        )
        pieces = [gather_zone(rest).reshape(2, HALF, -1)]
        piece_rows = [0, HALF]
    w_heads = front[:, :HEAD_COLS]
    small = front[:, HEAD_COLS:].astype(F32)
    gain_a, shift_a, bias_q, bias_v, b_proj, gain_b, shift_b, b_out = (small[:, i] for i in range(8))
    b_fc = small[:, 8 : 8 + wide].T.reshape(1, FF)
    bias_q = lax.dynamic_slice_in_dim(bias_q, core * HALF, HALF)
    bias_v = lax.dynamic_slice_in_dim(bias_v, core * HALF, HALF)
    none = jnp.zeros((HALF,), F32)
    vec_a = jnp.stack(
        [gain_a, shift_a, jnp.concatenate([none, bias_v]), jnp.concatenate([bias_q, none])]
        + [jnp.zeros((D,), F32)] * 4
    )
    vec_b = jnp.pad(jnp.stack([b_proj, gain_b, shift_b, b_out]), ((0, 4), (0, 0)))

    cont_mate = swap(cont_in)
    plan_mate = swap(cont_prompt[:, 0, :].astype(F32)).astype(jnp.int32)

    def balanced(index):
        ends = fsdp // NPR
        other = index // ends * ends + ends - 1 - (index % ends - index % 2)
        return index + (index % 2) * (other - index)

    own_place = balanced(place)
    mate_place = balanced(place + 1 - 2 * core)
    own_row = own_place * prow
    mate_row = mate_place * prow
    own_pairs = [(i, balanced(i)) for i in range(fsdp)]
    mate_pairs = [(i, balanced(i ^ 1)) for i in range(fsdp)]

    def send_home(own, other):
        return (
            jnp.concatenate([lax.ppermute(own[:prow], "fsdp", own_pairs), own[prow:]], axis=0),
            jnp.concatenate(
                [lax.ppermute(other[:prow], "fsdp", mate_pairs), swap(other[prow:])], axis=0
            ),
        )

    def send_back(own, other):
        return [
            lax.ppermute(own[:prow], "fsdp", [(b, a) for a, b in own_pairs]),
            own[prow:],
            lax.ppermute(other[:prow], "fsdp", [(b, a) for a, b in mate_pairs]),
            swap(other[prow:]),
        ]

    def prompt_plan(row):
        row = row + TQ * jnp.arange(prow // TQ)
        spot = row % PLEN
        return jnp.stack(
            [
                row - spot,
                spot // TK,
                spot % TK // TQ,
                row - spot + spot // TK * TK,
                row,
            ],
            axis=1,
        )

    def cont_plan(follows, first):
        blocks = clen // TQ
        follows = jnp.repeat(follows, blocks)
        index = jnp.arange(conts * blocks)
        begin = prompt_rows + first + index // blocks * clen
        return jnp.stack(
            [
                follows * PLEN,
                jnp.full(index.shape, PLEN // TK),
                index % blocks,
                begin,
                begin + index % blocks * TQ,
            ],
            axis=1,
        )

    def plan_of(m):
        return jnp.concatenate(
            [
                prompt_plan(own_row),
                cont_plan(cont_prompt[m, 0], 0),
                prompt_plan(mate_row),
                cont_plan(plan_mate[m], crow),
            ],
            axis=0,
        ).astype(jnp.int32)

    blocks = []
    for kind, count in (("own", prow), ("cont", crow), ("mate", prow), ("other", crow)):
        for index in range(count // TQ):
            prompt = (mate_row if kind in ("mate", "other") else own_row) // TQ
            last = prow // TQ - 1
            if kind in ("own", "mate"):
                blocks.append((0, prompt + index, 0 if kind == "own" else crow // TQ - 1))
            else:
                first = 0 if kind == "cont" else crow // TQ
                blocks.append((1, prompt + last, first + index))
    spot = jnp.stack(
        [
            jnp.stack([jnp.asarray(value, jnp.int32) for value in entry + (own_place, mate_place)])
            for entry in blocks
        ]
    ).astype(jnp.int32)

    saved = []
    outs_mine = []
    outs_mate = []
    for m in range(MB):
        x_prompt = prompt_all[m]
        if m > 0:
            x_prompt, saved[-1][-1] = pin(x_prompt, saved[-1][-1])
        if square and m == 1:
            x_prompt, *rest_boths = pin(x_prompt, *rest_boths)
            rest_fars = spread_two(rest_boths)
        x_cont = jnp.concatenate([cont_in[m], cont_mate[m]], axis=0)
        plan = plan_of(m)
        o, lse, query, kv = attend_forward(plan, spot, x_prompt, x_cont, w_heads, vec_a, TQ, prow)
        if square and m == 1:
            lse, *rest_fars = pin(lse, *rest_fars)
        own, other = send_home(o[:mine], o[mine:])
        outs_mine.append(own)
        outs_mate.append(other)
        saved.append([x_prompt, x_cont, kv, query, plan, o, lse])

    if square:
        pieces, piece_rows = join_rest(rest_boths, rest_fars)

    groups, block_share = (4, share) if square else (1, 8)
    places = jnp.stack([core] + [jnp.asarray(row, jnp.int32) for row in piece_rows]).astype(jnp.int32)
    (
        prompt_out,
        cont_out,
        prompt_dh,
        cont_dh,
        d_mine,
        d_mate,
        g_vec,
        g_fc_bias,
        g_rest,
        g_more,
    ) = feed_forward(
        cont_len[:, 0, :],
        places,
        prompt_in,
        cont_in,
        prompt_cot,
        cont_cot,
        jnp.stack(outs_mine),
        jnp.stack(outs_mate),
        vec_b,
        b_fc,
        pieces,
        groups,
        block_share,
    )
    returned = [send_back(d_mine[m], d_mate[m]) for m in range(MB)]
    g_rest, g_more, *returned[0] = pin(g_rest, g_more, *returned[0])

    def along_fsdp(value):
        if square:
            return lax.psum_scatter(value, "fsdp", scatter_dimension=0, tiled=True)
        value = value.reshape(D, value.shape[2])
        return lax.psum_scatter(value, ALL, scatter_dimension=0, tiled=True)

    g_rest, g_more = along_fsdp(g_rest), along_fsdp(g_more)

    totals = None
    tables = []
    conts_back = []
    for m in range(MB):
        x_prompt, x_cont, kv, query, plan, o, lse = saved[m]
        if m > 0:
            tables[-1], *returned[m] = pin(tables[-1], *returned[m])
            tables[-1] = lax.psum_scatter(tables[-1], "fsdp", scatter_dimension=0, tiled=True)
        if m > 1:
            g_more, *returned[m] = pin(g_more, *returned[m])
        if m == 1:
            g_rest, *returned[m] = pin(g_rest, *returned[m])
        do = jnp.concatenate(returned[m], axis=0)
        table, table_cont, *totals = attend_backward(
            plan, spot, x_prompt, x_cont, kv, query, do, o, lse, w_heads, vec_a, totals, TQ, prow
        )
        tables.append(table)
        conts_back.append(
            table_cont[:crow].astype(F32) + swap(table_cont[crow:]).astype(F32)
        )
    if MB > 1:
        *tables, conts_back[-1] = pin(*tables, conts_back[-1])
    tables[-1] = lax.psum_scatter(tables[-1], "fsdp", scatter_dimension=0, tiled=True)
    early = jnp.concatenate([g_rest, g_more], axis=-1)
    for step in square_steps(core) if square else ():
        early = step(early)
    *totals, conts_back[-1] = pin(*totals, conts_back[-1])
    g_heads, g_first, g_bias = totals

    def spread(value):
        return jnp.where((jnp.arange(2) == core)[:, None], value[None, :], 0.0).reshape(D)

    sums = jnp.stack(
        [
            g_first[0],
            g_first[1],
            spread(g_bias[0, :HALF]),
            spread(g_bias[0, 2 * HALF :]),
            g_vec[0],
            g_vec[1],
            g_vec[2],
            g_vec[3],
        ]
        + [g_fc_bias[0, i * D : (i + 1) * D] for i in range(wide)],
        axis=0,
    )
    sums_high = sums.astype(BF)
    sums_low = (sums - sums_high.astype(F32)).astype(BF)
    count = sums.shape[0]
    sums = jnp.concatenate(
        [sums_high, sums_low, jnp.zeros((SMALL_COLS - 2 * count, D), BF)], axis=0
    ).T
    late = reduce_parameters(jnp.concatenate([g_heads.astype(BF), sums], axis=1))
    late_own, late_other = own_rows(late, core)
    sums = late_own[:, HEAD_COLS:].astype(F32) + late_other[:, HEAD_COLS:].astype(F32)
    sums = (sums[:, :count] + sums[:, count : 2 * count]).T

    def by_core(own, other):
        return jnp.where(core == 0, own, other), jnp.where(core == 0, other, own)

    late = jnp.stack(by_core(late_own[:, :HEAD_COLS], late_other[:, :HEAD_COLS]), axis=1)
    late = late.reshape(share, 2, 3, HALF).transpose(0, 2, 1, 3).reshape(share, 3 * D)
    early = early.astype(F32)
    g_fc = early[:, D : D + FF].reshape(share, wide, devices, share)
    g_fc = g_fc.transpose(0, 2, 1, 3).reshape(share, FF)
    g_out = early[:, D + FF :].reshape(share, wide, D).transpose(1, 0, 2).reshape(share * wide, D)

    def input_grad(source, slope, change):
        source = source.astype(F32)
        center = source - jnp.mean(source, axis=-1, keepdims=True)
        rate = lax.rsqrt(jnp.mean(center * center, axis=-1, keepdims=True) + EPSILON)
        hat = center * rate
        e1 = change * gain_a
        change = e1 - jnp.mean(e1, axis=-1, keepdims=True)
        change = change - hat * jnp.mean(e1 * hat, axis=-1, keepdims=True)
        return (slope.astype(F32) + rate * change).astype(BF)

    prompt_grad = jnp.stack(
        [input_grad(prompt_in[m], prompt_dh[m], tables[m].astype(F32)) for m in range(MB)]
    )
    cont_grad = jnp.stack([input_grad(cont_in[m], cont_dh[m], conts_back[m]) for m in range(MB)])
    return (
        prompt_out,
        cont_out,
        prompt_grad,
        cont_grad,
        sums[0],
        sums[1],
        late.astype(F32),
        sums[2:4],
        early[:, :D],
        sums[4],
        sums[5],
        sums[6],
        g_fc,
        sums[8:].reshape(share * wide),
        g_out,
        sums[7],
    )


def solution(mesh):
    rows = P(None, ALL, None)
    conts = P(None, "grp", "fsdp")
    vector = P(ALL)
    matrix = P(ALL, None)
    pair = P(None, ALL)
    params = (
        vector,
        vector,
        matrix,
        pair,
        matrix,
        vector,
        vector,
        vector,
        matrix,
        vector,
        matrix,
        vector,
    )
    return jax.shard_map(
        body,
        mesh=mesh,
        in_specs=(rows, rows, rows, rows, conts, conts) + params,
        out_specs=(rows, rows, rows, rows) + params,
        check_vma=False,
    )
```

```python
import functools
import math

import jax
import jax.numpy as jnp
from jax import lax
from jax.experimental import pallas as pl
from jax.experimental.pallas import tpu as pltpu
from jax.sharding import PartitionSpec as P

D = 768
HEADS = 12
HEAD_DIM = 64
FF = 3072
MB = 3
NPR = 2
PLEN = 2048
ALL = ("grp", "fsdp")

EPSILON = 1e-05
MASKED = -1e30
BF = jnp.bfloat16
F32 = jnp.float32

HALF = D // 2
NH = HEADS // 2
PAIRS = NH // 2
TK = 512
LOG2E = math.log2(math.e)
QSCALE = HEAD_DIM ** (-0.5) * LOG2E


def dot_nt(a, b):
    return lax.dot_general(a, b, (((1,), (1,)), ((), ())), preferred_element_type=F32)


def dot_nn(a, b):
    return lax.dot_general(a, b, (((1,), (0,)), ((), ())), preferred_element_type=F32)


def half_masks(rows):
    lane = lax.broadcasted_iota(jnp.int32, (rows, 128), 1)
    return (lane < HEAD_DIM, lane >= HEAD_DIM)


def normal_form(value):
    center = value - jnp.mean(value, axis=1, keepdims=True)
    return center * lax.rsqrt(jnp.mean(center * center, axis=1, keepdims=True) + EPSILON)


def flip(value):
    return jnp.transpose(value.astype(F32)).astype(BF)


def stream_rows(xp_hbm, xc_hbm, rows, sems, visit):
    size = rows.shape[1]
    count = xp_hbm.shape[0] // size
    crow = xc_hbm.shape[0] // 2
    part = min(size, crow)

    def fetch(index, slot):
        row = pl.multiple_of(index * size, size)
        return pltpu.make_async_copy(xp_hbm.at[pl.ds(row, size)], rows.at[slot], sems.at[slot])

    fetch(0, 0).start()

    def one(index, carry):
        slot = lax.rem(index, 2)

        @pl.when(index + 1 < count)
        def _():
            fetch(index + 1, 1 - slot).start()

        fetch(index, slot).wait()
        visit(pl.multiple_of(index * size, size), size, rows[slot].astype(F32))
        return carry

    lax.fori_loop(0, count, one, 0)
    for index in range(2 * crow // part):
        copy = pltpu.make_async_copy(
            xc_hbm.at[pl.ds(index * part, part)], rows.at[0, pl.ds(0, part)], sems.at[0]
        )
        copy.start()
        copy.wait()
        visit(count * size + index * part, part, rows[0, :part].astype(F32))


def attend_forward_kernel(
    info,
    spot,
    xp_hbm,
    xc_hbm,
    xqp_ref,
    xqc_ref,
    w_ref,
    vec_ref,
    o_ref,
    lse_ref,
    q_ref,
    kv_hbm,
    kv,
    rows,
    qm,
    s_ref,
    mx,
    acc,
    sems,
    done,
):
    block = pl.program_id(0)
    gain, shift, bias_kv, bias_q = (vec_ref[i : i + 1, :] for i in range(4))

    def store(row, size):
        index = row // rows.shape[1]
        if isinstance(row, int):
            index = xp_hbm.shape[0] // rows.shape[1] + (row - xp_hbm.shape[0]) // size
        return pltpu.make_async_copy(
            kv.at[pl.ds(row, size)], kv_hbm.at[pl.ds(row, size)], done.at[index]
        )

    @pl.when(block == 0)
    def _():
        def visit(row, size, x):
            normed = (normal_form(x) * gain + shift).astype(BF)
            kv[pl.ds(row, size), :] = (dot_nn(normed, w_ref[:, HALF:]) + bias_kv).astype(BF)
            store(row, size).start()

        stream_rows(xp_hbm, xc_hbm, rows, sems, visit)

    TQ = q_ref.shape[0]
    x = jnp.where(spot[block, 0] > 0, xqc_ref[...].astype(F32), xqp_ref[...].astype(F32))
    normed = (normal_form(x) * gain + shift).astype(BF)
    query = ((dot_nn(normed, w_ref[:, :HALF]) + bias_q[:, :HALF]) * QSCALE).astype(BF)
    q_ref[...] = query
    base = pl.multiple_of(info[block, 0], TQ)
    tiles = info[block, 1]
    extra = info[block, 2]
    extra_row = pl.multiple_of(info[block, 3], TQ)
    diag = pl.multiple_of(info[block, 4], TQ)
    low, high = half_masks(TQ)
    zero = jnp.zeros((TQ, 128), BF)
    for pair in range(PAIRS):
        part = query[:, pair * 128 : (pair + 1) * 128]
        qm[2 * pair] = jnp.where(low, part, zero)
        qm[2 * pair + 1] = jnp.where(high, part, zero)

    def score(pair, row, size, column, first, masked):
        keys = kv[pl.ds(row, size), pair * 128 : (pair + 1) * 128]
        for side in (0, 1):
            raw = dot_nt(qm[2 * pair + side], keys)
            if masked:
                across = lax.broadcasted_iota(jnp.int32, (TQ, size), 1)
                down = lax.broadcasted_iota(jnp.int32, (TQ, size), 0)
                raw = jnp.where(across <= down, raw, MASKED)
            slot = 2 * (pair % 2) + side
            s_ref[slot, :, pl.ds(column, size)] = raw
            top = raw[:, :128]
            for piece in range(1, size // 128):
                top = jnp.maximum(top, raw[:, piece * 128 : (piece + 1) * 128])
            if not first:
                top = jnp.maximum(top, mx[slot])
            mx[slot] = top

    def settle(pair):
        for side in (0, 1):
            slot = 2 * (pair % 2) + side
            top = jnp.max(mx[slot], axis=1, keepdims=True)
            mx[slot] = jnp.broadcast_to(top, (TQ, 128))

    def blend(pair, row, size, column, first):
        vals = kv[pl.ds(row, size), HALF + pair * 128 : HALF + (pair + 1) * 128]
        wide = jnp.concatenate([vals, jnp.ones((size, 128), BF)], axis=1)
        for side in (0, 1):
            slot = 2 * (pair % 2) + side
            top = jnp.concatenate([mx[slot]] * (size // 128), axis=1)
            power = jnp.exp2(s_ref[slot, :, pl.ds(column, size)] - top).astype(BF)
            new = dot_nn(power, wide)
            if first:
                acc[side] = new
            else:
                acc[side] += new

    def sweep(step):
        step(diag, TQ, 0, True)

        def some(index, carry):
            row = pl.multiple_of(extra_row + index * TQ, TQ)
            step(row, TQ, pl.multiple_of(TQ + index * TQ, TQ), False)
            return carry

        lax.fori_loop(0, extra, some, 0)

        def one(index, carry):
            row = pl.multiple_of(base + index * TK, TQ)
            step(row, TK, pl.multiple_of(TK + index * TK, TQ), False)
            return carry

        lax.fori_loop(0, tiles, one, 0)

    sweep(lambda row, size, column, first: score(0, row, size, column, first, first))
    for pair in range(PAIRS):
        settle(pair)

        def both(row, size, column, first):
            if pair + 1 < PAIRS:
                score(pair + 1, row, size, column, first, first)
            blend(pair, row, size, column, first)

        sweep(both)
        sides = []
        for side in (0, 1):
            total = acc[side][:, 128:]
            sides.append(acc[side][:, :128] / total)
            tall = jnp.transpose(mx[2 * (pair % 2) + side] + jnp.log2(total))
            lse_ref[0, 2 * pair + side] = tall[0]
        o_ref[:, pair * 128 : (pair + 1) * 128] = jnp.where(low, sides[0], sides[1]).astype(BF)

    @pl.when(block == pl.num_programs(0) - 1)
    def _():
        size = rows.shape[1]
        part = min(size, xc_hbm.shape[0] // 2)
        for row in range(0, xp_hbm.shape[0], size):
            pltpu.make_async_copy(
                kv.at[pl.ds(row, size)], kv_hbm.at[pl.ds(row, size)], done.at[row // size]
            ).wait()
        for row in range(xp_hbm.shape[0], kv.shape[0], part):
            store(row, part).wait()


def query_specs(TQ):
    prompts = pl.BlockSpec((TQ, D), lambda i, s, t: (t[i, 1], 0))
    conts = pl.BlockSpec((TQ, D), lambda i, s, t: (t[i, 2], 0))
    return prompts, conts


def attend_forward(info, spot, xp, xc, weight, vec, TQ, size):
    blocks = info.shape[0]
    count = blocks * TQ
    keys = xp.shape[0] + xc.shape[0]
    tiles = xp.shape[0] // size + xc.shape[0] // min(size, xc.shape[0] // 2)
    whole = pl.BlockSpec(memory_space=pl.ANY)
    heads = pl.BlockSpec((TQ, HALF), lambda i, s, t: (i, 0))
    shape = jax.ShapeDtypeStruct
    return pl.pallas_call(
        attend_forward_kernel,
        grid_spec=pltpu.PrefetchScalarGridSpec(
            num_scalar_prefetch=2,
            grid=(blocks,),
            in_specs=[
                whole,
                whole,
                *query_specs(TQ),
                pl.BlockSpec(weight.shape, lambda i, s, t: (0, 0)),
                pl.BlockSpec(vec.shape, lambda i, s, t: (0, 0)),
            ],
            out_specs=[heads, pl.BlockSpec((1, 8, TQ), lambda i, s, t: (i, 0, 0)), heads, whole],
            scratch_shapes=[
                pltpu.VMEM((keys, D), BF),
                pltpu.VMEM((2, size, D), BF),
                pltpu.VMEM((NH, TQ, 128), BF),
                pltpu.VMEM((4, TQ, PLEN + TK), F32),
                pltpu.VMEM((4, TQ, 128), F32),
                pltpu.VMEM((2, TQ, 256), F32),
                pltpu.SemaphoreType.DMA((2,)),
                pltpu.SemaphoreType.DMA((tiles,)),
            ],
        ),
        out_shape=(
            shape((count, HALF), BF),
            shape((blocks, 8, TQ), F32),
            shape((count, HALF), BF),
            shape((keys, D), BF),
        ),
        compiler_params=pltpu.CompilerParams(
            dimension_semantics=("arbitrary",), vmem_limit_bytes=56 << 20
        ),
        cost_estimate=pl.CostEstimate(
            flops=int(4 * count * PLEN * HALF * 4) + 2 * D * D * keys,
            bytes_accessed=20 << 20,
            transcendentals=0,
        ),
        name="attend_forward",
    )(info, spot, xp, xc, xp, xc, weight, vec)


def attend_backward_kernel(
    chained,
    bounds,
    info,
    spot,
    xp_hbm,
    xc_hbm,
    kv_hbm,
    xqp_ref,
    xqc_ref,
    q_ref,
    o_ref,
    lse_ref,
    w_ref,
    vec_ref,
    *refs,
):
    parts, refs = refs[:4], refs[4:]
    if chained:
        old_w, old_vec, old_bias = refs[:3]
        refs = refs[3:]
    (
        tp_hbm,
        tc_hbm,
        gw_hbm,
        gvec_ref,
        gbias_ref,
        kv,
        kt,
        dkv,
        gw,
        qd,
        rows,
        table,
        qm,
        dom,
        dqt,
        drow,
        do_ref,
        sems,
        done,
    ) = refs
    block = pl.program_id(0)
    TQ = q_ref.shape[0]
    keys_all = kv.shape[0]
    gain, shift = (vec_ref[i : i + 1, :] for i in range(2))
    for part, (begin, end) in zip(parts, bounds):

        @pl.when((block >= begin) & (block < end))
        def _():
            do_ref[...] = part[...]


    @pl.when(block == 0)
    def _():
        load = pltpu.make_async_copy(kv_hbm, kv, sems.at[0])
        load.start()
        if chained:
            more = pltpu.make_async_copy(old_w, gw, sems.at[1])
            more.start()
            gvec_ref[...] = old_vec[...]
            gbias_ref[...] = old_bias[...]
        else:
            gw[...] = jnp.zeros_like(gw)
            gvec_ref[...] = jnp.zeros_like(gvec_ref)
            gbias_ref[...] = jnp.zeros_like(gbias_ref)

        def clear(index, carry):
            dkv[pl.ds(pl.multiple_of(index * TQ, TQ), TQ), :] = jnp.zeros((TQ, D), F32)
            return carry

        lax.fori_loop(0, keys_all // TQ, clear, 0)
        load.wait()

        def prepare(index, carry):
            row = pl.multiple_of(index * TQ, TQ)
            kt[:, pl.ds(row, TQ)] = flip(kv[pl.ds(row, TQ), :HALF])
            return carry

        lax.fori_loop(0, keys_all // TQ, prepare, 0)
        if chained:
            more.wait()

    base = pl.multiple_of(info[block, 0], TQ)
    tiles = info[block, 1]
    extra = info[block, 2]
    extra_row = pl.multiple_of(info[block, 3], TQ)
    diag = pl.multiple_of(info[block, 4], TQ)
    low, high = half_masks(TQ)
    zero = jnp.zeros((TQ, 128), BF)
    for pair in range(PAIRS):
        lanes = slice(pair * 128, (pair + 1) * 128)
        part = q_ref[:, lanes]
        qm[2 * pair] = jnp.where(low, part, zero)
        qm[2 * pair + 1] = jnp.where(high, part, zero)
        part = do_ref[:, lanes]
        dom[2 * pair] = jnp.where(low, part, zero)
        dom[2 * pair + 1] = jnp.where(high, part, zero)
        product = jnp.transpose(part.astype(F32) * o_ref[:, lanes].astype(F32))
        drow[2 * pair] = jnp.sum(product[:HEAD_DIM], axis=0)
        drow[2 * pair + 1] = jnp.sum(product[HEAD_DIM:], axis=0)

    def step(row, size, first):
        for pair in range(PAIRS):
            lanes = slice(pair * 128, (pair + 1) * 128)
            more = slice(HALF + pair * 128, HALF + (pair + 1) * 128)
            keys = kv[pl.ds(row, size), lanes]
            vals = kv[pl.ds(row, size), more]
            dk = None
            dv = None
            for side in (0, 1):
                head = 2 * pair + side
                raw = dot_nt(keys, qm[head])
                if first:
                    across = lax.broadcasted_iota(jnp.int32, (size, TQ), 1)
                    down = lax.broadcasted_iota(jnp.int32, (size, TQ), 0)
                    raw = jnp.where(down <= across, raw, MASKED)
                probs = jnp.exp2(raw - lse_ref[0, head : head + 1, :])
                grad = dot_nt(vals, dom[head])
                slope = (probs * (grad - drow[head : head + 1, :])).astype(BF)
                probs = probs.astype(BF)
                part_v = dot_nn(probs, dom[head])
                part_k = dot_nn(slope, qm[head])
                dv = part_v if dv is None else dv + part_v
                dk = part_k if dk is None else dk + part_k
                spot = slice(head * HEAD_DIM, (head + 1) * HEAD_DIM)
                new = dot_nn(kt[spot, pl.ds(row, size)], slope)
                if first:
                    dqt[spot, :] = new
                else:
                    dqt[spot, :] += new
            dkv[pl.ds(row, size), lanes] += dk
            dkv[pl.ds(row, size), more] += dv

    step(diag, TQ, True)

    def some(index, carry):
        step(pl.multiple_of(extra_row + index * TQ, TQ), TQ, False)
        return carry

    lax.fori_loop(0, extra, some, 0)

    def one(index, carry):
        step(pl.multiple_of(base + index * TK, TQ), TK, False)
        return carry

    lax.fori_loop(0, tiles, one, 0)
    x = jnp.where(spot[block, 0] > 0, xqc_ref[...].astype(F32), xqp_ref[...].astype(F32))
    dq_full = jnp.transpose(dqt[...]) * HEAD_DIM ** (-0.5)
    dq = dq_full.astype(BF)
    gw[:, :HALF] += dot_nn(flip(normal_form(x) * gain + shift), dq)
    gbias_ref[0:1, :HALF] += jnp.sum(dq_full, axis=0, keepdims=True)
    qd[pl.ds(pl.multiple_of(block * TQ, TQ), TQ), :] = dot_nt(dq, w_ref[:, :HALF])

    @pl.when(block == pl.num_programs(0) - 1)
    def _():
        prompt_rows = xp_hbm.shape[0]
        size = rows.shape[1]
        crow = xc_hbm.shape[0] // 2
        part = min(size, crow)
        count = prompt_rows // size
        own, mate = spot[0, 3], spot[0, 4]

        def send(slot, row):
            return pltpu.make_async_copy(
                table.at[slot], tp_hbm.at[pl.ds(row, size)], done.at[slot]
            )

        def visit(row, size_now, x):
            hat = normal_form(x)
            grad_k = dkv[pl.ds(row, size_now), :HALF] * (1.0 / LOG2E)
            grad_v = dkv[pl.ds(row, size_now), HALF:]
            grad = jnp.concatenate([grad_k.astype(BF), grad_v.astype(BF)], axis=1)
            gw[:, HALF:] += dot_nn(flip(hat * gain + shift), grad)
            gbias_ref[0:1, HALF : 2 * HALF] += jnp.sum(grad_k, axis=0, keepdims=True)
            gbias_ref[0:1, 2 * HALF :] += jnp.sum(grad_v, axis=0, keepdims=True)
            change = dot_nt(grad, w_ref[:, HALF:])
            if isinstance(row, int):
                first = row - prompt_rows
                which = first // crow
                begin = which * (size + crow) + size + first - which * crow
                change = change + qd[begin : begin + size_now, :]
            else:
                index = row // size
                begin = jnp.where(index == mate, size + crow, 0)
                begin = pl.multiple_of(begin, math.gcd(size, crow))
                weight = jnp.where((index == own) | (index == mate), 1.0, 0.0)
                change = change + weight * qd[pl.ds(begin, size_now), :]
            gvec_ref[0:1, :] += jnp.sum(change * hat, axis=0, keepdims=True)
            gvec_ref[1:2, :] += jnp.sum(change, axis=0, keepdims=True)
            change = change.astype(BF)
            if isinstance(row, int):
                slot = (first // part) % 2
                if first // part >= 2:
                    pltpu.make_async_copy(
                        table.at[slot, pl.ds(0, part)],
                        tc_hbm.at[pl.ds(first - 2 * part, part)],
                        done.at[slot],
                    ).wait()
                else:
                    send(slot, prompt_rows - (2 - slot) * size).wait()
                table[slot, :part] = change
                pltpu.make_async_copy(
                    table.at[slot, pl.ds(0, part)],
                    tc_hbm.at[pl.ds(first, part)],
                    done.at[slot],
                ).start()
            else:
                slot = lax.rem(index, 2)

                @pl.when(index >= 2)
                def _():
                    send(slot, pl.multiple_of(row - 2 * size, size)).wait()

                table[slot] = change
                send(slot, row).start()

        stream_rows(xp_hbm, xc_hbm, rows, sems, visit)
        last = 2 * crow // part
        for index in range(last - 2, last):
            pltpu.make_async_copy(
                table.at[index % 2, pl.ds(0, part)],
                tc_hbm.at[pl.ds(index * part, part)],
                done.at[index % 2],
            ).wait()
        out = pltpu.make_async_copy(gw, gw_hbm, sems.at[0])
        out.start()
        out.wait()


def attend_backward(info, spot, xp, xc, kv, q, do, o, lse, weight, vec, totals, TQ, size):
    blocks = info.shape[0]
    count = blocks * TQ
    keys = kv.shape[0]
    whole = pl.BlockSpec(memory_space=pl.ANY)
    heads = pl.BlockSpec((TQ, HALF), lambda i, s, t: (i, 0))
    shape = jax.ShapeDtypeStruct
    fixed = [
        pl.BlockSpec((8, D), lambda i, s, t: (0, 0)),
        pl.BlockSpec((8, 3 * HALF), lambda i, s, t: (0, 0)),
    ]
    extra = () if totals is None else tuple(totals)
    bounds, parts_in, begin = [], [], 0
    for part in do:
        end = begin + part.shape[0] // TQ
        bounds.append((begin, end))
        parts_in.append(
            pl.BlockSpec(
                (TQ, HALF),
                lambda i, s, t, begin=begin, end=end: (jnp.clip(i - begin, 0, end - begin - 1), 0),
            )
        )
        begin = end
    return pl.pallas_call(
        functools.partial(attend_backward_kernel, totals is not None, bounds),
        grid_spec=pltpu.PrefetchScalarGridSpec(
            num_scalar_prefetch=2,
            grid=(blocks,),
            in_specs=[
                whole,
                whole,
                whole,
                *query_specs(TQ),
                heads,
                heads,
                pl.BlockSpec((1, 8, TQ), lambda i, s, t: (i, 0, 0)),
                pl.BlockSpec(weight.shape, lambda i, s, t: (0, 0)),
                pl.BlockSpec(vec.shape, lambda i, s, t: (0, 0)),
                *parts_in,
            ]
            + ([whole] + fixed if extra else []),
            out_specs=[whole, whole, whole] + fixed,
            scratch_shapes=[
                pltpu.VMEM((keys, D), BF),
                pltpu.VMEM((HALF, keys), BF),
                pltpu.VMEM((keys, D), F32),
                pltpu.VMEM((D, 3 * HALF), F32),
                pltpu.VMEM((count, D), F32),
                pltpu.VMEM((2, size, D), BF),
                pltpu.VMEM((2, size, D), BF),
                pltpu.VMEM((NH, TQ, 128), BF),
                pltpu.VMEM((NH, TQ, 128), BF),
                pltpu.VMEM((HALF, TQ), F32),
                pltpu.VMEM((8, TQ), F32),
                pltpu.VMEM((TQ, HALF), BF),
                pltpu.SemaphoreType.DMA((2,)),
                pltpu.SemaphoreType.DMA((2,)),
            ],
        ),
        out_shape=(
            shape(xp.shape, BF),
            shape(xc.shape, BF),
            shape((D, 3 * HALF), F32),
            shape((8, D), F32),
            shape((8, 3 * HALF), F32),
        ),
        compiler_params=pltpu.CompilerParams(
            dimension_semantics=("arbitrary",), vmem_limit_bytes=62 << 20
        ),
        cost_estimate=pl.CostEstimate(
            flops=int(10 * count * PLEN * HALF * 4) + 4 * D * D * keys,
            bytes_accessed=30 << 20,
            transcendentals=0,
        ),
        name="attend_backward",
    )(info, spot, xp, xc, kv, xp, xc, q, o, lse, weight, vec, *do, *extra)


def gelu_parts(value):
    rate = math.sqrt(2.0 / math.pi)
    square = value * value
    half = 0.5 + 0.5 * jnp.tanh(value * (rate + (rate * 0.044715) * square))
    slope = half + value * (half * (1.0 - half)) * (2.0 * rate + (6.0 * rate * 0.044715) * square)
    return value * half, slope


def feed_forward_kernel(
    prompt_parts,
    clen,
    count,
    groups,
    lens,
    places,
    xp_ref,
    xc_ref,
    gp_ref,
    gc_ref,
    vec_ref,
    bfc_ref,
    *refs,
):
    heads, refs = refs[: 4 * MB], refs[4 * MB :]
    pieces = refs[:count]
    (
        fp_ref,
        fc_ref,
        hp_ref,
        hc_ref,
        dmine_ref,
        dmate_ref,
        gvec_ref,
        gbfc_ref,
        grads_hbm,
        more_hbm,
        wp,
        wfc,
        wout,
        ap,
        afc,
        aout,
        stage,
        mine_ref,
        mate_ref,
        sems,
    ) = refs[count:]
    core = places[0]
    batch = pl.program_id(0)
    part = pl.program_id(1)
    tile = mine_ref.shape[0]
    is_cont = part >= prompt_parts
    begin = (batch == 0) & (part == 0)

    @pl.when(begin)
    def _():
        def loads_of(first_half):
            moves = []
            for index, piece in enumerate(pieces):
                size = piece.shape[1]
                half = None
                if first_half is not None:
                    half = first_half if index < count // 2 else 1 - first_half
                split = (D + 2 * FF) // 2 - D
                spans = [(wp, 0, 0, D), (wfc, 0, D, FF)]
                spans += [(wout, block * D, D + FF + block * D, D) for block in range(FF // D)]
                if half == 0:
                    spans = [(wp, 0, 0, D), (wfc, (0, 0), D, split)]
                elif half == 1:
                    spans = [(wfc, (0, split), 0, FF - split)]
                    spans += [
                        (wout, block * D, FF - split + block * D, D) for block in range(FF // D)
                    ]
                for inner in range(piece.shape[0]):
                    row = pl.multiple_of(places[1 + index * piece.shape[0] + inner], 16)
                    turned = pl.multiple_of(lax.rem(row + core * HALF, D), 16)
                    for target, offset, column, width in spans:
                        source = piece.at[inner, :, pl.ds(column, width)]
                        if target is wp:
                            view = wp.at[pl.ds(turned, size), :]
                        elif target is wfc:
                            begin = offset[1] if isinstance(offset, tuple) else 0
                            view = wfc.at[pl.ds(row, size), pl.ds(begin, width)]
                        else:
                            view = wout.at[pl.ds(offset + row, size), :]
                        moves.append((source, view))
            return [
                pltpu.make_async_copy(source, view, sems.at[index])
                for index, (source, view) in enumerate(moves)
            ]

        def load_all(first_half):
            loads = loads_of(first_half)
            for load in loads:
                load.start()
            for load in loads:
                load.wait()

        ap[...] = jnp.zeros_like(ap)
        gvec_ref[...] = jnp.zeros_like(gvec_ref)
        gbfc_ref[...] = jnp.zeros_like(gbfc_ref)

        def clear(index, carry):
            row = pl.multiple_of(index * 64, 64)
            afc[pl.ds(row, 64), :] = jnp.zeros((64, FF), F32)
            aout[pl.ds(row, 64), :] = jnp.zeros((64, FF), F32)
            return carry

        lax.fori_loop(0, D // 64, clear, 0)
        if groups == 1:
            load_all(None)
        else:

            @pl.when(core == 0)
            def _():
                load_all(0)

            @pl.when(core != 0)
            def _():
                load_all(1)

    b_proj = vec_ref[0:1, :]
    gain = vec_ref[1:2, :]
    shift = vec_ref[2:3, :]
    b_out = vec_ref[3:4, :]
    x = jnp.where(is_cont, xc_ref[0].astype(F32), xp_ref[0].astype(F32))
    gy = jnp.where(is_cont, gc_ref[0].astype(F32), gp_ref[0].astype(F32))
    start = jnp.maximum(part - prompt_parts, 0) * tile
    length = lens[batch, start // clen]
    place = lax.broadcasted_iota(jnp.int32, (tile, 1), 0) + start % clen
    valid = jnp.where(jnp.logical_not(is_cont) | (place < length), 1.0, 0.0)

    for m in range(MB):
        for kind, wanted in enumerate((jnp.logical_not(is_cont), is_cont)):

            @pl.when((batch == m) & wanted)
            def _():
                mine_ref[...] = heads[4 * m + kind][...]
                mate_ref[...] = heads[4 * m + 2 + kind][...]

    mine = mine_ref[...]
    mate = mate_ref[...]
    h = x + valid * (dot_nn(mine, wp[:HALF, :]) + dot_nn(mate, wp[HALF:, :]) + b_proj)
    center = h - jnp.mean(h, axis=1, keepdims=True)
    rate = lax.rsqrt(jnp.mean(center * center, axis=1, keepdims=True) + EPSILON)
    hat = center * rate
    second = (hat * gain + shift).astype(BF)
    dz_full = valid * gy
    dz = dz_full.astype(BF)
    second_t = flip(second)
    dz_t = flip(dz)
    result = None
    back = None
    for index in range(FF // D):
        cols = slice(index * D, (index + 1) * D)
        inner = dot_nn(second, wfc[:, cols]) + bfc_ref[:, cols]
        act, slope = gelu_parts(inner)
        act = act.astype(BF)
        du_full = dot_nt(dz, wout[cols, :]) * slope
        du = du_full.astype(BF)
        gbfc_ref[0:1, cols] += jnp.sum(du_full, axis=0, keepdims=True)
        new = dot_nn(act, wout[cols, :])
        result = new if result is None else result + new
        new = dot_nt(du, wfc[:, cols])
        back = new if back is None else back + new
        aout[:, cols] += dot_nn(dz_t, act)
        afc[:, cols] += dot_nn(second_t, du)
    final = (h + valid * (result + b_out)).astype(BF)
    e2 = back * gain
    dh = gy + rate * (
        e2
        - jnp.mean(e2, axis=1, keepdims=True)
        - hat * jnp.mean(e2 * hat, axis=1, keepdims=True)
    )
    dy_full = valid * dh
    dy = dy_full.astype(BF)
    gvec_ref[0:1, :] += jnp.sum(dy_full, axis=0, keepdims=True)
    gvec_ref[1:2, :] += jnp.sum(back * hat, axis=0, keepdims=True)
    gvec_ref[2:3, :] += jnp.sum(back, axis=0, keepdims=True)
    gvec_ref[3:4, :] += jnp.sum(dz.astype(F32), axis=0, keepdims=True)
    ap[:HALF, :] += dot_nn(flip(mine), dy)
    ap[HALF:, :] += dot_nn(flip(mate), dy)
    dmine_ref[0] = dot_nt(dy, wp[:HALF, :]).astype(BF)
    dmate_ref[0] = dot_nt(dy, wp[HALF:, :]).astype(BF)
    dh = dh.astype(BF)

    @pl.when(jnp.logical_not(is_cont))
    def _():
        fp_ref[0] = final
        hp_ref[0] = dh

    @pl.when(is_cont)
    def _():
        fc_ref[0] = final
        hc_ref[0] = dh

    @pl.when((batch == pl.num_programs(0) - 1) & (part == pl.num_programs(1) - 1))
    def _():
        blocks, share = stage.shape[1], stage.shape[2]
        sends = []

        def send(column, fetch):
            slot = len(sends) % 2
            if len(sends) >= 2:
                sends[-2].wait()
            for block in range(blocks):
                stage[slot, block] = fetch(block).astype(BF)
            width = grads_hbm.shape[2]
            if column < width:
                target = grads_hbm.at[:, :, pl.ds(column, D)]
            else:
                target = more_hbm.at[:, :, pl.ds(column - width, D)]
            sends.append(pltpu.make_async_copy(stage.at[slot], target, sems.at[slot]))
            sends[-1].start()

        def first_row(block):
            return (block % groups * (blocks // groups) + block // groups) * share

        def proj_rows(block):
            row = lax.rem(first_row(block) + core * HALF, D)
            return ap[pl.ds(pl.multiple_of(row, math.gcd(share, HALF)), share), :]

        send(0, proj_rows)
        for part_of in range(FF // D):
            cols = slice(part_of * D, (part_of + 1) * D)
            send(D + part_of * D, lambda block: afc[first_row(block) : first_row(block) + share, cols])
        for part_of in range(FF // D):
            cols = slice(part_of * D, (part_of + 1) * D)
            ap[...] = jnp.transpose(aout[:, cols])
            send(
                D + FF + part_of * D,
                lambda block: ap[first_row(block) : first_row(block) + share, :],
            )
        for copy in sends[-2:]:
            copy.wait()


def feed_forward(lens, places, prompt_in, cont_in, prompt_cot, cont_cot, heads_in, vec, bfc, pieces, groups, share):
    prow = prompt_in.shape[1]
    crow = cont_in.shape[1]
    clen = crow // lens.shape[1]
    tile = min(256, prow, clen)
    prompt_parts = prow // tile
    parts = prompt_parts + crow // tile
    prompts = pl.BlockSpec((1, tile, D), lambda m, i, s, t: (m, jnp.minimum(i, prompt_parts - 1), 0))
    conts = pl.BlockSpec((1, tile, D), lambda m, i, s, t: (m, jnp.maximum(i - prompt_parts, 0), 0))
    heads = pl.BlockSpec((1, tile, HALF), lambda m, i, s, t: (m, i, 0))
    whole = pl.BlockSpec(memory_space=pl.ANY)
    def part_spec(own, first, count):
        def place(m, i, s, t):
            inside = jnp.clip(i - first, 0, count - 1)
            return (jnp.where(m == own, inside, jnp.where(m < own, 0, count - 1)), 0)

        return pl.BlockSpec((tile, HALF), place)

    parts_in = []
    for own in range(MB):
        parts_in += [part_spec(own, 0, prompt_parts), part_spec(own, prompt_parts, crow // tile)] * 2
    fixed = pl.BlockSpec((8, D), lambda m, i, s, t: (0, 0))
    long = pl.BlockSpec((8, FF), lambda m, i, s, t: (0, 0))
    shape = jax.ShapeDtypeStruct
    rows = MB * (prow + crow)
    return pl.pallas_call(
        functools.partial(feed_forward_kernel, prompt_parts, clen, len(pieces), groups),
        grid_spec=pltpu.PrefetchScalarGridSpec(
            num_scalar_prefetch=2,
            grid=(MB, parts),
            in_specs=[
                prompts,
                conts,
                prompts,
                conts,
                fixed,
                pl.BlockSpec((1, FF), lambda m, i, s, t: (0, 0)),
            ]
            + parts_in
            + [whole] * len(pieces),
            out_specs=[prompts, conts, prompts, conts, heads, heads, fixed, long, whole, whole],
            scratch_shapes=[
                pltpu.VMEM((D, D), BF),
                pltpu.VMEM((D, FF), BF),
                pltpu.VMEM((FF, D), BF),
                pltpu.VMEM((D, D), F32),
                pltpu.VMEM((D, FF), F32),
                pltpu.VMEM((D, FF), F32),
                pltpu.VMEM((2, D // share, share, D), BF),
                pltpu.VMEM((tile, HALF), BF),
                pltpu.VMEM((tile, HALF), BF),
                pltpu.SemaphoreType.DMA(
                    (max(16, (2 + FF // D) * sum(piece.shape[0] for piece in pieces)),)
                ),
            ],
        ),
        out_shape=(
            shape(prompt_in.shape, BF),
            shape(cont_in.shape, BF),
            shape(prompt_in.shape, BF),
            shape(cont_in.shape, BF),
            shape((MB, prow + crow, HALF), BF),
            shape((MB, prow + crow, HALF), BF),
            shape((8, D), F32),
            shape((8, FF), F32),
            shape((D // share, share, D + FF + FF // 2), BF),
            shape((D // share, share, FF // 2), BF),
        ),
        compiler_params=pltpu.CompilerParams(
            dimension_semantics=("arbitrary", "arbitrary"), vmem_limit_bytes=63 << 20
        ),
        cost_estimate=pl.CostEstimate(
            flops=6 * rows * (D * D + 2 * D * FF), bytes_accessed=50 << 20, transcendentals=0
        ),
        name="feed_forward",
    )(lens, places, prompt_in, cont_in, prompt_cot, cont_cot, vec, bfc, *heads_in, *pieces)


def input_grad_kernel(x_ref, slope_ref, vec_ref, *refs):
    batch = pl.program_id(0)
    out_ref, change_ref = refs[MB:]
    for m in range(MB):

        @pl.when(batch == m)
        def _():
            change_ref[...] = refs[m][...].astype(F32)

    x = x_ref[0].astype(F32)
    center = x - jnp.mean(x, axis=1, keepdims=True)
    rate = lax.rsqrt(jnp.mean(center * center, axis=1, keepdims=True) + EPSILON)
    hat = center * rate
    e1 = change_ref[...] * vec_ref[0:1, :]
    change = e1 - jnp.mean(e1, axis=1, keepdims=True)
    change = change - hat * jnp.mean(e1 * hat, axis=1, keepdims=True)
    out_ref[0] = (slope_ref[0].astype(F32) + rate * change).astype(BF)


def input_grads(x, slope, vec, tables, tile):
    count = x.shape[1] // tile

    def table_spec(own):
        def place(m, i):
            return (jnp.where(m == own, i, jnp.where(m < own, 0, count - 1)), 0)

        return pl.BlockSpec((tile, D), place)

    rows = pl.BlockSpec((1, tile, D), lambda m, i: (m, i, 0))
    return pl.pallas_call(
        input_grad_kernel,
        grid=(MB, count),
        in_specs=[rows, rows, pl.BlockSpec(vec.shape, lambda m, i: (0, 0))]
        + [table_spec(own) for own in range(MB)],
        out_specs=rows,
        out_shape=jax.ShapeDtypeStruct(x.shape, BF),
        scratch_shapes=[pltpu.VMEM((tile, D), F32)],
        compiler_params=pltpu.CompilerParams(
            dimension_semantics=("arbitrary", "arbitrary"), vmem_limit_bytes=24 << 20
        ),
        name="input_grads",
    )(x, slope, vec, *tables)


HEAD_COLS = 3 * HALF
SMALL_COLS = 128


def neighbour(value, axis, distance):
    pairs = [(i, i ^ distance) for i in range(lax.axis_size(axis))]
    return lax.ppermute(value, axis, pairs)


def swap(value):
    return neighbour(value, "fsdp", 1)


def is_square():
    return lax.axis_size("grp") == 4 and lax.axis_size("fsdp") == 8


def spread_one(block):
    half = block.shape[0] // 2
    pieces = [block[:half], block[half:]]
    return [
        jnp.stack([piece, neighbour(piece, "grp", distance)])
        for piece, distance in zip(pieces, (1, 2))
    ]


def spread_two(boths):
    return [neighbour(both, "grp", distance) for both, distance in zip(boths, (2, 1))]


def spread_pieces(boths, fars):
    return [
        (boths[0], (0, 1), 0),
        (fars[0], (2, 3), 0),
        (boths[1], (0, 2), 1),
        (fars[1], (1, 3), 1),
    ]


def gather_zone(packed):
    if not is_square():
        return lax.all_gather(packed, ALL, axis=0, tiled=True)
    groups = [list(range(c, lax.axis_size("fsdp"), 2)) for c in (0, 1)]
    return lax.all_gather(packed, "fsdp", axis=0, tiled=True, axis_index_groups=groups)


def chip_rows(keep, send, core):
    other = swap(send)
    return jnp.where(
        core == 0,
        jnp.concatenate([keep, other], axis=0),
        jnp.concatenate([other, keep], axis=0),
    )


def join_front(boths, fars):
    own = lax.axis_index("grp")
    parts = {}
    for pair, offsets, index in spread_pieces(boths, fars):
        for which, offset in enumerate(offsets):
            parts[offset, index] = pair[which]
    table = jnp.stack([jnp.concatenate([parts[k, 0], parts[k, 1]], axis=0) for k in range(4)])
    return jnp.concatenate(
        [lax.dynamic_index_in_dim(table, own ^ k, 0, keepdims=False) for k in range(4)], axis=0
    )


def join_rest(boths, fars):
    own = lax.axis_index("grp")
    size = boths[0].shape[1]
    pieces, rows = [], []
    for pair, offsets, index in spread_pieces(boths, fars):
        pieces.append(pair)
        for offset in offsets:
            rows.append((own ^ offset) * 2 * size + index * size)
    return pieces + [swap(piece) for piece in pieces], rows + rows


def pin(*values):
    return list(lax.optimization_barrier(tuple(values)))


def pick(array, index, axis):
    return lax.dynamic_index_in_dim(array, index, axis, keepdims=False)


def meet(array, index, axis, name, distance):
    other = neighbour(pick(array, 1 - index, axis), name, distance)
    return (pick(array, index, axis).astype(F32) + other.astype(F32)).astype(BF)


def reduce_steps():
    if not is_square():
        groups = [list(range(c, lax.axis_size("fsdp"), 2)) for c in (0, 1)]

        def along_grp(value):
            return lax.psum_scatter(value, "grp", scatter_dimension=0, tiled=True)

        def along_chips(value):
            return lax.psum_scatter(
                value, "fsdp", scatter_dimension=0, tiled=True, axis_index_groups=groups
            )

        return [along_grp, along_chips]

    own = lax.axis_index("grp")
    x, y = own % 2, own // 2
    z = lax.axis_index("fsdp") // 2

    def one(value):
        value = value.reshape(2, 2, 2, value.shape[0] // 8, value.shape[1])
        return meet(value[:, :, 0], x, 1, "grp", 1), meet(value[:, :, 1], y, 0, "grp", 2)

    def two(pair):
        value = jnp.concatenate(
            [meet(pair[0], y, 0, "grp", 2), meet(pair[1], x, 0, "grp", 1)], axis=0
        )
        return value.reshape(2, 2, value.shape[0] // 4, value.shape[1])

    def three(value):
        return meet(value, z % 2, 1, "fsdp", 2)

    def four(value):
        return meet(value, z // 2, 0, "fsdp", 4)

    return [one, two, three, four]


def reduce_parameters(value):
    for step in reduce_steps():
        value = step(value)
    return value


def own_rows(value, core):
    share = value.shape[0] // 2
    keep = lax.dynamic_slice_in_dim(value, core * share, share, 0)
    other = swap(lax.dynamic_slice_in_dim(value, (1 - core) * share, share, 0))
    return keep, other


def square_steps(core):
    own = lax.axis_index("grp")
    x, y = own % 2, own // 2

    def one(value):
        cols = value.shape[-1] // 2
        value = value.reshape((2, 2) + value.shape[1:])
        return (
            meet(value[..., :cols], x, 1, "grp", 1),
            meet(value[..., cols:], y, 0, "grp", 2),
        )

    def two(pair):
        return jnp.concatenate(
            [meet(pair[0], y, 0, "grp", 2), meet(pair[1], x, 0, "grp", 1)], axis=1
        )

    return [one, two]


def body(
    prompt_in,
    cont_in,
    prompt_cot,
    cont_cot,
    cont_prompt,
    cont_len,
    ln1_gain,
    ln1_bias,
    attn_weight,
    attn_bias,
    proj_weight,
    proj_bias,
    ln2_gain,
    ln2_bias,
    fc_weight,
    fc_bias,
    out_weight,
    out_bias,
):
    fsdp = lax.axis_size("fsdp")
    devices = fsdp * lax.axis_size("grp")
    prow = prompt_in.shape[1]
    crow = cont_in.shape[1]
    conts = cont_prompt.shape[2]
    clen = crow // conts
    mine = prow + crow
    TQ = min(256, prow, clen)
    prompt_rows = NPR * PLEN
    place = lax.axis_index("fsdp")
    core = place % 2
    share = D // devices
    wide = FF // D

    vectors = (ln1_gain, ln1_bias, attn_bias[0], attn_bias[1], proj_bias, ln2_gain, ln2_bias, out_bias)
    columns = jnp.concatenate(
        [v[:, None] for v in vectors] + [fc_bias.reshape(wide, share).T], axis=1
    )
    columns = jnp.pad(columns, ((0, 0), (0, SMALL_COLS - columns.shape[1])))
    prompt_all = [lax.all_gather(prompt_in[m], "fsdp", axis=0, tiled=True) for m in range(MB)]
    square = is_square()
    columns = columns.astype(BF)
    heads = attn_weight.astype(BF).reshape(share, 3, 2, HALF)
    keep = lax.dynamic_index_in_dim(heads, core, 2, keepdims=False).reshape(share, HEAD_COLS)
    send = lax.dynamic_index_in_dim(heads, 1 - core, 2, keepdims=False).reshape(share, HEAD_COLS)
    rest = jnp.concatenate(
        [
            proj_weight,
            fc_weight.reshape(share, devices, wide, share).transpose(0, 2, 1, 3).reshape(share, FF),
            out_weight.reshape(wide, share, D).transpose(1, 0, 2).reshape(share, FF),
        ],
        axis=1,
    ).astype(BF)
    if square:
        zone = gather_zone(
            chip_rows(
                jnp.concatenate([keep, columns], axis=1),
                jnp.concatenate([send, columns], axis=1),
                core,
            )
        )
        half = rest.shape[1] // 2
        rest = chip_rows(
            lax.dynamic_slice_in_dim(rest, core * half, half, 1),
            lax.dynamic_slice_in_dim(rest, (1 - core) * half, half, 1),
            core,
        )
        cut = half // 256 * 128
        first, zone = pin(rest[:, :cut], zone)
        zones = [gather_zone(first)]
        front_boths = spread_one(zone)
        zones[0], second, *front_boths = pin(zones[0], rest[:, cut:], *front_boths)
        zones.append(gather_zone(second))
        front_fars = spread_two(front_boths)
        zones[1], *front_fars = pin(zones[1], *front_fars)
        front = join_front(front_boths, front_fars)
        rest_boths = spread_one(jnp.concatenate(zones, axis=1))
    else:
        zone = gather_zone(jnp.concatenate([heads.reshape(share, 3 * D), columns], axis=1))
        front = jnp.concatenate(
            [
                lax.dynamic_index_in_dim(
                    zone[:, : 3 * D].reshape(D, 3, 2, HALF), core, 2, keepdims=False
                ).reshape(D, HEAD_COLS),
                zone[:, 3 * D :],
            ],
            axis=1,
        )
        pieces = [gather_zone(rest).reshape(2, HALF, -1)]
        piece_rows = [0, HALF]
    w_heads = front[:, :HEAD_COLS]
    small = front[:, HEAD_COLS:].astype(F32)
    gain_a, shift_a, bias_q, bias_v, b_proj, gain_b, shift_b, b_out = (small[:, i] for i in range(8))
    b_fc = small[:, 8 : 8 + wide].T.reshape(1, FF)
    bias_q = lax.dynamic_slice_in_dim(bias_q, core * HALF, HALF)
    bias_v = lax.dynamic_slice_in_dim(bias_v, core * HALF, HALF)
    none = jnp.zeros((HALF,), F32)
    vec_a = jnp.stack(
        [gain_a, shift_a, jnp.concatenate([none, bias_v]), jnp.concatenate([bias_q, none])]
        + [jnp.zeros((D,), F32)] * 4
    )
    vec_b = jnp.pad(jnp.stack([b_proj, gain_b, shift_b, b_out]), ((0, 4), (0, 0)))

    cont_mate = swap(cont_in)
    plan_mate = swap(cont_prompt[:, 0, :].astype(F32)).astype(jnp.int32)

    def balanced(index):
        ends = fsdp // NPR
        other = index // ends * ends + ends - 1 - (index % ends - index % 2)
        return index + (index % 2) * (other - index)

    own_place = balanced(place)
    mate_place = balanced(place + 1 - 2 * core)
    own_row = own_place * prow
    mate_row = mate_place * prow
    own_pairs = [(i, balanced(i)) for i in range(fsdp)]
    mate_pairs = [(i, balanced(i ^ 1)) for i in range(fsdp)]

    def send_home(own, other):
        return (
            lax.ppermute(own[:prow], "fsdp", own_pairs),
            own[prow:],
            lax.ppermute(other[:prow], "fsdp", mate_pairs),
            swap(other[prow:]),
        )

    def send_back(own, other):
        return [
            lax.ppermute(own[:prow], "fsdp", [(b, a) for a, b in own_pairs]),
            own[prow:],
            lax.ppermute(other[:prow], "fsdp", [(b, a) for a, b in mate_pairs]),
            swap(other[prow:]),
        ]

    def prompt_plan(row):
        row = row + TQ * jnp.arange(prow // TQ)
        spot = row % PLEN
        return jnp.stack(
            [
                row - spot,
                spot // TK,
                spot % TK // TQ,
                row - spot + spot // TK * TK,
                row,
            ],
            axis=1,
        )

    def cont_plan(follows, first):
        blocks = clen // TQ
        follows = jnp.repeat(follows, blocks)
        index = jnp.arange(conts * blocks)
        begin = prompt_rows + first + index // blocks * clen
        return jnp.stack(
            [
                follows * PLEN,
                jnp.full(index.shape, PLEN // TK),
                index % blocks,
                begin,
                begin + index % blocks * TQ,
            ],
            axis=1,
        )

    def plan_of(m):
        return jnp.concatenate(
            [
                prompt_plan(own_row),
                cont_plan(cont_prompt[m, 0], 0),
                prompt_plan(mate_row),
                cont_plan(plan_mate[m], crow),
            ],
            axis=0,
        ).astype(jnp.int32)

    blocks = []
    for kind, count in (("own", prow), ("cont", crow), ("mate", prow), ("other", crow)):
        for index in range(count // TQ):
            prompt = (mate_row if kind in ("mate", "other") else own_row) // TQ
            last = prow // TQ - 1
            if kind in ("own", "mate"):
                blocks.append((0, prompt + index, 0 if kind == "own" else crow // TQ - 1))
            else:
                first = 0 if kind == "cont" else crow // TQ
                blocks.append((1, prompt + last, first + index))
    spot = jnp.stack(
        [
            jnp.stack([jnp.asarray(value, jnp.int32) for value in entry + (own_place, mate_place)])
            for entry in blocks
        ]
    ).astype(jnp.int32)

    saved = []
    outs = []
    for m in range(MB):
        x_prompt = prompt_all[m]
        if m > 0:
            x_prompt, saved[-1][-1] = pin(x_prompt, saved[-1][-1])
        if square and m == 1:
            x_prompt, *rest_boths = pin(x_prompt, *rest_boths)
            rest_fars = spread_two(rest_boths)
        x_cont = jnp.concatenate([cont_in[m], cont_mate[m]], axis=0)
        plan = plan_of(m)
        o, lse, query, kv = attend_forward(plan, spot, x_prompt, x_cont, w_heads, vec_a, TQ, prow)
        if square and m == 1:
            lse, *rest_fars = pin(lse, *rest_fars)
        outs.append(send_home(o[:mine], o[mine:]))
        saved.append([x_prompt, x_cont, kv, query, plan, o, lse])

    if square:
        pieces, piece_rows = join_rest(rest_boths, rest_fars)

    groups, block_share = (4, share) if square else (1, 8)
    places = jnp.stack([core] + [jnp.asarray(row, jnp.int32) for row in piece_rows]).astype(jnp.int32)
    (
        prompt_out,
        cont_out,
        prompt_dh,
        cont_dh,
        d_mine,
        d_mate,
        g_vec,
        g_fc_bias,
        g_rest,
        g_more,
    ) = feed_forward(
        cont_len[:, 0, :],
        places,
        prompt_in,
        cont_in,
        prompt_cot,
        cont_cot,
        [part for parts in outs for part in parts],
        vec_b,
        b_fc,
        pieces,
        groups,
        block_share,
    )
    returned = [send_back(d_mine[m], d_mate[m]) for m in range(MB)]
    g_rest, g_more, *returned[0] = pin(g_rest, g_more, *returned[0])

    def along_fsdp(value):
        if square:
            return lax.psum_scatter(value, "fsdp", scatter_dimension=0, tiled=True)
        value = value.reshape(D, value.shape[2])
        return lax.psum_scatter(value, ALL, scatter_dimension=0, tiled=True)

    g_rest, g_more = along_fsdp(g_rest), along_fsdp(g_more)

    totals = None
    tables = []
    conts_back = []
    for m in range(MB):
        x_prompt, x_cont, kv, query, plan, o, lse = saved[m]
        if m > 0:
            tables[-1], *returned[m] = pin(tables[-1], *returned[m])
            tables[-1] = lax.psum_scatter(tables[-1], "fsdp", scatter_dimension=0, tiled=True)
        if m > 1:
            g_more, *returned[m] = pin(g_more, *returned[m])
        if m == 1:
            g_rest, *returned[m] = pin(g_rest, *returned[m])
        do = returned[m]
        table, table_cont, *totals = attend_backward(
            plan, spot, x_prompt, x_cont, kv, query, do, o, lse, w_heads, vec_a, totals, TQ, prow
        )
        tables.append(table)
        conts_back.append(
            table_cont[:crow].astype(F32) + swap(table_cont[crow:]).astype(F32)
        )
    if MB > 1:
        tables = pin(*tables)
    tables[-1] = lax.psum_scatter(tables[-1], "fsdp", scatter_dimension=0, tiled=True)
    g_heads, g_first, g_bias = totals

    def spread(value):
        return jnp.where((jnp.arange(2) == core)[:, None], value[None, :], 0.0).reshape(D)

    sums = jnp.stack(
        [
            g_first[0],
            g_first[1],
            spread(g_bias[0, :HALF]),
            spread(g_bias[0, 2 * HALF :]),
            g_vec[0],
            g_vec[1],
            g_vec[2],
            g_vec[3],
        ]
        + [g_fc_bias[0, i * D : (i + 1) * D] for i in range(wide)],
        axis=0,
    )
    sums_high = sums.astype(BF)
    sums_low = (sums - sums_high.astype(F32)).astype(BF)
    count = sums.shape[0]
    sums = jnp.concatenate(
        [sums_high, sums_low, jnp.zeros((SMALL_COLS - 2 * count, D), BF)], axis=0
    ).T
    late = jnp.concatenate([g_heads.astype(BF), sums], axis=1)
    for index, step in enumerate(reduce_steps()):
        late = step(late)
        if square and index == 1:
            late, g_rest, g_more = pin(late, g_rest, g_more)
    early = jnp.concatenate([g_rest, g_more], axis=-1)
    for step in square_steps(core) if square else ():
        early = step(early)
    late_own, late_other = own_rows(late, core)
    sums = late_own[:, HEAD_COLS:].astype(F32) + late_other[:, HEAD_COLS:].astype(F32)
    sums = (sums[:, :count] + sums[:, count : 2 * count]).T

    def by_core(own, other):
        return jnp.where(core == 0, own, other), jnp.where(core == 0, other, own)

    late = jnp.stack(by_core(late_own[:, :HEAD_COLS], late_other[:, :HEAD_COLS]), axis=1)
    late = late.reshape(share, 2, 3, HALF).transpose(0, 2, 1, 3).reshape(share, 3 * D)
    early = early.astype(F32)
    g_fc = early[:, D : D + FF].reshape(share, wide, devices, share)
    g_fc = g_fc.transpose(0, 2, 1, 3).reshape(share, FF)
    g_out = early[:, D + FF :].reshape(share, wide, D).transpose(1, 0, 2).reshape(share * wide, D)

    def input_grad(source, slope, change):
        source = source.astype(F32)
        center = source - jnp.mean(source, axis=-1, keepdims=True)
        rate = lax.rsqrt(jnp.mean(center * center, axis=-1, keepdims=True) + EPSILON)
        hat = center * rate
        e1 = change * gain_a
        change = e1 - jnp.mean(e1, axis=-1, keepdims=True)
        change = change - hat * jnp.mean(e1 * hat, axis=-1, keepdims=True)
        return (slope.astype(F32) + rate * change).astype(BF)

    prompt_grad = input_grads(prompt_in, prompt_dh, vec_a, tables, TQ)
    cont_grad = jnp.stack([input_grad(cont_in[m], cont_dh[m], conts_back[m]) for m in range(MB)])
    return (
        prompt_out,
        cont_out,
        prompt_grad,
        cont_grad,
        sums[0],
        sums[1],
        late.astype(F32),
        sums[2:4],
        early[:, :D],
        sums[4],
        sums[5],
        sums[6],
        g_fc,
        sums[8:].reshape(share * wide),
        g_out,
        sums[7],
    )


def solution(mesh):
    rows = P(None, ALL, None)
    conts = P(None, "grp", "fsdp")
    vector = P(ALL)
    matrix = P(ALL, None)
    pair = P(None, ALL)
    params = (
        vector,
        vector,
        matrix,
        pair,
        matrix,
        vector,
        vector,
        vector,
        matrix,
        vector,
        matrix,
        vector,
    )
    return jax.shard_map(
        body,
        mesh=mesh,
        in_specs=(rows, rows, rows, rows, conts, conts) + params,
        out_specs=(rows, rows, rows, rows) + params,
        check_vma=False,
    )
```

```python
import functools
import math

import jax
import jax.numpy as jnp
from jax import lax
from jax.experimental import pallas as pl
from jax.experimental.pallas import tpu as pltpu
from jax.sharding import PartitionSpec as P

D = 768
HEADS = 12
HEAD_DIM = 64
FF = 3072
MB = 3
NPR = 2
PLEN = 2048
ALL = ("grp", "fsdp")

EPSILON = 1e-05
MASKED = -1e30
BF = jnp.bfloat16
F32 = jnp.float32

HALF = D // 2
NH = HEADS // 2
PAIRS = NH // 2
TK = 512
LOG2E = math.log2(math.e)
QSCALE = HEAD_DIM ** (-0.5) * LOG2E


def dot_nt(a, b):
    return lax.dot_general(a, b, (((1,), (1,)), ((), ())), preferred_element_type=F32)


def dot_nn(a, b):
    return lax.dot_general(a, b, (((1,), (0,)), ((), ())), preferred_element_type=F32)


def half_masks(rows):
    lane = lax.broadcasted_iota(jnp.int32, (rows, 128), 1)
    return (lane < HEAD_DIM, lane >= HEAD_DIM)


def normal_form(value):
    center = value - jnp.mean(value, axis=1, keepdims=True)
    return center * lax.rsqrt(jnp.mean(center * center, axis=1, keepdims=True) + EPSILON)


def flip(value):
    return jnp.transpose(value.astype(F32)).astype(BF)


def stream_rows(xp_hbm, xc_hbm, rows, sems, visit):
    size = rows.shape[1]
    count = xp_hbm.shape[0] // size
    crow = xc_hbm.shape[0] // 2
    part = min(size, crow)

    def fetch(index, slot):
        row = pl.multiple_of(index * size, size)
        return pltpu.make_async_copy(xp_hbm.at[pl.ds(row, size)], rows.at[slot], sems.at[slot])

    fetch(0, 0).start()

    def one(index, carry):
        slot = lax.rem(index, 2)

        @pl.when(index + 1 < count)
        def _():
            fetch(index + 1, 1 - slot).start()

        fetch(index, slot).wait()
        visit(pl.multiple_of(index * size, size), size, rows[slot].astype(F32))
        return carry

    lax.fori_loop(0, count, one, 0)
    for index in range(2 * crow // part):
        copy = pltpu.make_async_copy(
            xc_hbm.at[pl.ds(index * part, part)], rows.at[0, pl.ds(0, part)], sems.at[0]
        )
        copy.start()
        copy.wait()
        visit(count * size + index * part, part, rows[0, :part].astype(F32))


def attend_forward_kernel(
    info,
    spot,
    xp_hbm,
    xc_hbm,
    xqp_ref,
    xqc_ref,
    w_ref,
    vec_ref,
    o_ref,
    lse_ref,
    q_ref,
    kv_hbm,
    kv,
    rows,
    qm,
    s_ref,
    mx,
    acc,
    sems,
    done,
):
    block = pl.program_id(0)
    gain, shift, bias_kv, bias_q = (vec_ref[i : i + 1, :] for i in range(4))

    def store(row, size):
        index = row // rows.shape[1]
        if isinstance(row, int):
            index = xp_hbm.shape[0] // rows.shape[1] + (row - xp_hbm.shape[0]) // size
        return pltpu.make_async_copy(
            kv.at[pl.ds(row, size)], kv_hbm.at[pl.ds(row, size)], done.at[index]
        )

    @pl.when(block == 0)
    def _():
        def visit(row, size, x):
            normed = (normal_form(x) * gain + shift).astype(BF)
            kv[pl.ds(row, size), :] = (dot_nn(normed, w_ref[:, HALF:]) + bias_kv).astype(BF)
            store(row, size).start()

        stream_rows(xp_hbm, xc_hbm, rows, sems, visit)

    TQ = q_ref.shape[0]
    x = jnp.where(spot[block, 0] > 0, xqc_ref[...].astype(F32), xqp_ref[...].astype(F32))
    normed = (normal_form(x) * gain + shift).astype(BF)
    query = ((dot_nn(normed, w_ref[:, :HALF]) + bias_q[:, :HALF]) * QSCALE).astype(BF)
    q_ref[...] = query
    base = pl.multiple_of(info[block, 0], TQ)
    tiles = info[block, 1]
    extra = info[block, 2]
    extra_row = pl.multiple_of(info[block, 3], TQ)
    diag = pl.multiple_of(info[block, 4], TQ)
    low, high = half_masks(TQ)
    zero = jnp.zeros((TQ, 128), BF)
    for pair in range(PAIRS):
        part = query[:, pair * 128 : (pair + 1) * 128]
        qm[2 * pair] = jnp.where(low, part, zero)
        qm[2 * pair + 1] = jnp.where(high, part, zero)

    def score(pair, row, size, column, first, masked):
        keys = kv[pl.ds(row, size), pair * 128 : (pair + 1) * 128]
        for side in (0, 1):
            raw = dot_nt(qm[2 * pair + side], keys)
            if masked:
                across = lax.broadcasted_iota(jnp.int32, (TQ, size), 1)
                down = lax.broadcasted_iota(jnp.int32, (TQ, size), 0)
                raw = jnp.where(across <= down, raw, MASKED)
            slot = 2 * (pair % 2) + side
            s_ref[slot, :, pl.ds(column, size)] = raw
            top = raw[:, :128]
            for piece in range(1, size // 128):
                top = jnp.maximum(top, raw[:, piece * 128 : (piece + 1) * 128])
            if not first:
                top = jnp.maximum(top, mx[slot])
            mx[slot] = top

    def settle(pair):
        for side in (0, 1):
            slot = 2 * (pair % 2) + side
            top = jnp.max(mx[slot], axis=1, keepdims=True)
            mx[slot] = jnp.broadcast_to(top, (TQ, 128))

    def blend(pair, row, size, column, first):
        vals = kv[pl.ds(row, size), HALF + pair * 128 : HALF + (pair + 1) * 128]
        wide = jnp.concatenate([vals, jnp.ones((size, 128), BF)], axis=1)
        for side in (0, 1):
            slot = 2 * (pair % 2) + side
            top = jnp.concatenate([mx[slot]] * (size // 128), axis=1)
            power = jnp.exp2(s_ref[slot, :, pl.ds(column, size)] - top).astype(BF)
            new = dot_nn(power, wide)
            if first:
                acc[side] = new
            else:
                acc[side] += new

    def sweep(step):
        step(diag, TQ, 0, True)

        def some(index, carry):
            row = pl.multiple_of(extra_row + index * TQ, TQ)
            step(row, TQ, pl.multiple_of(TQ + index * TQ, TQ), False)
            return carry

        lax.fori_loop(0, extra, some, 0)

        def one(index, carry):
            row = pl.multiple_of(base + index * TK, TQ)
            step(row, TK, pl.multiple_of(TK + index * TK, TQ), False)
            return carry

        lax.fori_loop(0, tiles, one, 0)

    sweep(lambda row, size, column, first: score(0, row, size, column, first, first))
    for pair in range(PAIRS):
        settle(pair)

        def both(row, size, column, first):
            if pair + 1 < PAIRS:
                score(pair + 1, row, size, column, first, first)
            blend(pair, row, size, column, first)

        sweep(both)
        sides = []
        for side in (0, 1):
            total = acc[side][:, 128:]
            sides.append(acc[side][:, :128] / total)
            tall = jnp.transpose(mx[2 * (pair % 2) + side] + jnp.log2(total))
            lse_ref[0, 2 * pair + side] = tall[0]
        o_ref[:, pair * 128 : (pair + 1) * 128] = jnp.where(low, sides[0], sides[1]).astype(BF)

    @pl.when(block == pl.num_programs(0) - 1)
    def _():
        size = rows.shape[1]
        part = min(size, xc_hbm.shape[0] // 2)
        for row in range(0, xp_hbm.shape[0], size):
            pltpu.make_async_copy(
                kv.at[pl.ds(row, size)], kv_hbm.at[pl.ds(row, size)], done.at[row // size]
            ).wait()
        for row in range(xp_hbm.shape[0], kv.shape[0], part):
            store(row, part).wait()


def query_specs(TQ):
    prompts = pl.BlockSpec((TQ, D), lambda i, s, t: (t[i, 1], 0))
    conts = pl.BlockSpec((TQ, D), lambda i, s, t: (t[i, 2], 0))
    return prompts, conts


def attend_forward(info, spot, xp, xc, weight, vec, TQ, size):
    blocks = info.shape[0]
    count = blocks * TQ
    keys = xp.shape[0] + xc.shape[0]
    tiles = xp.shape[0] // size + xc.shape[0] // min(size, xc.shape[0] // 2)
    whole = pl.BlockSpec(memory_space=pl.ANY)
    heads = pl.BlockSpec((TQ, HALF), lambda i, s, t: (i, 0))
    shape = jax.ShapeDtypeStruct
    return pl.pallas_call(
        attend_forward_kernel,
        grid_spec=pltpu.PrefetchScalarGridSpec(
            num_scalar_prefetch=2,
            grid=(blocks,),
            in_specs=[
                whole,
                whole,
                *query_specs(TQ),
                pl.BlockSpec(weight.shape, lambda i, s, t: (0, 0)),
                pl.BlockSpec(vec.shape, lambda i, s, t: (0, 0)),
            ],
            out_specs=[heads, pl.BlockSpec((1, 8, TQ), lambda i, s, t: (i, 0, 0)), heads, whole],
            scratch_shapes=[
                pltpu.VMEM((keys, D), BF),
                pltpu.VMEM((2, size, D), BF),
                pltpu.VMEM((NH, TQ, 128), BF),
                pltpu.VMEM((4, TQ, PLEN + TK), F32),
                pltpu.VMEM((4, TQ, 128), F32),
                pltpu.VMEM((2, TQ, 256), F32),
                pltpu.SemaphoreType.DMA((2,)),
                pltpu.SemaphoreType.DMA((tiles,)),
            ],
        ),
        out_shape=(
            shape((count, HALF), BF),
            shape((blocks, 8, TQ), F32),
            shape((count, HALF), BF),
            shape((keys, D), BF),
        ),
        compiler_params=pltpu.CompilerParams(
            dimension_semantics=("arbitrary",), vmem_limit_bytes=56 << 20
        ),
        cost_estimate=pl.CostEstimate(
            flops=int(4 * count * PLEN * HALF * 4) + 2 * D * D * keys,
            bytes_accessed=20 << 20,
            transcendentals=0,
        ),
        name="attend_forward",
    )(info, spot, xp, xc, xp, xc, weight, vec)


def attend_backward_kernel(
    chained,
    bounds,
    info,
    spot,
    xp_hbm,
    xc_hbm,
    kv_hbm,
    xqp_ref,
    xqc_ref,
    q_ref,
    o_ref,
    lse_ref,
    w_ref,
    vec_ref,
    *refs,
):
    parts, refs = refs[:4], refs[4:]
    if chained:
        old_w, old_vec, old_bias = refs[:3]
        refs = refs[3:]
    (
        tp_hbm,
        tc_hbm,
        gw_hbm,
        gvec_ref,
        gbias_ref,
        kv,
        kt,
        dkv,
        gw,
        qd,
        rows,
        table,
        qm,
        dom,
        dqt,
        drow,
        do_ref,
        sems,
        done,
    ) = refs
    block = pl.program_id(0)
    TQ = q_ref.shape[0]
    keys_all = kv.shape[0]
    gain, shift = (vec_ref[i : i + 1, :] for i in range(2))
    for part, (begin, end) in zip(parts, bounds):

        @pl.when((block >= begin) & (block < end))
        def _():
            do_ref[...] = part[...]


    @pl.when(block == 0)
    def _():
        load = pltpu.make_async_copy(kv_hbm, kv, sems.at[0])
        load.start()
        if chained:
            more = pltpu.make_async_copy(old_w, gw, sems.at[1])
            more.start()
            gvec_ref[...] = old_vec[...]
            gbias_ref[...] = old_bias[...]
        else:
            gw[...] = jnp.zeros_like(gw)
            gvec_ref[...] = jnp.zeros_like(gvec_ref)
            gbias_ref[...] = jnp.zeros_like(gbias_ref)

        def clear(index, carry):
            dkv[pl.ds(pl.multiple_of(index * TQ, TQ), TQ), :] = jnp.zeros((TQ, D), F32)
            return carry

        lax.fori_loop(0, keys_all // TQ, clear, 0)
        load.wait()

        def prepare(index, carry):
            row = pl.multiple_of(index * TQ, TQ)
            kt[:, pl.ds(row, TQ)] = flip(kv[pl.ds(row, TQ), :HALF])
            return carry

        lax.fori_loop(0, keys_all // TQ, prepare, 0)
        if chained:
            more.wait()

    base = pl.multiple_of(info[block, 0], TQ)
    tiles = info[block, 1]
    extra = info[block, 2]
    extra_row = pl.multiple_of(info[block, 3], TQ)
    diag = pl.multiple_of(info[block, 4], TQ)
    low, high = half_masks(TQ)
    zero = jnp.zeros((TQ, 128), BF)
    for pair in range(PAIRS):
        lanes = slice(pair * 128, (pair + 1) * 128)
        part = q_ref[:, lanes]
        qm[2 * pair] = jnp.where(low, part, zero)
        qm[2 * pair + 1] = jnp.where(high, part, zero)
        part = do_ref[:, lanes]
        dom[2 * pair] = jnp.where(low, part, zero)
        dom[2 * pair + 1] = jnp.where(high, part, zero)
        product = jnp.transpose(part.astype(F32) * o_ref[:, lanes].astype(F32))
        drow[2 * pair] = jnp.sum(product[:HEAD_DIM], axis=0)
        drow[2 * pair + 1] = jnp.sum(product[HEAD_DIM:], axis=0)

    def step(row, size, first):
        for pair in range(PAIRS):
            lanes = slice(pair * 128, (pair + 1) * 128)
            more = slice(HALF + pair * 128, HALF + (pair + 1) * 128)
            keys = kv[pl.ds(row, size), lanes]
            vals = kv[pl.ds(row, size), more]
            dk = None
            dv = None
            for side in (0, 1):
                head = 2 * pair + side
                raw = dot_nt(keys, qm[head])
                if first:
                    across = lax.broadcasted_iota(jnp.int32, (size, TQ), 1)
                    down = lax.broadcasted_iota(jnp.int32, (size, TQ), 0)
                    raw = jnp.where(down <= across, raw, MASKED)
                probs = jnp.exp2(raw - lse_ref[0, head : head + 1, :])
                grad = dot_nt(vals, dom[head])
                slope = (probs * (grad - drow[head : head + 1, :])).astype(BF)
                probs = probs.astype(BF)
                part_v = dot_nn(probs, dom[head])
                part_k = dot_nn(slope, qm[head])
                dv = part_v if dv is None else dv + part_v
                dk = part_k if dk is None else dk + part_k
                spot = slice(head * HEAD_DIM, (head + 1) * HEAD_DIM)
                new = dot_nn(kt[spot, pl.ds(row, size)], slope)
                if first:
                    dqt[spot, :] = new
                else:
                    dqt[spot, :] += new
            dkv[pl.ds(row, size), lanes] += dk
            dkv[pl.ds(row, size), more] += dv

    step(diag, TQ, True)

    def some(index, carry):
        step(pl.multiple_of(extra_row + index * TQ, TQ), TQ, False)
        return carry

    lax.fori_loop(0, extra, some, 0)

    def one(index, carry):
        step(pl.multiple_of(base + index * TK, TQ), TK, False)
        return carry

    lax.fori_loop(0, tiles, one, 0)
    x = jnp.where(spot[block, 0] > 0, xqc_ref[...].astype(F32), xqp_ref[...].astype(F32))
    dq_full = jnp.transpose(dqt[...]) * HEAD_DIM ** (-0.5)
    dq = dq_full.astype(BF)
    gw[:, :HALF] += dot_nn(flip(normal_form(x) * gain + shift), dq)
    gbias_ref[0:1, :HALF] += jnp.sum(dq_full, axis=0, keepdims=True)
    qd[pl.ds(pl.multiple_of(block * TQ, TQ), TQ), :] = dot_nt(dq, w_ref[:, :HALF])

    @pl.when(block == pl.num_programs(0) - 1)
    def _():
        prompt_rows = xp_hbm.shape[0]
        size = rows.shape[1]
        crow = xc_hbm.shape[0] // 2
        part = min(size, crow)
        count = prompt_rows // size
        own, mate = spot[0, 3], spot[0, 4]

        def send(slot, row):
            return pltpu.make_async_copy(
                table.at[slot], tp_hbm.at[pl.ds(row, size)], done.at[slot]
            )

        def visit(row, size_now, x):
            hat = normal_form(x)
            grad_k = dkv[pl.ds(row, size_now), :HALF] * (1.0 / LOG2E)
            grad_v = dkv[pl.ds(row, size_now), HALF:]
            grad = jnp.concatenate([grad_k.astype(BF), grad_v.astype(BF)], axis=1)
            gw[:, HALF:] += dot_nn(flip(hat * gain + shift), grad)
            gbias_ref[0:1, HALF : 2 * HALF] += jnp.sum(grad_k, axis=0, keepdims=True)
            gbias_ref[0:1, 2 * HALF :] += jnp.sum(grad_v, axis=0, keepdims=True)
            change = dot_nt(grad, w_ref[:, HALF:])
            if isinstance(row, int):
                first = row - prompt_rows
                which = first // crow
                begin = which * (size + crow) + size + first - which * crow
                change = change + qd[begin : begin + size_now, :]
            else:
                index = row // size
                begin = jnp.where(index == mate, size + crow, 0)
                begin = pl.multiple_of(begin, math.gcd(size, crow))
                weight = jnp.where((index == own) | (index == mate), 1.0, 0.0)
                change = change + weight * qd[pl.ds(begin, size_now), :]
            gvec_ref[0:1, :] += jnp.sum(change * hat, axis=0, keepdims=True)
            gvec_ref[1:2, :] += jnp.sum(change, axis=0, keepdims=True)
            change = change.astype(BF)
            if isinstance(row, int):
                slot = (first // part) % 2
                if first // part >= 2:
                    pltpu.make_async_copy(
                        table.at[slot, pl.ds(0, part)],
                        tc_hbm.at[pl.ds(first - 2 * part, part)],
                        done.at[slot],
                    ).wait()
                else:
                    send(slot, prompt_rows - (2 - slot) * size).wait()
                table[slot, :part] = change
                pltpu.make_async_copy(
                    table.at[slot, pl.ds(0, part)],
                    tc_hbm.at[pl.ds(first, part)],
                    done.at[slot],
                ).start()
            else:
                slot = lax.rem(index, 2)

                @pl.when(index >= 2)
                def _():
                    send(slot, pl.multiple_of(row - 2 * size, size)).wait()

                table[slot] = change
                send(slot, row).start()

        stream_rows(xp_hbm, xc_hbm, rows, sems, visit)
        last = 2 * crow // part
        for index in range(last - 2, last):
            pltpu.make_async_copy(
                table.at[index % 2, pl.ds(0, part)],
                tc_hbm.at[pl.ds(index * part, part)],
                done.at[index % 2],
            ).wait()
        out = pltpu.make_async_copy(gw, gw_hbm, sems.at[0])
        out.start()
        out.wait()


def attend_backward(info, spot, xp, xc, kv, q, do, o, lse, weight, vec, totals, TQ, size):
    blocks = info.shape[0]
    count = blocks * TQ
    keys = kv.shape[0]
    whole = pl.BlockSpec(memory_space=pl.ANY)
    heads = pl.BlockSpec((TQ, HALF), lambda i, s, t: (i, 0))
    shape = jax.ShapeDtypeStruct
    fixed = [
        pl.BlockSpec((8, D), lambda i, s, t: (0, 0)),
        pl.BlockSpec((8, 3 * HALF), lambda i, s, t: (0, 0)),
    ]
    extra = () if totals is None else tuple(totals)
    bounds, parts_in, begin = [], [], 0
    for part in do:
        end = begin + part.shape[0] // TQ
        bounds.append((begin, end))
        parts_in.append(
            pl.BlockSpec(
                (TQ, HALF),
                lambda i, s, t, begin=begin, end=end: (jnp.clip(i - begin, 0, end - begin - 1), 0),
            )
        )
        begin = end
    return pl.pallas_call(
        functools.partial(attend_backward_kernel, totals is not None, bounds),
        grid_spec=pltpu.PrefetchScalarGridSpec(
            num_scalar_prefetch=2,
            grid=(blocks,),
            in_specs=[
                whole,
                whole,
                whole,
                *query_specs(TQ),
                heads,
                heads,
                pl.BlockSpec((1, 8, TQ), lambda i, s, t: (i, 0, 0)),
                pl.BlockSpec(weight.shape, lambda i, s, t: (0, 0)),
                pl.BlockSpec(vec.shape, lambda i, s, t: (0, 0)),
                *parts_in,
            ]
            + ([whole] + fixed if extra else []),
            out_specs=[whole, whole, whole] + fixed,
            scratch_shapes=[
                pltpu.VMEM((keys, D), BF),
                pltpu.VMEM((HALF, keys), BF),
                pltpu.VMEM((keys, D), F32),
                pltpu.VMEM((D, 3 * HALF), F32),
                pltpu.VMEM((count, D), F32),
                pltpu.VMEM((2, size, D), BF),
                pltpu.VMEM((2, size, D), BF),
                pltpu.VMEM((NH, TQ, 128), BF),
                pltpu.VMEM((NH, TQ, 128), BF),
                pltpu.VMEM((HALF, TQ), F32),
                pltpu.VMEM((8, TQ), F32),
                pltpu.VMEM((TQ, HALF), BF),
                pltpu.SemaphoreType.DMA((2,)),
                pltpu.SemaphoreType.DMA((2,)),
            ],
        ),
        out_shape=(
            shape(xp.shape, BF),
            shape(xc.shape, BF),
            shape((D, 3 * HALF), F32),
            shape((8, D), F32),
            shape((8, 3 * HALF), F32),
        ),
        compiler_params=pltpu.CompilerParams(
            dimension_semantics=("arbitrary",), vmem_limit_bytes=62 << 20
        ),
        cost_estimate=pl.CostEstimate(
            flops=int(10 * count * PLEN * HALF * 4) + 4 * D * D * keys,
            bytes_accessed=30 << 20,
            transcendentals=0,
        ),
        name="attend_backward",
    )(info, spot, xp, xc, kv, xp, xc, q, o, lse, weight, vec, *do, *extra)


def gelu_parts(value):
    rate = math.sqrt(2.0 / math.pi)
    square = value * value
    half = 0.5 + 0.5 * jnp.tanh(value * (rate + (rate * 0.044715) * square))
    slope = half + value * (half * (1.0 - half)) * (2.0 * rate + (6.0 * rate * 0.044715) * square)
    return value * half, slope


def feed_forward_kernel(
    prompt_parts,
    clen,
    count,
    groups,
    lens,
    places,
    xp_ref,
    xc_ref,
    gp_ref,
    gc_ref,
    vec_ref,
    bfc_ref,
    *refs,
):
    heads, refs = refs[: 4 * MB], refs[4 * MB :]
    pieces = refs[:count]
    (
        fp_ref,
        fc_ref,
        hp_ref,
        hc_ref,
        dmine_ref,
        dmate_ref,
        gvec_ref,
        gbfc_ref,
        grads_hbm,
        more_hbm,
        wp,
        wfc,
        wout,
        ap,
        afc,
        aout,
        stage,
        mine_ref,
        mate_ref,
        sems,
    ) = refs[count:]
    core = places[0]
    batch = pl.program_id(0)
    part = pl.program_id(1)
    tile = mine_ref.shape[0]
    is_cont = part >= prompt_parts
    begin = (batch == 0) & (part == 0)

    @pl.when(begin)
    def _():
        def loads_of(first_half):
            moves = []
            for index, piece in enumerate(pieces):
                size = piece.shape[1]
                half = None
                if first_half is not None:
                    half = first_half if index < count // 2 else 1 - first_half
                split = (D + 2 * FF) // 2 - D
                spans = [(wp, 0, 0, D), (wfc, 0, D, FF)]
                spans += [(wout, block * D, D + FF + block * D, D) for block in range(FF // D)]
                if half == 0:
                    spans = [(wp, 0, 0, D), (wfc, (0, 0), D, split)]
                elif half == 1:
                    spans = [(wfc, (0, split), 0, FF - split)]
                    spans += [
                        (wout, block * D, FF - split + block * D, D) for block in range(FF // D)
                    ]
                for inner in range(piece.shape[0]):
                    row = pl.multiple_of(places[1 + index * piece.shape[0] + inner], 16)
                    turned = pl.multiple_of(lax.rem(row + core * HALF, D), 16)
                    for target, offset, column, width in spans:
                        source = piece.at[inner, :, pl.ds(column, width)]
                        if target is wp:
                            view = wp.at[pl.ds(turned, size), :]
                        elif target is wfc:
                            begin = offset[1] if isinstance(offset, tuple) else 0
                            view = wfc.at[pl.ds(row, size), pl.ds(begin, width)]
                        else:
                            view = wout.at[pl.ds(offset + row, size), :]
                        moves.append((source, view))
            return [
                pltpu.make_async_copy(source, view, sems.at[index])
                for index, (source, view) in enumerate(moves)
            ]

        def load_all(first_half):
            loads = loads_of(first_half)
            for load in loads:
                load.start()
            for load in loads:
                load.wait()

        ap[...] = jnp.zeros_like(ap)
        gvec_ref[...] = jnp.zeros_like(gvec_ref)
        gbfc_ref[...] = jnp.zeros_like(gbfc_ref)

        def clear(index, carry):
            row = pl.multiple_of(index * 64, 64)
            afc[pl.ds(row, 64), :] = jnp.zeros((64, FF), F32)
            aout[pl.ds(row, 64), :] = jnp.zeros((64, FF), F32)
            return carry

        lax.fori_loop(0, D // 64, clear, 0)
        if groups == 1:
            load_all(None)
        else:

            @pl.when(core == 0)
            def _():
                load_all(0)

            @pl.when(core != 0)
            def _():
                load_all(1)

    b_proj = vec_ref[0:1, :]
    gain = vec_ref[1:2, :]
    shift = vec_ref[2:3, :]
    b_out = vec_ref[3:4, :]
    x = jnp.where(is_cont, xc_ref[0].astype(F32), xp_ref[0].astype(F32))
    gy = jnp.where(is_cont, gc_ref[0].astype(F32), gp_ref[0].astype(F32))
    start = jnp.maximum(part - prompt_parts, 0) * tile
    length = lens[batch, start // clen]
    place = lax.broadcasted_iota(jnp.int32, (tile, 1), 0) + start % clen
    valid = jnp.where(jnp.logical_not(is_cont) | (place < length), 1.0, 0.0)

    for m in range(MB):
        for kind, wanted in enumerate((jnp.logical_not(is_cont), is_cont)):

            @pl.when((batch == m) & wanted)
            def _():
                mine_ref[...] = heads[4 * m + kind][...]
                mate_ref[...] = heads[4 * m + 2 + kind][...]

    mine = mine_ref[...]
    mate = mate_ref[...]
    h = x + valid * (dot_nn(mine, wp[:HALF, :]) + dot_nn(mate, wp[HALF:, :]) + b_proj)
    center = h - jnp.mean(h, axis=1, keepdims=True)
    rate = lax.rsqrt(jnp.mean(center * center, axis=1, keepdims=True) + EPSILON)
    hat = center * rate
    second = (hat * gain + shift).astype(BF)
    dz_full = valid * gy
    dz = dz_full.astype(BF)
    second_t = flip(second)
    dz_t = flip(dz)
    result = None
    back = None
    for index in range(FF // D):
        cols = slice(index * D, (index + 1) * D)
        inner = dot_nn(second, wfc[:, cols]) + bfc_ref[:, cols]
        act, slope = gelu_parts(inner)
        act = act.astype(BF)
        du_full = dot_nt(dz, wout[cols, :]) * slope
        du = du_full.astype(BF)
        gbfc_ref[0:1, cols] += jnp.sum(du_full, axis=0, keepdims=True)
        new = dot_nn(act, wout[cols, :])
        result = new if result is None else result + new
        new = dot_nt(du, wfc[:, cols])
        back = new if back is None else back + new
        aout[:, cols] += dot_nn(dz_t, act)
        afc[:, cols] += dot_nn(second_t, du)
    final = (h + valid * (result + b_out)).astype(BF)
    e2 = back * gain
    dh = gy + rate * (
        e2
        - jnp.mean(e2, axis=1, keepdims=True)
        - hat * jnp.mean(e2 * hat, axis=1, keepdims=True)
    )
    dy_full = valid * dh
    dy = dy_full.astype(BF)
    gvec_ref[0:1, :] += jnp.sum(dy_full, axis=0, keepdims=True)
    gvec_ref[1:2, :] += jnp.sum(back * hat, axis=0, keepdims=True)
    gvec_ref[2:3, :] += jnp.sum(back, axis=0, keepdims=True)
    gvec_ref[3:4, :] += jnp.sum(dz.astype(F32), axis=0, keepdims=True)
    ap[:HALF, :] += dot_nn(flip(mine), dy)
    ap[HALF:, :] += dot_nn(flip(mate), dy)
    dmine_ref[0] = dot_nt(dy, wp[:HALF, :]).astype(BF)
    dmate_ref[0] = dot_nt(dy, wp[HALF:, :]).astype(BF)
    dh = dh.astype(BF)

    @pl.when(jnp.logical_not(is_cont))
    def _():
        fp_ref[0] = final
        hp_ref[0] = dh

    @pl.when(is_cont)
    def _():
        fc_ref[0] = final
        hc_ref[0] = dh

    @pl.when((batch == pl.num_programs(0) - 1) & (part == pl.num_programs(1) - 1))
    def _():
        blocks, share = stage.shape[1], stage.shape[2]
        sends = []

        def send(column, fetch):
            slot = len(sends) % 2
            if len(sends) >= 2:
                sends[-2].wait()
            for block in range(blocks):
                stage[slot, block] = fetch(block).astype(BF)
            width = grads_hbm.shape[2]
            if column < width:
                target = grads_hbm.at[:, :, pl.ds(column, D)]
            else:
                target = more_hbm.at[:, :, pl.ds(column - width, D)]
            sends.append(pltpu.make_async_copy(stage.at[slot], target, sems.at[slot]))
            sends[-1].start()

        def first_row(block):
            return (block % groups * (blocks // groups) + block // groups) * share

        def proj_rows(block):
            row = lax.rem(first_row(block) + core * HALF, D)
            return ap[pl.ds(pl.multiple_of(row, math.gcd(share, HALF)), share), :]

        send(0, proj_rows)
        for part_of in range(FF // D):
            cols = slice(part_of * D, (part_of + 1) * D)
            send(D + part_of * D, lambda block: afc[first_row(block) : first_row(block) + share, cols])
        for part_of in range(FF // D):
            cols = slice(part_of * D, (part_of + 1) * D)
            ap[...] = jnp.transpose(aout[:, cols])
            send(
                D + FF + part_of * D,
                lambda block: ap[first_row(block) : first_row(block) + share, :],
            )
        for copy in sends[-2:]:
            copy.wait()


def feed_forward(lens, places, prompt_in, cont_in, prompt_cot, cont_cot, heads_in, vec, bfc, pieces, groups, share):
    prow = prompt_in.shape[1]
    crow = cont_in.shape[1]
    clen = crow // lens.shape[1]
    tile = min(256, prow, clen)
    prompt_parts = prow // tile
    parts = prompt_parts + crow // tile
    prompts = pl.BlockSpec((1, tile, D), lambda m, i, s, t: (m, jnp.minimum(i, prompt_parts - 1), 0))
    conts = pl.BlockSpec((1, tile, D), lambda m, i, s, t: (m, jnp.maximum(i - prompt_parts, 0), 0))
    heads = pl.BlockSpec((1, tile, HALF), lambda m, i, s, t: (m, i, 0))
    whole = pl.BlockSpec(memory_space=pl.ANY)
    def part_spec(own, first, count):
        def place(m, i, s, t):
            inside = jnp.clip(i - first, 0, count - 1)
            return (jnp.where(m == own, inside, jnp.where(m < own, 0, count - 1)), 0)

        return pl.BlockSpec((tile, HALF), place)

    parts_in = []
    for own in range(MB):
        parts_in += [part_spec(own, 0, prompt_parts), part_spec(own, prompt_parts, crow // tile)] * 2
    fixed = pl.BlockSpec((8, D), lambda m, i, s, t: (0, 0))
    long = pl.BlockSpec((8, FF), lambda m, i, s, t: (0, 0))
    shape = jax.ShapeDtypeStruct
    rows = MB * (prow + crow)
    return pl.pallas_call(
        functools.partial(feed_forward_kernel, prompt_parts, clen, len(pieces), groups),
        grid_spec=pltpu.PrefetchScalarGridSpec(
            num_scalar_prefetch=2,
            grid=(MB, parts),
            in_specs=[
                prompts,
                conts,
                prompts,
                conts,
                fixed,
                pl.BlockSpec((1, FF), lambda m, i, s, t: (0, 0)),
            ]
            + parts_in
            + [whole] * len(pieces),
            out_specs=[prompts, conts, prompts, conts, heads, heads, fixed, long, whole, whole],
            scratch_shapes=[
                pltpu.VMEM((D, D), BF),
                pltpu.VMEM((D, FF), BF),
                pltpu.VMEM((FF, D), BF),
                pltpu.VMEM((D, D), F32),
                pltpu.VMEM((D, FF), F32),
                pltpu.VMEM((D, FF), F32),
                pltpu.VMEM((2, D // share, share, D), BF),
                pltpu.VMEM((tile, HALF), BF),
                pltpu.VMEM((tile, HALF), BF),
                pltpu.SemaphoreType.DMA(
                    (max(16, (2 + FF // D) * sum(piece.shape[0] for piece in pieces)),)
                ),
            ],
        ),
        out_shape=(
            shape(prompt_in.shape, BF),
            shape(cont_in.shape, BF),
            shape(prompt_in.shape, BF),
            shape(cont_in.shape, BF),
            shape((MB, prow + crow, HALF), BF),
            shape((MB, prow + crow, HALF), BF),
            shape((8, D), F32),
            shape((8, FF), F32),
            shape((D // share, share, D + FF + FF // 2), BF),
            shape((D // share, share, FF // 2), BF),
        ),
        compiler_params=pltpu.CompilerParams(
            dimension_semantics=("arbitrary", "arbitrary"), vmem_limit_bytes=63 << 20
        ),
        cost_estimate=pl.CostEstimate(
            flops=6 * rows * (D * D + 2 * D * FF), bytes_accessed=50 << 20, transcendentals=0
        ),
        name="feed_forward",
    )(lens, places, prompt_in, cont_in, prompt_cot, cont_cot, vec, bfc, *heads_in, *pieces)


def input_grad_kernel(x_ref, slope_ref, vec_ref, *refs):
    batch = pl.program_id(0)
    out_ref, change_ref = refs[MB:]
    for m in range(MB):

        @pl.when(batch == m)
        def _():
            change_ref[...] = refs[m][...].astype(F32)

    x = x_ref[0].astype(F32)
    center = x - jnp.mean(x, axis=1, keepdims=True)
    rate = lax.rsqrt(jnp.mean(center * center, axis=1, keepdims=True) + EPSILON)
    hat = center * rate
    e1 = change_ref[...] * vec_ref[0:1, :]
    change = e1 - jnp.mean(e1, axis=1, keepdims=True)
    change = change - hat * jnp.mean(e1 * hat, axis=1, keepdims=True)
    out_ref[0] = (slope_ref[0].astype(F32) + rate * change).astype(BF)


def input_grads(x, slope, vec, tables, tile):
    count = x.shape[1] // tile

    def table_spec(own):
        def place(m, i):
            return (jnp.where(m == own, i, jnp.where(m < own, 0, count - 1)), 0)

        return pl.BlockSpec((tile, D), place)

    rows = pl.BlockSpec((1, tile, D), lambda m, i: (m, i, 0))
    return pl.pallas_call(
        input_grad_kernel,
        grid=(MB, count),
        in_specs=[rows, rows, pl.BlockSpec(vec.shape, lambda m, i: (0, 0))]
        + [table_spec(own) for own in range(MB)],
        out_specs=rows,
        out_shape=jax.ShapeDtypeStruct(x.shape, BF),
        scratch_shapes=[pltpu.VMEM((tile, D), F32)],
        compiler_params=pltpu.CompilerParams(
            dimension_semantics=("arbitrary", "arbitrary"), vmem_limit_bytes=24 << 20
        ),
        name="input_grads",
    )(x, slope, vec, *tables)


HEAD_COLS = 3 * HALF
SMALL_COLS = 128


def neighbour(value, axis, distance):
    pairs = [(i, i ^ distance) for i in range(lax.axis_size(axis))]
    return lax.ppermute(value, axis, pairs)


def swap(value):
    return neighbour(value, "fsdp", 1)


def is_square():
    return lax.axis_size("grp") == 4 and lax.axis_size("fsdp") == 8


def spread_one(block):
    half = block.shape[0] // 2
    pieces = [block[:half], block[half:]]
    return [
        jnp.stack([piece, neighbour(piece, "grp", distance)])
        for piece, distance in zip(pieces, (1, 2))
    ]


def spread_two(boths):
    return [neighbour(both, "grp", distance) for both, distance in zip(boths, (2, 1))]


def spread_pieces(boths, fars):
    return [
        (boths[0], (0, 1), 0),
        (fars[0], (2, 3), 0),
        (boths[1], (0, 2), 1),
        (fars[1], (1, 3), 1),
    ]


def gather_zone(packed):
    if not is_square():
        return lax.all_gather(packed, ALL, axis=0, tiled=True)
    groups = [list(range(c, lax.axis_size("fsdp"), 2)) for c in (0, 1)]
    return lax.all_gather(packed, "fsdp", axis=0, tiled=True, axis_index_groups=groups)


def chip_rows(keep, send, core):
    other = swap(send)
    return jnp.where(
        core == 0,
        jnp.concatenate([keep, other], axis=0),
        jnp.concatenate([other, keep], axis=0),
    )


def join_front(boths, fars):
    own = lax.axis_index("grp")
    parts = {}
    for pair, offsets, index in spread_pieces(boths, fars):
        for which, offset in enumerate(offsets):
            parts[offset, index] = pair[which]
    table = jnp.stack([jnp.concatenate([parts[k, 0], parts[k, 1]], axis=0) for k in range(4)])
    return jnp.concatenate(
        [lax.dynamic_index_in_dim(table, own ^ k, 0, keepdims=False) for k in range(4)], axis=0
    )


def join_rest(boths, fars):
    own = lax.axis_index("grp")
    size = boths[0].shape[1]
    pieces, rows = [], []
    for pair, offsets, index in spread_pieces(boths, fars):
        pieces.append(pair)
        for offset in offsets:
            rows.append((own ^ offset) * 2 * size + index * size)
    return pieces + [swap(piece) for piece in pieces], rows + rows


def pin(*values):
    return list(lax.optimization_barrier(tuple(values)))


def pick(array, index, axis):
    return lax.dynamic_index_in_dim(array, index, axis, keepdims=False)


def meet(array, index, axis, name, distance):
    other = neighbour(pick(array, 1 - index, axis), name, distance)
    return (pick(array, index, axis).astype(F32) + other.astype(F32)).astype(BF)


def reduce_steps():
    if not is_square():
        groups = [list(range(c, lax.axis_size("fsdp"), 2)) for c in (0, 1)]

        def along_grp(value):
            return lax.psum_scatter(value, "grp", scatter_dimension=0, tiled=True)

        def along_chips(value):
            return lax.psum_scatter(
                value, "fsdp", scatter_dimension=0, tiled=True, axis_index_groups=groups
            )

        return [along_grp, along_chips]

    own = lax.axis_index("grp")
    x, y = own % 2, own // 2
    z = lax.axis_index("fsdp") // 2

    def one(value):
        value = value.reshape(2, 2, 2, value.shape[0] // 8, value.shape[1])
        return meet(value[:, :, 0], x, 1, "grp", 1), meet(value[:, :, 1], y, 0, "grp", 2)

    def two(pair):
        value = jnp.concatenate(
            [meet(pair[0], y, 0, "grp", 2), meet(pair[1], x, 0, "grp", 1)], axis=0
        )
        return value.reshape(2, 2, value.shape[0] // 4, value.shape[1])

    def three(value):
        return meet(value, z % 2, 1, "fsdp", 2)

    def four(value):
        return meet(value, z // 2, 0, "fsdp", 4)

    return [one, two, three, four]


def reduce_parameters(value):
    for step in reduce_steps():
        value = step(value)
    return value


def own_rows(value, core):
    share = value.shape[0] // 2
    keep = lax.dynamic_slice_in_dim(value, core * share, share, 0)
    other = swap(lax.dynamic_slice_in_dim(value, (1 - core) * share, share, 0))
    return keep, other


def square_steps(core):
    own = lax.axis_index("grp")
    x, y = own % 2, own // 2

    def one(value):
        cols = value.shape[-1] // 2
        value = value.reshape((2, 2) + value.shape[1:])
        return (
            meet(value[..., :cols], x, 1, "grp", 1),
            meet(value[..., cols:], y, 0, "grp", 2),
        )

    def two(pair):
        return jnp.concatenate(
            [meet(pair[0], y, 0, "grp", 2), meet(pair[1], x, 0, "grp", 1)], axis=1
        )

    return [one, two]


def body(
    prompt_in,
    cont_in,
    prompt_cot,
    cont_cot,
    cont_prompt,
    cont_len,
    ln1_gain,
    ln1_bias,
    attn_weight,
    attn_bias,
    proj_weight,
    proj_bias,
    ln2_gain,
    ln2_bias,
    fc_weight,
    fc_bias,
    out_weight,
    out_bias,
):
    fsdp = lax.axis_size("fsdp")
    devices = fsdp * lax.axis_size("grp")
    prow = prompt_in.shape[1]
    crow = cont_in.shape[1]
    conts = cont_prompt.shape[2]
    clen = crow // conts
    mine = prow + crow
    TQ = min(256, prow, clen)
    prompt_rows = NPR * PLEN
    place = lax.axis_index("fsdp")
    core = place % 2
    share = D // devices
    wide = FF // D

    vectors = (ln1_gain, ln1_bias, attn_bias[0], attn_bias[1], proj_bias, ln2_gain, ln2_bias, out_bias)
    columns = jnp.concatenate(
        [v[:, None] for v in vectors] + [fc_bias.reshape(wide, share).T], axis=1
    )
    columns = jnp.pad(columns, ((0, 0), (0, SMALL_COLS - columns.shape[1])))
    prompt_all = [lax.all_gather(prompt_in[m], "fsdp", axis=0, tiled=True) for m in range(MB)]
    square = is_square()
    columns = columns.astype(BF)
    heads = attn_weight.astype(BF).reshape(share, 3, 2, HALF)
    keep = lax.dynamic_index_in_dim(heads, core, 2, keepdims=False).reshape(share, HEAD_COLS)
    send = lax.dynamic_index_in_dim(heads, 1 - core, 2, keepdims=False).reshape(share, HEAD_COLS)
    rest = jnp.concatenate(
        [
            proj_weight,
            fc_weight.reshape(share, devices, wide, share).transpose(0, 2, 1, 3).reshape(share, FF),
            out_weight.reshape(wide, share, D).transpose(1, 0, 2).reshape(share, FF),
        ],
        axis=1,
    ).astype(BF)
    if square:
        zone = gather_zone(
            chip_rows(
                jnp.concatenate([keep, columns], axis=1),
                jnp.concatenate([send, columns], axis=1),
                core,
            )
        )
        half = rest.shape[1] // 2
        rest = chip_rows(
            lax.dynamic_slice_in_dim(rest, core * half, half, 1),
            lax.dynamic_slice_in_dim(rest, (1 - core) * half, half, 1),
            core,
        )
        cut = half // 256 * 128
        first, zone = pin(rest[:, :cut], zone)
        zones = [gather_zone(first)]
        front_boths = spread_one(zone)
        zones[0], second, *front_boths = pin(zones[0], rest[:, cut:], *front_boths)
        zones.append(gather_zone(second))
        front_fars = spread_two(front_boths)
        zones[1], *front_fars = pin(zones[1], *front_fars)
        front = join_front(front_boths, front_fars)
        rest_boths = spread_one(jnp.concatenate(zones, axis=1))
    else:
        zone = gather_zone(jnp.concatenate([heads.reshape(share, 3 * D), columns], axis=1))
        front = jnp.concatenate(
            [
                lax.dynamic_index_in_dim(
                    zone[:, : 3 * D].reshape(D, 3, 2, HALF), core, 2, keepdims=False
                ).reshape(D, HEAD_COLS),
                zone[:, 3 * D :],
            ],
            axis=1,
        )
        pieces = [gather_zone(rest).reshape(2, HALF, -1)]
        piece_rows = [0, HALF]
    w_heads = front[:, :HEAD_COLS]
    small = front[:, HEAD_COLS:].astype(F32)
    gain_a, shift_a, bias_q, bias_v, b_proj, gain_b, shift_b, b_out = (small[:, i] for i in range(8))
    b_fc = small[:, 8 : 8 + wide].T.reshape(1, FF)
    bias_q = lax.dynamic_slice_in_dim(bias_q, core * HALF, HALF)
    bias_v = lax.dynamic_slice_in_dim(bias_v, core * HALF, HALF)
    none = jnp.zeros((HALF,), F32)
    vec_a = jnp.stack(
        [gain_a, shift_a, jnp.concatenate([none, bias_v]), jnp.concatenate([bias_q, none])]
        + [jnp.zeros((D,), F32)] * 4
    )
    vec_b = jnp.pad(jnp.stack([b_proj, gain_b, shift_b, b_out]), ((0, 4), (0, 0)))

    cont_mate = swap(cont_in)
    plan_mate = swap(cont_prompt[:, 0, :].astype(F32)).astype(jnp.int32)

    def balanced(index):
        ends = fsdp // NPR
        other = index // ends * ends + ends - 1 - (index % ends - index % 2)
        return index + (index % 2) * (other - index)

    own_place = balanced(place)
    mate_place = balanced(place + 1 - 2 * core)
    own_row = own_place * prow
    mate_row = mate_place * prow
    own_pairs = [(i, balanced(i)) for i in range(fsdp)]
    mate_pairs = [(i, balanced(i ^ 1)) for i in range(fsdp)]

    def send_home(own, other):
        return (
            lax.ppermute(own[:prow], "fsdp", own_pairs),
            own[prow:],
            lax.ppermute(other[:prow], "fsdp", mate_pairs),
            swap(other[prow:]),
        )

    def send_back(own, other):
        return [
            lax.ppermute(own[:prow], "fsdp", [(b, a) for a, b in own_pairs]),
            own[prow:],
            lax.ppermute(other[:prow], "fsdp", [(b, a) for a, b in mate_pairs]),
            swap(other[prow:]),
        ]

    def prompt_plan(row):
        row = row + TQ * jnp.arange(prow // TQ)
        spot = row % PLEN
        return jnp.stack(
            [
                row - spot,
                spot // TK,
                spot % TK // TQ,
                row - spot + spot // TK * TK,
                row,
            ],
            axis=1,
        )

    def cont_plan(follows, first):
        blocks = clen // TQ
        follows = jnp.repeat(follows, blocks)
        index = jnp.arange(conts * blocks)
        begin = prompt_rows + first + index // blocks * clen
        return jnp.stack(
            [
                follows * PLEN,
                jnp.full(index.shape, PLEN // TK),
                index % blocks,
                begin,
                begin + index % blocks * TQ,
            ],
            axis=1,
        )

    def plan_of(m):
        return jnp.concatenate(
            [
                prompt_plan(own_row),
                cont_plan(cont_prompt[m, 0], 0),
                prompt_plan(mate_row),
                cont_plan(plan_mate[m], crow),
            ],
            axis=0,
        ).astype(jnp.int32)

    blocks = []
    for kind, count in (("own", prow), ("cont", crow), ("mate", prow), ("other", crow)):
        for index in range(count // TQ):
            prompt = (mate_row if kind in ("mate", "other") else own_row) // TQ
            last = prow // TQ - 1
            if kind in ("own", "mate"):
                blocks.append((0, prompt + index, 0 if kind == "own" else crow // TQ - 1))
            else:
                first = 0 if kind == "cont" else crow // TQ
                blocks.append((1, prompt + last, first + index))
    spot = jnp.stack(
        [
            jnp.stack([jnp.asarray(value, jnp.int32) for value in entry + (own_place, mate_place)])
            for entry in blocks
        ]
    ).astype(jnp.int32)

    saved = []
    outs = []
    for m in range(MB):
        x_prompt = prompt_all[m]
        if m > 0:
            x_prompt, saved[-1][-1] = pin(x_prompt, saved[-1][-1])
        if square and m == 1:
            x_prompt, *rest_boths = pin(x_prompt, *rest_boths)
            rest_fars = spread_two(rest_boths)
        x_cont = jnp.concatenate([cont_in[m], cont_mate[m]], axis=0)
        plan = plan_of(m)
        o, lse, query, kv = attend_forward(plan, spot, x_prompt, x_cont, w_heads, vec_a, TQ, prow)
        if square and m == 1:
            lse, *rest_fars = pin(lse, *rest_fars)
        outs.append(send_home(o[:mine], o[mine:]))
        saved.append([x_prompt, x_cont, kv, query, plan, o, lse])

    if square:
        pieces, piece_rows = join_rest(rest_boths, rest_fars)

    groups, block_share = (4, share) if square else (1, 8)
    places = jnp.stack([core] + [jnp.asarray(row, jnp.int32) for row in piece_rows]).astype(jnp.int32)
    (
        prompt_out,
        cont_out,
        prompt_dh,
        cont_dh,
        d_mine,
        d_mate,
        g_vec,
        g_fc_bias,
        g_rest,
        g_more,
    ) = feed_forward(
        cont_len[:, 0, :],
        places,
        prompt_in,
        cont_in,
        prompt_cot,
        cont_cot,
        [part for parts in outs for part in parts],
        vec_b,
        b_fc,
        pieces,
        groups,
        block_share,
    )
    returned = [send_back(d_mine[m], d_mate[m]) for m in range(MB)]
    g_rest, g_more, *returned[0] = pin(g_rest, g_more, *returned[0])

    def along_fsdp(value):
        if square:
            return lax.psum_scatter(value, "fsdp", scatter_dimension=0, tiled=True)
        value = value.reshape(D, value.shape[2])
        return lax.psum_scatter(value, ALL, scatter_dimension=0, tiled=True)

    g_rest, g_more = along_fsdp(g_rest), along_fsdp(g_more)

    totals = None
    tables = []
    conts_back = []
    for m in range(MB):
        x_prompt, x_cont, kv, query, plan, o, lse = saved[m]
        if m > 0:
            tables[-1], *returned[m] = pin(tables[-1], *returned[m])
            tables[-1] = lax.psum_scatter(tables[-1], "fsdp", scatter_dimension=0, tiled=True)
        if m > 1:
            g_more, *returned[m] = pin(g_more, *returned[m])
        if m == 1:
            g_rest, *returned[m] = pin(g_rest, *returned[m])
        do = returned[m]
        table, table_cont, *totals = attend_backward(
            plan, spot, x_prompt, x_cont, kv, query, do, o, lse, w_heads, vec_a, totals, TQ, prow
        )
        tables.append(table)
        conts_back.append(
            table_cont[:crow].astype(F32) + swap(table_cont[crow:]).astype(F32)
        )
    if MB > 1:
        tables = pin(*tables)
    tables[-1] = lax.psum_scatter(tables[-1], "fsdp", scatter_dimension=0, tiled=True)
    g_heads, g_first, g_bias = totals

    def spread(value):
        return jnp.where((jnp.arange(2) == core)[:, None], value[None, :], 0.0).reshape(D)

    sums = jnp.stack(
        [
            g_first[0],
            g_first[1],
            spread(g_bias[0, :HALF]),
            spread(g_bias[0, 2 * HALF :]),
            g_vec[0],
            g_vec[1],
            g_vec[2],
            g_vec[3],
        ]
        + [g_fc_bias[0, i * D : (i + 1) * D] for i in range(wide)],
        axis=0,
    )
    sums_high = sums.astype(BF)
    sums_low = (sums - sums_high.astype(F32)).astype(BF)
    count = sums.shape[0]
    sums = jnp.concatenate(
        [sums_high, sums_low, jnp.zeros((SMALL_COLS - 2 * count, D), BF)], axis=0
    ).T
    late = jnp.concatenate([g_heads.astype(BF), sums], axis=1)
    for step in reduce_steps():
        late = step(late)
    early = jnp.concatenate([g_rest, g_more], axis=-1)
    for step in square_steps(core) if square else ():
        early = step(early)
    late_own, late_other = own_rows(late, core)
    sums = late_own[:, HEAD_COLS:].astype(F32) + late_other[:, HEAD_COLS:].astype(F32)
    sums = (sums[:, :count] + sums[:, count : 2 * count]).T

    def by_core(own, other):
        return jnp.where(core == 0, own, other), jnp.where(core == 0, other, own)

    late = jnp.stack(by_core(late_own[:, :HEAD_COLS], late_other[:, :HEAD_COLS]), axis=1)
    late = late.reshape(share, 2, 3, HALF).transpose(0, 2, 1, 3).reshape(share, 3 * D)
    early = early.astype(F32)
    g_fc = early[:, D : D + FF].reshape(share, wide, devices, share)
    g_fc = g_fc.transpose(0, 2, 1, 3).reshape(share, FF)
    g_out = early[:, D + FF :].reshape(share, wide, D).transpose(1, 0, 2).reshape(share * wide, D)

    def input_grad(source, slope, change):
        source = source.astype(F32)
        center = source - jnp.mean(source, axis=-1, keepdims=True)
        rate = lax.rsqrt(jnp.mean(center * center, axis=-1, keepdims=True) + EPSILON)
        hat = center * rate
        e1 = change * gain_a
        change = e1 - jnp.mean(e1, axis=-1, keepdims=True)
        change = change - hat * jnp.mean(e1 * hat, axis=-1, keepdims=True)
        return (slope.astype(F32) + rate * change).astype(BF)

    prompt_grad = input_grads(prompt_in, prompt_dh, vec_a, tables, TQ)
    cont_grad = jnp.stack([input_grad(cont_in[m], cont_dh[m], conts_back[m]) for m in range(MB)])
    return (
        prompt_out,
        cont_out,
        prompt_grad,
        cont_grad,
        sums[0],
        sums[1],
        late.astype(F32),
        sums[2:4],
        early[:, :D],
        sums[4],
        sums[5],
        sums[6],
        g_fc,
        sums[8:].reshape(share * wide),
        g_out,
        sums[7],
    )


def solution(mesh):
    rows = P(None, ALL, None)
    conts = P(None, "grp", "fsdp")
    vector = P(ALL)
    matrix = P(ALL, None)
    pair = P(None, ALL)
    params = (
        vector,
        vector,
        matrix,
        pair,
        matrix,
        vector,
        vector,
        vector,
        matrix,
        vector,
        matrix,
        vector,
    )
    return jax.shard_map(
        body,
        mesh=mesh,
        in_specs=(rows, rows, rows, rows, conts, conts) + params,
        out_specs=(rows, rows, rows, rows) + params,
        check_vma=False,
    )
```
